32 devices in a mesh: batch: 4 (over z), head: 4 (over y, x), ctx: 2 (over core).
Axes of the slice: x: 2, y: 2, z: 4, core: 2. Of those that a mesh axis runs over, the one named last changes fastest.
Arguments:
- hidden_in: bfloat16 [4, 1024, 960], P('batch', 'ctx'), may hold values from -6 to 6
- cotangent: bfloat16 [4, 1024, 960], P('batch', 'ctx'), may hold values from -6 to 6
- lengths: int32 [4], P('batch'), may hold values from 64 to 1024, as said below
- owners: int32 [5], replicated, may hold values from 0 to 3, as said below
- w_query: bfloat16 [960, 960], replicated, may hold values from -0.1875 to 0.1875
- w_key: bfloat16 [960, 320], replicated, may hold values from -0.1875 to 0.1875
- w_value: bfloat16 [960, 320], replicated, may hold values from -0.1875 to 0.1875
- w_output: bfloat16 [960, 960], replicated, may hold values from -2 to 2
- gate_weight: bfloat16 [960, 2560], P(None, 'head'), may hold values from -0.1875 to 0.1875
- up_weight: bfloat16 [960, 2560], P(None, 'head'), may hold values from -0.1875 to 0.1875
- down_weight: bfloat16 [2560, 960], P('head'), may hold values from -0.125 to 0.125
- gain_attn: float32 [960], replicated, may hold values from 0.1 to 1.9
- gain_ffn: float32 [960], replicated, may hold values from 0.1 to 1.9
Outputs:
- output: bfloat16 [4, 1024, 960], P('batch', 'ctx')
- grad_input: float32 [4, 1024, 960], P('batch', 'ctx')
- grad_query: float32 [960, 1536], P(None, 'head')
- grad_key: float32 [960, 512], P(None, 'head')
- grad_value: float32 [960, 512], P(None, 'head')
- grad_output: float32 [1536, 960], P('head')
- grad_gate: float32 [960, 2560], P(None, 'head')
- grad_up: float32 [960, 2560], P(None, 'head')
- grad_down: float32 [2560, 960], P('head')
- grad_gain_attn: float32 [960], replicated
- grad_gain_ffn: float32 [960], replicated
The draws below stay inside these ranges and needn't reach their ends.
Inputs may be any that keep to these rules, and one draw needn't show every extreme that they name: `lengths`: at least one sequence has all 1024 slots valid. `owners`: every head index computes one or two groups.
All inputs are finite; a program needn't handle non-finite values.
Results may differ from the reference program's by a relative error of at most 0.034.
Values may be sent and summed in bfloat16 or wider, within the bound.
A program may use at most 192 MiB of HBM per device.

```python
import math
import jax
import jax.numpy as jnp
from jax import lax

D = 960
FF = 2560
QH = 15
KV = 5
HD = 64
GQ = 3
SLOT = 1024
SEQS = 4
N_HEAD = 4


def draw_lengths(key, part):
    first_key = jax.random.fold_in(key, 11)
    second_key = jax.random.fold_in(key, 12)
    shortest = max(SLOT // 16, 1)
    drawn_lengths = jax.random.randint(first_key, (SEQS,), shortest, SLOT + 1, dtype=jnp.int32)
    longest_at = jax.random.randint(second_key, (), 0, SEQS, dtype=jnp.int32)
    return jnp.where(jnp.arange(SEQS, dtype=jnp.int32) == longest_at, SLOT, drawn_lengths).astype(jnp.int32)


def draw_owners(key, part):
    ordering = jax.random.permutation(jax.random.fold_in(key, 21), KV).astype(jnp.int32)
    offset = jax.random.randint(jax.random.fold_in(key, 22), (), 0, KV - 1, dtype=jnp.int32)
    return ((ordering + offset) % (KV - 1)).astype(jnp.int32)


def shard_levels(rng, shape, pieces, least, high):
    def one(axis_at, blocks):
        steps = jax.random.uniform(jax.random.fold_in(jax.random.fold_in(rng, 6), axis_at), (blocks,), jnp.float32, least / len(pieces), high / len(pieces))
        return jnp.repeat(jnp.exp(steps), shape[axis_at] // blocks).reshape((-1,) + (1,) * (len(shape) - axis_at - 1))

    factor_of = one(*pieces[0])
    for cut in pieces[1:]:
        factor_of = factor_of * one(*cut)
    return factor_of


def gaussian(stream_key, extent, scale, bound, pieces=(), kind=jnp.bfloat16):
    values = scale * jax.random.normal(stream_key, extent, jnp.float32)
    if pieces:
        values = values * shard_levels(stream_key, extent, pieces, -0.22, 0.18)
    return jnp.clip(values, -bound, bound).astype(kind)


def setup_inputs(seed: int = 0) -> dict:
    streams_of = jax.random.split(jax.random.key(seed), 14)
    hidden_in = gaussian(streams_of[0], (SEQS, SLOT, D), 1.0, 6.0, ((0, 4), (1, 2)))
    cotangent = gaussian(streams_of[1], (SEQS, SLOT, D), 1.0, 6.0, ((0, 4), (1, 2)))
    lengths = draw_lengths(jax.random.fold_in(streams_of[13], 71), 0)
    owners = draw_owners(jax.random.fold_in(streams_of[13], 71), 0)
    w_query = gaussian(streams_of[4], (D, QH * HD), D ** -0.5, 0.1875)
    w_key = gaussian(streams_of[5], (D, KV * HD), D ** -0.5, 0.1875)
    w_value = gaussian(streams_of[6], (D, KV * HD), D ** -0.5, 0.1875)
    w_output = gaussian(streams_of[7], (QH * HD, D), (max(HD // 8, 2)) ** -0.5, 2.0)
    gate_weight = gaussian(streams_of[8], (D, FF), D ** -0.5, 0.1875, ((1, 4),))
    up_weight = gaussian(streams_of[9], (D, FF), D ** -0.5, 0.1875, ((1, 4),))
    down_weight = gaussian(streams_of[10], (FF, D), FF ** -0.5, 0.125, ((0, 4),))
    gain_attn = jnp.clip(1.0 + 0.18 * jax.random.normal(streams_of[11], (D,), jnp.float32), 0.1, 1.9)
    gain_ffn = jnp.clip(1.0 + 0.18 * jax.random.normal(streams_of[12], (D,), jnp.float32), 0.1, 1.9)
    return {"hidden_in": hidden_in, "cotangent": cotangent, "lengths": lengths, "owners": owners, "w_query": w_query, "w_key": w_key, "w_value": w_value, "w_output": w_output, "gate_weight": gate_weight, "up_weight": up_weight, "down_weight": down_weight, "gain_attn": gain_attn, "gain_ffn": gain_ffn}


EPSILON = 1e-05
MASKED_OUT = -1e+30

@jax.custom_vjp
def low(v):
    return lax.optimization_barrier(v.astype(jnp.bfloat16)).astype(jnp.float32)

@jax.custom_vjp
def low_back(v):
    return v

def low_keep(v):
    return (low(v), None)

def low_pass(kept, grad):
    return (grad,)

def back_keep(v):
    return (v, None)

def back_low(kept, grad):
    return (low(grad),)
low.defvjp(low_keep, low_pass)
low_back.defvjp(back_keep, back_low)

def dense_dot(left, right):
    return jnp.dot(left, right, precision=lax.Precision.HIGHEST, preferred_element_type=jnp.float32)

def rms_normed(residual, gain_vec):
    inv_rms = lax.rsqrt(lax.optimization_barrier(jnp.mean(residual * residual, axis=-1, keepdims=True)) + EPSILON)
    return residual * inv_rms * gain_vec

def rope_tables(positions):
    steps_half = jnp.arange(HD // 2, dtype=jnp.float32)
    inverse = jnp.exp(steps_half * (-2.0 * math.log(10000.0) / HD))
    angles = positions.astype(jnp.float32)[:, None] * inverse[None, :]
    return (jnp.cos(angles), jnp.sin(angles))

def rotate(tensor, cos_tab, sin_tab):
    half_width = tensor.shape[-1] // 2
    first_half = tensor[..., :half_width]
    second_half = tensor[..., half_width:]
    return jnp.concatenate([first_half * cos_tab - second_half * sin_tab, second_half * cos_tab + first_half * sin_tab], axis=-1)

def group_attention(feed_in, query_cols, key_cols, value_cols, out_rows, allowed, cos_tab, sin_tab):
    score_scale = HD ** (-0.5)
    query_pre = low_back(dense_dot(feed_in, query_cols))
    key_rows = low(rotate(low_back(dense_dot(feed_in, key_cols)), cos_tab, sin_tab))
    value_rows = low(low_back(dense_dot(feed_in, value_cols)))
    heads_out = []
    for head_idx in range(GQ):
        query_head = low(rotate(query_pre[:, head_idx * HD:(head_idx + 1) * HD], cos_tab, sin_tab))
        raw_scores = low_back(dense_dot(query_head, key_rows.T) * score_scale)
        masked = jnp.where(allowed, raw_scores, MASKED_OUT)
        row_peak = lax.optimization_barrier(jnp.max(masked, axis=-1, keepdims=True))
        exp_scores = jnp.exp(masked - row_peak)
        soft_probs = exp_scores / lax.optimization_barrier(jnp.sum(exp_scores, axis=-1, keepdims=True))
        heads_out.append(dense_dot(low(soft_probs), value_rows))
    attention_result = low_back(low(jnp.concatenate(heads_out, axis=-1)))
    return dense_dot(attention_result, out_rows)

def one_pass(residual, params, valid_rows, allowed, cos_tab, sin_tab, select):
    w_query, w_key, w_value, w_output, gate_weight, up_weight, down_weight, gain_attn, gain_ffn = params
    group_width = GQ * HD
    ffn_width = FF // N_HEAD
    attention_normalized = low(rms_normed(residual, gain_attn))
    feed_list = [low_back(attention_normalized) for device in range(N_HEAD)]
    attend = jax.checkpoint(group_attention)
    group_outs = []
    for group_idx in range(KV):
        feed_in = feed_list[0] * select[group_idx, 0]
        for device in range(1, N_HEAD):
            feed_in = feed_in + feed_list[device] * select[group_idx, device]
        group_outs.append(attend(feed_in, w_query[:, group_idx * group_width:(group_idx + 1) * group_width], w_key[:, group_idx * HD:(group_idx + 1) * HD], w_value[:, group_idx * HD:(group_idx + 1) * HD], w_output[group_idx * group_width:(group_idx + 1) * group_width, :], allowed, cos_tab, sin_tab))
    attn_total = jnp.zeros_like(residual)
    for device in range(N_HEAD):
        part_sum = group_outs[0] * select[0, device]
        for group_idx in range(1, KV):
            part_sum = part_sum + group_outs[group_idx] * select[group_idx, device]
        attn_total = attn_total + low(low_back(part_sum))
    middle = residual + attn_total
    feedforward_normalized = low(rms_normed(middle, gain_ffn))
    ffn_total = jnp.zeros_like(residual)
    for device in range(N_HEAD):
        feed_in = low_back(feedforward_normalized)
        gate_preactivation = low_back(dense_dot(feed_in, gate_weight[:, device * ffn_width:(device + 1) * ffn_width]))
        up_preactivation = low_back(dense_dot(feed_in, up_weight[:, device * ffn_width:(device + 1) * ffn_width]))
        activation_values = low(jax.nn.silu(gate_preactivation) * up_preactivation)
        ffn_total = ffn_total + low(low_back(dense_dot(activation_values, down_weight[device * ffn_width:(device + 1) * ffn_width, :])))
    return valid_rows * (middle + ffn_total)

def reference(hidden_in, cotangent, lengths, owners, w_query, w_key, w_value, w_output, gate_weight, up_weight, down_weight, gain_attn, gain_ffn):
    params = tuple((weight.astype(jnp.float32) for weight in (w_query, w_key, w_value, w_output, gate_weight, up_weight, down_weight, gain_attn, gain_ffn)))
    positions = jnp.arange(SLOT, dtype=jnp.int32)
    cos_tab, sin_tab = rope_tables(positions)
    select = (owners[:, None] == jnp.arange(N_HEAD, dtype=jnp.int32)[None, :]).astype(jnp.float32)

    def per_sequence(totals, inputs):
        sequence, tangent, length = inputs
        valid_rows = (positions < length).astype(jnp.float32)[:, None]
        allowed = (positions[None, :] <= positions[:, None]) & (positions[None, :] < length)

        def forward(residual, weights):
            middle = one_pass(residual, weights, valid_rows, allowed, cos_tab, sin_tab, select)
            return one_pass(middle, weights, valid_rows, allowed, cos_tab, sin_tab, select)
        result, pull_back = jax.vjp(forward, sequence.astype(jnp.float32), params)
        grad_in, grad_params = pull_back(tangent.astype(jnp.float32))
        totals = jax.tree.map(lambda total_grad, extra_grad: total_grad + extra_grad, totals, grad_params)
        return (totals, (result.astype(jnp.bfloat16), grad_in))
    zero_grads = jax.tree.map(jnp.zeros_like, params)
    totals, (outputs, grad_inputs) = lax.scan(per_sequence, zero_grads, (hidden_in, cotangent, lengths))
    g_query, g_key, g_value, g_output, g_gate, up_weight_gradient, g_down, g_gain_attn, g_gain_ffn = totals
    slot_groups = []
    slot_present = []
    for device in range(N_HEAD):
        owned_mask = (owners == device).astype(jnp.int32)
        ranked = jnp.cumsum(owned_mask) - 1
        for which_slot in range(2):
            chosen = owned_mask * (ranked == which_slot).astype(jnp.int32)
            slot_present.append(jnp.sum(chosen))
            slot_groups.append(jnp.sum(chosen * jnp.arange(KV, dtype=jnp.int32)))
    groups = jnp.stack(slot_groups).astype(jnp.int32)
    present = jnp.stack(slot_present).astype(jnp.float32)
    group_width = GQ * HD
    grad_query = (g_query.reshape(D, KV, group_width)[:, groups, :] * present[None, :, None]).reshape(D, N_HEAD * 2 * group_width)
    grad_key = (g_key.reshape(D, KV, HD)[:, groups, :] * present[None, :, None]).reshape(D, N_HEAD * 2 * HD)
    grad_value = (g_value.reshape(D, KV, HD)[:, groups, :] * present[None, :, None]).reshape(D, N_HEAD * 2 * HD)
    grad_output = (g_output.reshape(KV, group_width, D)[groups] * present[:, None, None]).reshape(N_HEAD * 2 * group_width, D)
    return (outputs, grad_inputs, grad_query, grad_key, grad_value, grad_output, g_gate, up_weight_gradient, g_down, g_gain_attn, g_gain_ffn)
```

```python
import functools
import math
from types import SimpleNamespace

import jax
import jax.numpy as jnp
import numpy as np
from jax import lax
from jax.experimental import pallas as pl
from jax.experimental.pallas import tpu as pltpu
from jax.sharding import PartitionSpec as P

KV = 5
HD = 64
GQ = 3
QH = KV * GQ
HEADS = 4
EPS = 1e-05
NEG = -1e30
MESH = pl.DeviceIdType.MESH
F32 = jnp.float32
BF16 = jnp.bfloat16


def nn(a, b):
    return lax.dot_general(a, b, (((1,), (0,)), ((), ())), preferred_element_type=F32)


def nt(a, b):
    return lax.dot_general(a, b, (((1,), (1,)), ((), ())), preferred_element_type=F32)


def tn(a, b):
    return lax.dot_general(a, b, (((0,), (0,)), ((), ())), preferred_element_type=F32)


def rope_table(slots):
    inverse = np.exp(np.arange(HD // 2, dtype=np.float32) * np.float32(-2.0 * math.log(10000.0) / HD))
    angles = np.arange(slots, dtype=np.float32)[:, None] * inverse[None, :].astype(np.float32)
    cos, sin = np.cos(angles).astype(np.float32), np.sin(angles).astype(np.float32)
    return np.concatenate([cos] * 4 + [sin] * 4, axis=1)


def peer_of(h, j):
    return (h, h + 1 - 2 * (h % 2), (h + 2) % 4, 3 - h)[j]


def scratch_of(rows, d, ff, nb):
    n = HEADS
    half = n * rows
    keys = 2 * half
    dp = -(-d // 128) * 128
    kp = -(-KV * HD // 128) * 128
    cr = d // 8
    v = pltpu.VMEM
    dma = pltpu.SemaphoreType.DMA
    return dict(
        hid_v=v((d, rows), BF16),
        cot_v=v((d, half), BF16),
        tab_v=v((rows, 256), F32),
        gains_v=v((2, d), F32),
        wq_v=v((d, QH * HD), BF16),
        wk_v=v((KV * HD, d), BF16),
        wv_v=v((KV * HD, d), BF16),
        wo_v=v((QH * HD, d), BF16),
        wf=v((3 * d, ff), BF16),
        res=v((2, rows, d), F32),
        mid=v((2, rows, d), F32),
        nat=v((d, 2 * rows), BF16),
        dat=v((d, 2 * rows), BF16),
        ql=v((2, KV, GQ * rows, 128), BF16),
        kv=v((2, KV, keys, 128), BF16),
        lse=v((2, rows, 128), F32),
        at=v((rows, d), BF16),
        nf=v((2, n, rows, d), BF16),
        gate=v((2, n, rows, ff), F32),
        up=v((2, n, rows, ff), F32),
        act=v((n, rows, ff), BF16),
        bias=v((rows, keys), F32),
        wide=v((rows, dp), F32),
        wide2=v((rows, kp), F32),
        wide3=v((rows, kp), F32),
        heads=v((QH, rows, 128), F32),
        part=v((rows, d), F32),
        psend=v((3, rows, d), BF16),
        precv=v((2, 3, rows, d), BF16),
        d_res=v((rows, d), F32),
        d_mid=v((rows, d), F32),
        df=v((2, n, rows, d), BF16),
        dg=v((n, rows, ff), BF16),
        du=v((n, rows, ff), BF16),
        ou=v((KV, GQ * rows, 128), BF16),
        dq=v((rows, d), BF16),
        dk=v((rows, KV * HD), BF16),
        dv=v((rows, KV * HD), BF16),
        dpg=v((KV, 2 * rows, 384), BF16),
        aog=v((KV, 2 * rows, 256), BF16),
        dkv=v((KV, 128, half), F32),
        dkv_ctx=v((KV, 128, half), BF16),
        dkv_ctx_r=v((2, KV, 128, half), BF16),
        dkv_s=v((3, KV, 128, rows), BF16),
        dkv_r=v((3, KV, 128, rows), BF16),
        fin=v((2, d, rows), BF16),
        gown=v((12, cr, ff), F32),
        sf=v((12, cr, ff), BF16),
        rf=v((12, cr, ff), BF16),
        rf2=v((12, cr, ff), BF16),
        zs=v((16, cr, ff), BF16),
        zu=v((16, cr, ff), BF16),
        zb=v((16, cr, ff), BF16),
        ha=v((KV, d // 2, 512), BF16),
        ra=v((KV, d // 2, 512), BF16),
        gain_v=v((2, d), F32),
        gain_p=v((2 * n, 2, d), F32),
        gain_z=v((nb, 2, d), F32),
        in_sem=dma((11,)),
        loc_sem=dma((8,)),
        kv_ss=dma((2, 4)),
        kv_rs=dma((2, 4)),
        kvc_ss=dma((2, 4)),
        kvc_rs=dma((2, 4)),
        nf_ss=dma((2, 4)),
        nf_rs=dma((2, 4)),
        p_ss=dma((4, 4)),
        p_rs=dma((4, 4)),
        df_ss=dma((4,)),
        df_rs=dma((4,)),
        dc_ss=dma((2,)),
        dc_rs=dma((2,)),
        dkv_ss=dma((2, 4)),
        dkv_rs=dma((2, 4)),
        fin_ss=dma((2, 4)),
        fin_rs=dma((2, 4)),
        f_ss=dma((3,)),
        f_rs=dma((3,)),
        z_s0=dma((16,)),
        z_s1=dma((16,)),
        z_ur=dma((16,)),
        z_br=dma((16,)),
        og_loc=dma((16,)),
        og_ss=dma((16,)),
        og_rs=dma((16,)),
        a_ss=dma((KV,)),
        a_rs=dma((KV,)),
        h_ss=dma((4,)),
        h_rs=dma((4,)),
        ex_loc=dma((4,)),
        ex_ss=dma((4, 8)),
        ex_rs=dma((4, 8)),
        gp_ss=dma((8,)),
        gp_rs=dma((8,)),
        gz_ss=dma((nb,)),
        gz_rs=dma((nb,)),
    )


def step_kernel(names, rows, d, ff, nb, *refs):
    r = SimpleNamespace(**dict(zip(names, refs)))
    wg_v, wu_v, wd_v = (r.wf.at[pl.ds(t * d, d)] for t in range(3))
    lhs = r.cot_v
    h = lax.axis_index("head")
    c = lax.axis_index("ctx")
    z = lax.axis_index("batch")
    half = HEADS * rows
    hd2 = d // 2
    cr = d // 8
    lane = lax.broadcasted_iota(jnp.int32, (rows, 128), 1)
    low = lane < HD
    quarter = (lane % HD) < HD // 2

    def copy_to(src, dst, ss, rs, where):
        return pltpu.make_async_remote_copy(
            src_ref=src, dst_ref=dst, send_sem=ss, recv_sem=rs, device_id=where, device_id_type=MESH
        )

    def remote(src, dst, ss, rs, j):
        return copy_to(src, dst, ss, rs, dict(head=peer_of(h, j)))

    def across(src, dst, ss, rs):
        return copy_to(src, dst, ss, rs, dict(ctx=1 - c))

    def load(k, src, dst):
        return pltpu.make_async_copy(src, dst, r.in_sem.at[k])

    my_rows = pl.ds(pl.multiple_of(h * rows, rows), rows)
    my_pos = pl.ds(pl.multiple_of(c * half + h * rows, rows), rows)
    loads = SimpleNamespace(
        hid=load(0, r.hid.at[:, my_rows], r.hid_v),
        gains=load(1, r.gains, r.gains_v),
        wk=load(3, r.wk, r.wk_v),
        wv=load(4, r.wv, r.wv_v),
        tab=load(5, r.tab.at[my_pos], r.tab_v),
        wq=load(2, r.wq, r.wq_v),
        wo=load(6, r.wo, r.wo_v),
        wg=load(7, r.wg, wg_v),
        wu=load(8, r.wu, wu_v),
        wd=load(9, r.wd, wd_v),
        cot=load(10, r.cot, r.cot_v),
    )
    for cp in vars(loads).values():
        cp.start()

    plane = [(j, x) for j in range(HEADS) for x in range(2) if (j, x) != (0, 0)]

    def plane_id(j, x):
        return dict(head=peer_of(h, j), ctx=1 - c if x else c)

    barrier = pltpu.get_barrier_semaphore()
    for j, x in plane:
        pl.semaphore_signal(barrier, inc=1, device_id=plane_id(j, x), device_id_type=MESH)
    for k in range(1, nb):
        pl.semaphore_signal(barrier, inc=1, device_id=dict(batch=(z + k) % nb), device_id_type=MESH)
    pl.semaphore_wait(barrier, len(plane) + nb - 1)

    length = r.len[0]
    row_pos = c * half + h * rows + lax.broadcasted_iota(jnp.int32, (rows, 1), 0)
    valid = (row_pos < length).astype(F32)

    for blk in range(2 * HEADS):
        own = blk < HEADS
        base = (c if own else 1 - c) * half + peer_of(h, blk % HEADS) * rows
        kp = base + lax.broadcasted_iota(jnp.int32, (rows, rows), 1)
        qp = c * half + h * rows + lax.broadcasted_iota(jnp.int32, (rows, rows), 0)
        ok = (kp <= qp) & (kp < length)
        r.bias[:, blk * rows : (blk + 1) * rows] = jnp.where(ok, 0.0, NEG)

    zero_w = jnp.zeros((rows, 128), F32)
    dp, kw = r.wide.shape[1], r.wide2.shape[1]
    r.wide[:, dp - 128 :] = zero_w
    r.wide2[:, kw - 128 :] = zero_w
    r.wide3[:, kw - 128 :] = zero_w
    r.lse[0] = zero_w
    r.lse[1] = zero_w

    @pl.when(c == 0)
    def _():
        for p in range(2):
            r.kv[p, :, half:, :] = jnp.zeros((KV, half, 128), BF16)

    def rms(x, gain):
        inv = lax.rsqrt(jnp.mean(x * x, axis=-1, keepdims=True) + EPS)
        return x * inv * gain

    def turned(x):
        return jnp.where(quarter, -pltpu.roll(x, 128 - HD // 2, 1), pltpu.roll(x, HD // 2, 1))

    def rope(x):
        return x * r.tab_v[:, 0:128] + turned(x) * r.tab_v[:, 128:256]

    def unrope(x):
        return x * r.tab_v[:, 0:128] - turned(x) * r.tab_v[:, 128:256]

    def swap(x):
        return pltpu.roll(x, HD, 1)

    def blocks(width):
        return [(b, b * 128, min(128, width - b * 128)) for b in range(-(-width // 128))]

    def head_row(i):
        return i // GQ, (i % GQ) * rows

    def store_t(dst, src):
        for b, lo, w in blocks(d):
            dst[lo : lo + w, :] = src[:, lo : lo + w].T

    gain_a = lambda: r.gains_v[0:1, :]
    gain_f = lambda: r.gains_v[1:2, :]

    loads.tab.wait()
    loads.gains.wait()
    loads.hid.wait()
    for b, lo, w in blocks(d):
        r.res[0, :, lo : lo + w] = r.hid_v[lo : lo + w, :].astype(F32).T

    def forward(p):
        x = r.res[p]
        na = rms(x, gain_a()).astype(BF16)
        store_t(r.nat.at[:, p * rows : (p + 1) * rows], na)
        if p == 0:
            loads.wk.wait()
            loads.wv.wait()
        r.wide2[:, : KV * HD] = nt(na, r.wk_v[...])
        r.wide3[:, : KV * HD] = nt(na, r.wv_v[...])
        for b in range(-(-KV // 2)):
            kb = rope(r.wide2[:, b * 128 : (b + 1) * 128])
            vb = r.wide3[:, b * 128 : (b + 1) * 128]
            r.kv[p, 2 * b, 0:rows, :] = jnp.where(low, kb, swap(vb)).astype(BF16)
            if 2 * b + 1 < KV:
                r.kv[p, 2 * b + 1, 0:rows, :] = jnp.where(low, swap(kb), vb).astype(BF16)
        sends = []
        for j in (1, 2, 3):
            cp = remote(
                r.kv.at[p, :, pl.ds(0, rows)], r.kv.at[p, :, pl.ds(j * rows, rows)],
                r.kv_ss.at[p, j], r.kv_rs.at[p, j], j,
            )
            cp.start()
            sends.append(cp)

        def to_partner(j):
            return across(
                r.kv.at[p, :, pl.ds(j * rows, rows)], r.kv.at[p, :, pl.ds(half + j * rows, rows)],
                r.kvc_ss.at[p, j], r.kvc_rs.at[p, j],
            )

        @pl.when(c == 0)
        def _():
            to_partner(0).start()

        if p == 0:
            loads.wq.wait()
        r.wide[:, :d] = nn(na, r.wq_v[...])
        for b, lo, w in blocks(d):
            y = rope(r.wide[:, lo : lo + 128]).astype(BF16).astype(F32) * HD ** (-0.5)
            g, o = head_row(2 * b)
            r.ql[p, g, o : o + rows, :] = jnp.where(low, y, 0.0).astype(BF16)
            if 2 * b + 1 < QH:
                g, o = head_row(2 * b + 1)
                r.ql[p, g, o : o + rows, :] = jnp.where(low, swap(y), 0.0).astype(BF16)

        for j in (1, 2, 3):
            sends[j - 1].wait_recv()

            @pl.when(c == 0)
            def _():
                to_partner(j).start()

        @pl.when(c == 1)
        def _():
            for j in range(HEADS):
                to_partner(j).wait_recv()

        @pl.loop(0, KV)
        def _(g):
            kv = r.kv[p, g]
            for k in range(GQ):
                s = nt(r.ql[p, g, k * rows : (k + 1) * rows, :], kv)
                s = jnp.where(r.bias[...] < 0.0, NEG, s)
                m = jnp.max(s, axis=-1, keepdims=True)
                e = jnp.exp(s - m)
                t = jnp.sum(e, axis=-1, keepdims=True)
                r.lse[p] += jnp.where(lane == g * GQ + k, m + jnp.log(t), 0.0)
                r.heads[g * GQ + k] = nn((e / t).astype(BF16), kv)

        mine = pl.ds(p * rows, rows)
        for g in range(KV):
            o0, o1, o2 = (r.heads[g * GQ + k] for k in range(GQ))
            r.aog[g, mine, 0:128] = jnp.where(low, 0.0, o0).astype(BF16)
            r.aog[g, mine, 128:256] = jnp.where(low, swap(o1), o2).astype(BF16)
        for b, lo, w in blocks(d):
            first = swap(r.heads[2 * b])
            both = jnp.where(low, first, r.heads[2 * b + 1]) if 2 * b + 1 < QH else first
            r.at[:, lo : lo + w] = both[:, :w].astype(BF16)
        if p == 0:
            loads.wo.wait()
        mid = r.res[p] + nn(r.at[...], r.wo_v[...])
        r.mid[p] = mid
        r.nf[p, 0] = rms(mid, gain_f()).astype(BF16)
        ag = []
        for j in (1, 2, 3):
            cp = remote(r.nf.at[p, 0], r.nf.at[p, j], r.nf_ss.at[p, j], r.nf_rs.at[p, j], j)
            cp.start()
            ag.append(cp)
        if p == 0:
            loads.wg.wait()
            loads.wu.wait()
            loads.wd.wait()
        rs = []
        for j in range(HEADS):
            if j:
                ag[j - 1].wait_recv()
            nf = r.nf[p, j]
            gate = nn(nf, wg_v[...])
            up = nn(nf, wu_v[...])
            r.gate[p, j] = gate
            r.up[p, j] = up
            act = (gate / (1.0 + jnp.exp(-gate)) * up).astype(BF16)
            part = nt(act, wd_v[...])
            if j == 0:
                r.part[...] = part
            else:
                r.psend[j - 1] = part.astype(BF16)
                cp = remote(r.psend.at[j - 1], r.precv.at[p, j - 1], r.p_ss.at[p, j], r.p_rs.at[p, j], j)
                cp.start()
                rs.append(cp)
        total = r.part[...].astype(BF16).astype(F32)
        for j in (1, 2, 3):
            rs[j - 1].wait_recv()
            total = total + r.precv[p, j - 1].astype(F32)
        result = valid * (r.mid[p] + total)
        if p == 0:
            r.res[1] = result
        else:
            r.d_res[...] = result
        for cp in sends + ag + rs:
            cp.wait_send()

        @pl.when(c == 0)
        def _():
            for j in range(HEADS):
                to_partner(j).wait_send()

    def finish(k, value, out):
        store_t(r.fin.at[k], value.astype(BF16))
        cps = []
        own = pltpu.make_async_copy(r.fin.at[k], out.at[:, my_rows], r.loc_sem.at[k])
        own.start()
        for j in (1, 2, 3):
            cp = remote(r.fin.at[k], out.at[:, my_rows], r.fin_ss.at[k, j], r.fin_rs.at[k, j], j)
            cp.start()
            cps.append(cp)
        return own, cps

    root = nb // 2 - 1 + c
    at_root = z == root
    above = z > root
    below = z < root
    has_u = (below & (z > 0)) | (above & (z < nb - 1)) | (at_root & (root > 0))
    outer = (below & (z > 0)) | (above & (z < nb - 1))
    has_b = at_root & (root < nb - 1)

    def zcopy(src, dst, ss, rs, dz):
        return copy_to(src, dst, ss, rs, dict(batch=z + dz))

    def piece(i, own):
        @pl.when(has_u)
        def _():
            zcopy(r.zu.at[i], r.zu.at[i], r.z_s0.at[i], r.z_ur.at[i], 0).wait_recv()

        @pl.when(has_b)
        def _():
            zcopy(r.zb.at[i], r.zb.at[i], r.z_s0.at[i], r.z_br.at[i], 0).wait_recv()

        @pl.when(jnp.logical_not(has_u))
        def _():
            r.zs[i] = own().astype(BF16)

        @pl.when(has_u & jnp.logical_not(has_b))
        def _():
            r.zs[i] = (own() + r.zu[i].astype(F32)).astype(BF16)

        @pl.when(has_u & has_b)
        def _():
            r.zs[i] = (own() + r.zu[i].astype(F32) + r.zb[i].astype(F32)).astype(BF16)

        @pl.when(below)
        def _():
            zcopy(r.zs.at[i], r.zu.at[i], r.z_s0.at[i], r.z_ur.at[i], 1).start()

        @pl.when(above & (z > root + 1))
        def _():
            zcopy(r.zs.at[i], r.zu.at[i], r.z_s0.at[i], r.z_ur.at[i], -1).start()

        @pl.when(z == root + 1)
        def _():
            zcopy(r.zs.at[i], r.zb.at[i], r.z_s0.at[i], r.z_br.at[i], -1).start()

        @pl.when(at_root)
        def _():
            @pl.when(root > 0)
            def _():
                zcopy(r.zs.at[i], r.zb.at[i], r.z_s0.at[i], r.z_br.at[i], -1).start()

            @pl.when(root < nb - 1)
            def _():
                zcopy(r.zs.at[i], r.zb.at[i], r.z_s1.at[i], r.z_br.at[i], 1).start()

    def og_local(i, src):
        return pltpu.make_async_copy(src.at[i], r.og.at[i // 4, c, i % 4], r.og_loc.at[i])

    def og_across(i, src):
        return across(src.at[i], r.og.at[i // 4, c, i % 4], r.og_ss.at[i], r.og_rs.at[i])

    def ex_local(q, src):
        return pltpu.make_async_copy(src.at[12 + q, :, pl.ds(512, 128)], r.ex.at[h, c, q], r.ex_loc.at[q])

    def ex_plane(q, src, j, x):
        return copy_to(
            src.at[12 + q, :, pl.ds(512, 128)], r.ex.at[h, c, q],
            r.ex_ss.at[q, 2 * j + x], r.ex_rs.at[q, 2 * j + x], plane_id(j, x),
        )

    def spread(i):
        def place(src):
            og_local(i, src).start()
            og_across(i, src).start()
            if isinstance(i, int) and i >= 12:
                ex_local(i - 12, src).start()
                for j, x in plane:
                    ex_plane(i - 12, src, j, x).start()

        @pl.when(jnp.logical_not(at_root))
        def _():
            zcopy(r.zb.at[i], r.zb.at[i], r.z_s1.at[i], r.z_br.at[i], 0).wait_recv()

            @pl.when(below & outer)
            def _():
                zcopy(r.zb.at[i], r.zb.at[i], r.z_s1.at[i], r.z_br.at[i], -1).start()

            @pl.when(above & outer)
            def _():
                zcopy(r.zb.at[i], r.zb.at[i], r.z_s1.at[i], r.z_br.at[i], 1).start()

            place(r.zb)

        @pl.when(at_root)
        def _():
            place(r.zs)

    def ffn_half(t):
        sl = pl.ds(4 * t, 4)
        return across(r.sf.at[sl], r.rf.at[sl], r.f_ss.at[t], r.f_rs.at[t])

    def ffn_piece(i):
        @pl.when(i % 4 == 0)
        def _():
            ffn_half(i // 4).wait_recv()

        piece(i, lambda: r.gown[i] + r.rf[i].astype(F32))

    forward(0)
    forward(1)
    out_own, out_cps = finish(0, r.d_res[...], r.out)

    def norm_bwd(x, gain, dn):
        inv = lax.rsqrt(jnp.mean(x * x, axis=-1, keepdims=True) + EPS)
        u = gain * dn
        dx = inv * u - x * (inv * inv * inv) * jnp.mean(x * u, axis=-1, keepdims=True)
        return dx, jnp.sum(dn * x * inv, axis=0, keepdims=True)

    mine_half = pl.ds(pl.multiple_of(c * hd2, hd2), hd2)
    other_half = pl.ds(pl.multiple_of((1 - c) * hd2, hd2), hd2)

    def backward(p):
        if p == 1:
            loads.cot.wait()
            for j in range(HEADS):
                pr = pl.ds(pl.multiple_of(peer_of(h, j) * rows, rows), rows)
                pos = c * half + peer_of(h, j) * rows + lax.broadcasted_iota(jnp.int32, (rows, 1), 0)
                ok = (pos < length).astype(F32)
                for b, lo, w in blocks(d):
                    block = r.cot_v[lo : lo + w, pr].astype(F32).T * ok
                    r.df[p, j, :, lo : lo + w] = block.astype(BF16)
                    if j == 0:
                        r.d_res[:, lo : lo + w] = block
        else:
            block = r.d_res[...] * valid
            r.d_res[...] = block
            r.df[p, 0] = block.astype(BF16)
        ag = []
        if p == 0:
            for j in (1, 2, 3):
                cp = remote(r.df.at[p, 0], r.df.at[p, j], r.df_ss.at[j], r.df_rs.at[j], j)
                cp.start()
                ag.append(cp)
        rs = []
        e = 3 - p
        for j in (1, 2, 3, 0) if p == 1 else (0, 1, 2, 3):
            if p == 0 and j:
                ag[j - 1].wait_recv()
            d_act = nn(r.df[p, j], wd_v[...])
            gate, up = r.gate[p, j], r.up[p, j]
            s = 1.0 / (1.0 + jnp.exp(-gate))
            dg = (d_act * up * s * (1.0 + gate * (1.0 - s))).astype(BF16)
            du = (d_act * (gate * s)).astype(BF16)
            r.act[j] = (gate * s * up).astype(BF16)
            r.dg[j] = dg
            r.du[j] = du
            part = nt(dg, wg_v[...]) + nt(du, wu_v[...])
            if j == 0:
                r.part[...] = part
            else:
                r.psend[j - 1] = part.astype(BF16)
                cp = remote(r.psend.at[j - 1], r.precv.at[1 - p, j - 1], r.p_ss.at[e, j], r.p_rs.at[e, j], j)
                cp.start()
                rs.append(cp)
        for t, rhs in ((0, r.dg), (1, r.du), (2, r.act)):
            if t != 1:
                src = r.nf if t == 0 else r.df
                for j in range(HEADS):
                    store_t(lhs.at[:, j * rows : (j + 1) * rows], src[p, j])
            right = rhs[...].reshape(half, ff)
            theirs = nn(lhs[other_half, :], right)
            for q in range(4):
                v = theirs[q * cr : (q + 1) * cr]
                if p == 0:
                    v = v + r.sf[4 * t + q].astype(F32)
                r.sf[4 * t + q] = v.astype(BF16)
            if p == 0:
                ffn_half(t).start()
            ours = nn(lhs[mine_half, :], right)
            for q in range(4):
                v = ours[q * cr : (q + 1) * cr]
                if p == 0:
                    v = v + r.gown[4 * t + q]
                r.gown[4 * t + q] = v
        dn = r.part[...].astype(BF16).astype(F32)
        for j in (1, 2, 3):
            rs[j - 1].wait_recv()
            dn = dn + r.precv[1 - p, j - 1].astype(F32)
        dx, dgain = norm_bwd(r.mid[p], gain_f(), dn)
        d_mid = r.d_res[...] + dx
        r.d_mid[...] = d_mid
        if p == 1:
            r.gain_v[1:2, :] = dgain
        else:
            r.gain_v[1:2, :] += dgain
        da = d_mid.astype(BF16)
        store_t(r.dat.at[:, p * rows : (p + 1) * rows], da)
        r.wide[:, :d] = nt(da, r.wo_v[...])
        for b, lo, w in blocks(d):
            y = r.wide[:, lo : lo + 128]
            g, o = head_row(2 * b)
            r.ou[g, o : o + rows, :] = jnp.where(low, 0.0, swap(y)).astype(BF16)
            if 2 * b + 1 < QH:
                g, o = head_row(2 * b + 1)
                r.ou[g, o : o + rows, :] = jnp.where(low, 0.0, y).astype(BF16)

        @pl.loop(0, KV)
        def _(g):
            kv = r.kv[p, g]
            acc = None
            for k in range(GQ):
                q = r.ql[p, g, k * rows : (k + 1) * rows, :]
                o = r.ou[g, k * rows : (k + 1) * rows, :]
                s = nt(q, kv)
                s = jnp.where(r.bias[...] < 0.0, NEG, s)
                lse = jnp.sum(jnp.where(lane == g * GQ + k, r.lse[p], 0.0), axis=-1, keepdims=True)
                pr = jnp.exp(s - lse)
                dpr = nt(o, kv)
                delta = jnp.sum(pr * dpr, axis=-1, keepdims=True)
                ds = (pr * (dpr - delta)).astype(BF16)
                r.heads[g * GQ + k] = unrope(nn(ds, kv) * HD ** (-0.5))
                t = nn(o.T, pr.astype(BF16)) + nn(q.T, ds)
                acc = t if acc is None else acc + t
            r.dkv[g] = acc[:, :half]
            r.dkv_ctx[g] = acc[:, half:].astype(BF16)
            if p == 0:
                ffn_piece(g)

                @pl.when(g >= 2)
                def _():
                    spread(g - 2)

        hop = across(r.dkv_ctx, r.dkv_ctx_r.at[p], r.dc_ss.at[p], r.dc_rs.at[p])

        @pl.when(c == 1)
        def _():
            hop.start()

        mine = pl.ds(p * rows, rows)
        for b, lo, w in blocks(d):
            y = r.heads[2 * b]
            if 2 * b + 1 < QH:
                y = jnp.where(low, y, swap(r.heads[2 * b + 1]))
            r.dq[:, lo : lo + w] = y[:, :w].astype(BF16)
        for g in range(KV):
            both = jnp.where(low, r.heads[g * GQ], swap(r.heads[g * GQ + 1]))
            r.dpg[g, mine, 0:128] = both.astype(BF16)

        @pl.when(c == 0)
        def _():
            hop.wait_recv()
            r.dkv[...] += r.dkv_ctx_r[p].astype(F32)

        ks = []
        for j in (1, 2, 3):
            r.dkv_s[j - 1] = r.dkv[:, :, j * rows : (j + 1) * rows].astype(BF16)
            cp = remote(r.dkv_s.at[j - 1], r.dkv_r.at[j - 1], r.dkv_ss.at[p, j], r.dkv_rs.at[p, j], j)
            cp.start()
            ks.append(cp)
        r.wide[:, :d] = nt(r.dq[...], r.wq_v[...])
        for j in (1, 2, 3):
            ks[j - 1].wait_recv()
        keys, vals = [], []
        for g in range(KV):
            t = r.dkv[g, :, 0:rows]
            for j in range(3):
                t = t + r.dkv_r[j, g].astype(F32)
            t = t.T
            kt, vt = unrope(t), swap(t)
            keys.append(kt)
            vals.append(t)
            r.dpg[g, mine, 128:256] = jnp.where(low, r.heads[g * GQ + 2], swap(kt)).astype(BF16)
            r.dpg[g, mine, 256:384] = jnp.where(low, vt, 0.0).astype(BF16)
        for b, lo, w in blocks(KV * HD):
            kb, vb = keys[2 * b], swap(vals[2 * b])
            if 2 * b + 1 < KV:
                kb = jnp.where(low, kb, swap(keys[2 * b + 1]))
                vb = jnp.where(low, vb, vals[2 * b + 1])
            r.dk[:, lo : lo + w] = kb[:, :w].astype(BF16)
            r.dv[:, lo : lo + w] = vb[:, :w].astype(BF16)
        dna = r.wide[:, :d] + nn(r.dk[...], r.wk_v[...]) + nn(r.dv[...], r.wv_v[...])
        dx, dgain = norm_bwd(r.res[p], gain_a(), dna)
        r.d_res[...] = r.d_mid[...] + dx
        if p == 1:
            r.gain_v[0:1, :] = dgain
        else:
            r.gain_v[0:1, :] += dgain
        for cp in ag + rs + ks:
            cp.wait_send()

        @pl.when(c == 1)
        def _():
            hop.wait_send()

    backward(1)
    backward(0)
    gin_own, gin_cps = finish(1, r.d_res[...], r.gin)

    me = 2 * h + c
    r.gain_p[me] = r.gain_v[...]
    gp = [copy_to(r.gain_p.at[me], r.gain_p.at[me], r.gp_ss.at[2 * j + x], r.gp_rs.at[2 * j + x], plane_id(j, x))
          for j, x in plane]
    for cp in gp:
        cp.start()

    def a_half(g):
        src = r.wf.at[pl.ds(pl.multiple_of(g * hd2, hd2), hd2), pl.ds(0, 512)]
        return across(src, r.ra.at[g], r.a_ss.at[g], r.a_rs.at[g])

    @pl.loop(0, KV)
    def _(g):
        def product(rows_of):
            first = nn(r.nat[rows_of, :], r.dpg[g])
            second = nn(r.dat[rows_of, :], r.aog[g])
            return first[:, :256], first[:, 256:] + second[:, :128], second[:, 128:]

        def put(dst, parts):
            dst[:, 0:256] = parts[0].astype(BF16)
            dst[:, 256:384] = parts[1].astype(BF16)
            dst[:, 384:512] = parts[2].astype(BF16)

        put(r.wf.at[pl.ds(pl.multiple_of(g * hd2, hd2), hd2)], product(other_half))
        a_half(g).start()
        put(r.ha.at[g], product(mine_half))

    for cp in gp:
        cp.wait_recv()
    total = r.gain_p[0]
    for k in range(1, 2 * HEADS):
        total = total + r.gain_p[k]
    r.gain_z[z] = total
    gz = [copy_to(r.gain_z.at[z], r.gain_z.at[z], r.gz_ss.at[k], r.gz_rs.at[k], dict(batch=(z + k) % nb))
          for k in range(1, nb)]
    for cp in gz:
        cp.start()

    @pl.loop(5, 9)
    def _(i):
        ffn_piece(i)
        spread(i - 2)

    @pl.loop(0, KV)
    def _(g):
        a_half(g).wait_recv()

    def own_share(to, q):
        at = pl.ds(q * cr, cr)
        g0, g1 = r.gid[to], r.gid[HEADS]
        first = r.ha[g0, at, :].astype(F32) + r.ra[g0, at, :].astype(F32)
        cols = pl.ds(pl.multiple_of(to * 128, 128), 128)
        second = r.ha[g1, at, cols].astype(F32) + r.ra[g1, at, cols].astype(F32)
        return jnp.concatenate([first, second], axis=1)

    for t in range(3):
        ffn_half(t).wait_send()

    def head_share(j):
        sl = pl.ds(4 * (j - 1), 4)
        return remote(r.sf.at[sl], r.rf2.at[sl], r.h_ss.at[j], r.h_rs.at[j], j)

    for j in (1, 2, 3):
        for q in range(4):
            r.sf[4 * (j - 1) + q] = own_share(peer_of(h, j), q).astype(BF16)
        head_share(j).start()

    @pl.loop(9, 12)
    def _(i):
        ffn_piece(i)
        spread(i - 2)

    spread(10)
    spread(11)
    for j in (1, 2, 3):
        head_share(j).wait_recv()

    for q in range(4):
        def own(q=q):
            v = own_share(h, q)
            for j in range(3):
                v = v + r.rf2[4 * j + q].astype(F32)
            return v

        piece(12 + q, own)
        if q:
            spread(11 + q)
    spread(15)

    for cp in gz:
        cp.wait_recv()
    total = r.gain_z[0]
    for k in range(1, nb):
        total = total + r.gain_z[k]
    r.gain_v[...] = total
    gains_out = pltpu.make_async_copy(r.gain_v, r.gains_out, r.loc_sem.at[2])
    gains_out.start()

    gains_out.wait()
    for cp in gp + gz:
        cp.wait_send()
    for j in (1, 2, 3):
        head_share(j).wait_send()

    @pl.loop(0, KV)
    def _(g):
        a_half(g).wait_send()

    @pl.loop(0, 16)
    def _(i):
        og_local(i, r.zs).wait()
        og_across(i, r.zs).wait_send()
        og_across(i, r.zs).wait_recv()

        @pl.when(jnp.logical_not(at_root) | (root > 0))
        def _():
            zcopy(r.zs.at[i], r.zs.at[i], r.z_s0.at[i], r.z_ur.at[i], 0).wait_send()

        @pl.when(outer | (at_root & (root < nb - 1)))
        def _():
            zcopy(r.zs.at[i], r.zs.at[i], r.z_s1.at[i], r.z_ur.at[i], 0).wait_send()

    for q in range(4):
        ex_local(q, r.zs).wait()
        for j, x in plane:
            ex_plane(q, r.zs, j, x).wait_send()
            ex_plane(q, r.zs, j, x).wait_recv()
    for own, cps in ((out_own, out_cps), (gin_own, gin_cps)):
        own.wait()
        for cp in cps:
            cp.wait_recv()
            cp.wait_send()


def body(nb, hidden_in, cotangent, lengths, owners, w_query, w_key, w_value, w_output, gate_weight, up_weight, down_weight,
         gain_attn, gain_ffn):
    half, d = hidden_in.shape[1:]
    ff = gate_weight.shape[1]
    rows = half // HEADS
    cr = d // 8
    scratch = scratch_of(rows, d, ff, nb)
    anyspec = pl.BlockSpec(memory_space=pl.ANY)
    smem = pl.BlockSpec(memory_space=pltpu.SMEM)
    sd = jax.ShapeDtypeStruct
    ins = dict(
        hid=anyspec, cot=anyspec, len=smem, gid=smem, gains=anyspec, tab=anyspec,
        wq=anyspec, wk=anyspec, wv=anyspec, wo=anyspec, wg=anyspec, wu=anyspec, wd=anyspec,
    )
    outs = dict(
        out=sd((d, half), BF16), gin=sd((d, half), BF16),
        og=sd((4, 2, 4, cr, ff), BF16), ex=sd((HEADS, 2, 4, cr, 128), BF16), gains_out=sd((2, d), F32),
    )
    names = tuple(ins) + tuple(outs) + tuple(scratch)
    owned = (owners[None, :] == jnp.arange(HEADS, dtype=jnp.int32)[:, None]).astype(jnp.int32)
    group = jnp.arange(KV, dtype=jnp.int32)
    first = jnp.min(jnp.where(owned == 1, group[None, :], KV), axis=1)
    last = jnp.max(jnp.where(owned == 1, group[None, :], -1), axis=1)
    second = jnp.max(jnp.where(last != first, last, -1))
    gid = jnp.concatenate([first, second[None]]).astype(jnp.int32)
    o, gin, og, ex, gains = pl.pallas_call(
        functools.partial(step_kernel, names, rows, d, ff, nb),
        out_shape=tuple(outs.values()),
        in_specs=list(ins.values()),
        out_specs=(anyspec,) * len(outs),
        scratch_shapes=list(scratch.values()),
        compiler_params=pltpu.CompilerParams(
            collective_id=0, has_side_effects=True, vmem_limit_bytes=67043328
        ),
    )(
        hidden_in[0].T, cotangent[0].T, lengths, gid, jnp.stack([gain_attn, gain_ffn]),
        jnp.asarray(rope_table(2 * half)), w_query, w_key.T, w_value.T, w_output, gate_weight, up_weight, down_weight.T,
    )
    og = og.reshape(4, d, ff)
    has_second = jnp.sum(owned[lax.axis_index("head")]) > 1
    slot0 = og[3, :, :512]
    slot1 = ex.reshape(HEADS, d, 128).transpose(1, 0, 2).reshape(d, 512)
    slot1 = jnp.where(has_second, slot1, jnp.zeros_like(slot1))
    gw = GQ * HD
    pair = lambda lo, hi: jnp.concatenate([slot0[:, lo:hi], slot1[:, lo:hi]], axis=1).astype(F32)
    gq, gk, gv, go = pair(0, gw), pair(gw, gw + HD), pair(gw + HD, gw + 2 * HD), pair(gw + 2 * HD, 512)
    return (
        o.T[None], gin.T.astype(F32)[None], gq, gk, gv, go.T,
        og[0].astype(F32), og[1].astype(F32), og[2].astype(F32).T, gains[0], gains[1],
    )


def solution(mesh):
    rep = P()
    io = P("batch", "ctx", None)
    in_specs = (io, io, P("batch"), rep, rep, rep, rep, rep, P(None, "head"), P(None, "head"), P("head", None), rep, rep)
    out_specs = (io, io, P(None, "head"), P(None, "head"), P(None, "head"), P("head", None), P(None, "head"),
                 P(None, "head"), P("head", None), rep, rep)
    return jax.shard_map(
        functools.partial(body, mesh.shape["batch"]), mesh=mesh, in_specs=in_specs, out_specs=out_specs, check_vma=False
    )
```

```python
import functools
import math
from types import SimpleNamespace

import jax
import jax.numpy as jnp
import numpy as np
from jax import lax
from jax.experimental import pallas as pl
from jax.experimental.pallas import tpu as pltpu
from jax.sharding import PartitionSpec as P

KV = 5
HD = 64
GQ = 3
QH = KV * GQ
HEADS = 4
EPS = 1e-05
NEG = -1e30
MESH = pl.DeviceIdType.MESH
F32 = jnp.float32
BF16 = jnp.bfloat16


def nn(a, b):
    return lax.dot_general(a, b, (((1,), (0,)), ((), ())), preferred_element_type=F32)


def nt(a, b):
    return lax.dot_general(a, b, (((1,), (1,)), ((), ())), preferred_element_type=F32)


def tn(a, b):
    return lax.dot_general(a, b, (((0,), (0,)), ((), ())), preferred_element_type=F32)


def rope_table(slots):
    inverse = np.exp(np.arange(HD // 2, dtype=np.float32) * np.float32(-2.0 * math.log(10000.0) / HD))
    angles = np.arange(slots, dtype=np.float32)[:, None] * inverse[None, :].astype(np.float32)
    cos, sin = np.cos(angles).astype(np.float32), np.sin(angles).astype(np.float32)
    return np.concatenate([cos] * 4 + [sin] * 4, axis=1)


def peer_of(h, j):
    return (h, h + 1 - 2 * (h % 2), (h + 2) % 4, 3 - h)[j]


def scratch_of(rows, d, ff, nb):
    n = HEADS
    half = n * rows
    keys = 2 * half
    dp = -(-d // 128) * 128
    kp = -(-KV * HD // 128) * 128
    cr = d // 8
    v = pltpu.VMEM
    dma = pltpu.SemaphoreType.DMA
    return dict(
        hid_v=v((d, rows), BF16),
        cot_v=v((d, half), BF16),
        tab_v=v((rows, 256), F32),
        gains_v=v((2, d), F32),
        wq_v=v((d, QH * HD), BF16),
        wk_v=v((KV * HD, d), BF16),
        wv_v=v((KV * HD, d), BF16),
        wo_v=v((QH * HD, d), BF16),
        wf=v((3 * d, ff), BF16),
        res=v((2, rows, d), F32),
        mid=v((2, rows, d), F32),
        nat=v((d, 2 * rows), BF16),
        dat=v((d, 2 * rows), BF16),
        ql=v((2, KV, GQ * rows, 128), BF16),
        kv=v((2, KV, keys, 128), BF16),
        lse=v((2, rows, 128), F32),
        at=v((rows, d), BF16),
        nf=v((2, n, rows, d), BF16),
        gate=v((2, n, rows, ff), F32),
        up=v((2, n, rows, ff), F32),
        act=v((n, rows, ff), BF16),
        bias=v((rows, keys), F32),
        wide=v((rows, dp), F32),
        wide2=v((rows, kp), F32),
        wide3=v((rows, kp), F32),
        heads=v((QH, rows, 128), F32),
        part=v((rows, d), F32),
        psend=v((3, rows, d), BF16),
        precv=v((2, 3, rows, d), BF16),
        d_res=v((rows, d), F32),
        d_mid=v((rows, d), F32),
        df=v((2, n, rows, d), BF16),
        dg=v((n, rows, ff), BF16),
        du=v((n, rows, ff), BF16),
        ou=v((KV, GQ * rows, 128), BF16),
        dq=v((rows, d), BF16),
        dk=v((rows, KV * HD), BF16),
        dv=v((rows, KV * HD), BF16),
        dpg=v((KV, 2 * rows, 384), BF16),
        aog=v((KV, 2 * rows, 256), BF16),
        dkv=v((KV, 128, half), F32),
        dkv_ctx=v((KV, 128, half), BF16),
        dkv_ctx_r=v((2, KV, 128, half), BF16),
        dkv_s=v((KV, 3, 128, rows), BF16),
        dkv_r=v((KV, 3, 128, rows), BF16),
        fin=v((2, d, rows), BF16),
        gown=v((12, cr, ff), F32),
        sf=v((12, cr, ff), BF16),
        rf=v((12, cr, ff), BF16),
        rf2=v((12, cr, ff), BF16),
        zs=v((16, cr, ff), BF16),
        zu=v((16, cr, ff), BF16),
        zb=v((16, cr, ff), BF16),
        ha=v((KV, d // 2, 512), BF16),
        ra=v((KV, d // 2, 512), BF16),
        gain_v=v((2, d), F32),
        gain_p=v((2 * n, 2, d), F32),
        gain_z=v((nb, 2, d), F32),
        in_sem=dma((11,)),
        loc_sem=dma((8,)),
        kv_ss=dma((2, KV)),
        kv_rs=dma((2, KV)),
        kvc_ss=dma((2, KV)),
        kvc_rs=dma((2, KV)),
        ag_ss=dma((5, 6)),
        ag_rs=dma((5, 6)),
        p_ss=dma((4, 4)),
        p_rs=dma((4, 4)),
        dc_ss=dma((2, KV)),
        dc_rs=dma((2, KV)),
        dkv_ss=dma((2, KV)),
        dkv_rs=dma((2, KV)),
        f_ss=dma((3,)),
        f_rs=dma((3,)),
        z_s0=dma((16,)),
        z_s1=dma((16,)),
        z_ur=dma((16,)),
        z_br=dma((16,)),
        og_loc=dma((16,)),
        og_ss=dma((16,)),
        og_rs=dma((16,)),
        a_ss=dma((KV,)),
        a_rs=dma((KV,)),
        h_ss=dma((4,)),
        h_rs=dma((4,)),
        ex_loc=dma((4,)),
        ex_ss=dma((4, 8)),
        ex_rs=dma((4, 8)),
        gp_ss=dma((8,)),
        gp_rs=dma((8,)),
        gz_ss=dma((nb,)),
        gz_rs=dma((nb,)),
    )


def step_kernel(names, rows, d, ff, nb, *refs):
    r = SimpleNamespace(**dict(zip(names, refs)))
    wg_v, wu_v, wd_v = (r.wf.at[pl.ds(t * d, d)] for t in range(3))
    lhs = r.cot_v
    h = lax.axis_index("head")
    c = lax.axis_index("ctx")
    z = lax.axis_index("batch")
    half = HEADS * rows
    hd2 = d // 2
    cr = d // 8
    lane = lax.broadcasted_iota(jnp.int32, (rows, 128), 1)
    low = lane < HD
    quarter = (lane % HD) < HD // 2

    def copy_to(src, dst, ss, rs, where):
        return pltpu.make_async_remote_copy(
            src_ref=src, dst_ref=dst, send_sem=ss, recv_sem=rs, device_id=where, device_id_type=MESH
        )

    def remote(src, dst, ss, rs, j):
        return copy_to(src, dst, ss, rs, dict(head=peer_of(h, j)))

    def across(src, dst, ss, rs):
        return copy_to(src, dst, ss, rs, dict(ctx=1 - c))

    def load(k, src, dst):
        return pltpu.make_async_copy(src, dst, r.in_sem.at[k])

    my_rows = pl.ds(pl.multiple_of(h * rows, rows), rows)
    my_pos = pl.ds(pl.multiple_of(c * half + h * rows, rows), rows)
    loads = SimpleNamespace(
        hid=load(0, r.hid.at[:, my_rows], r.hid_v),
        gains=load(1, r.gains, r.gains_v),
        wk=load(3, r.wk, r.wk_v),
        wv=load(4, r.wv, r.wv_v),
        tab=load(5, r.tab.at[my_pos], r.tab_v),
        wq=load(2, r.wq, r.wq_v),
        wo=load(6, r.wo, r.wo_v),
        wg=load(7, r.wg, wg_v),
        wu=load(8, r.wu, wu_v),
        wd=load(9, r.wd, wd_v),
        cot=load(10, r.cot, r.cot_v),
    )
    for cp in vars(loads).values():
        cp.start()

    plane = [(j, x) for j in range(HEADS) for x in range(2) if (j, x) != (0, 0)]

    def plane_id(j, x):
        return dict(head=peer_of(h, j), ctx=1 - c if x else c)

    barrier = pltpu.get_barrier_semaphore()
    for j, x in plane:
        pl.semaphore_signal(barrier, inc=1, device_id=plane_id(j, x), device_id_type=MESH)
    for k in range(1, nb):
        pl.semaphore_signal(barrier, inc=1, device_id=dict(batch=(z + k) % nb), device_id_type=MESH)
    pl.semaphore_wait(barrier, len(plane) + nb - 1)

    length = r.len[0]
    row_pos = c * half + h * rows + lax.broadcasted_iota(jnp.int32, (rows, 1), 0)
    valid = (row_pos < length).astype(F32)

    for blk in range(2 * HEADS):
        own = blk < HEADS
        base = (c if own else 1 - c) * half + peer_of(h, blk % HEADS) * rows
        kp = base + lax.broadcasted_iota(jnp.int32, (rows, rows), 1)
        qp = c * half + h * rows + lax.broadcasted_iota(jnp.int32, (rows, rows), 0)
        ok = (kp <= qp) & (kp < length)
        r.bias[:, blk * rows : (blk + 1) * rows] = jnp.where(ok, 0.0, NEG)

    zero_w = jnp.zeros((rows, 128), F32)
    dp, kw = r.wide.shape[1], r.wide2.shape[1]
    r.wide[:, dp - 128 :] = zero_w
    r.wide2[:, kw - 128 :] = zero_w
    r.wide3[:, kw - 128 :] = zero_w
    r.lse[0] = zero_w
    r.lse[1] = zero_w

    @pl.when(c == 0)
    def _():
        for p in range(2):
            r.kv[p, :, half:, :] = jnp.zeros((KV, half, 128), BF16)

    def rms(x, gain):
        inv = lax.rsqrt(jnp.mean(x * x, axis=-1, keepdims=True) + EPS)
        return x * inv * gain

    def turned(x):
        return jnp.where(quarter, -pltpu.roll(x, 128 - HD // 2, 1), pltpu.roll(x, HD // 2, 1))

    def rope(x):
        return x * r.tab_v[:, 0:128] + turned(x) * r.tab_v[:, 128:256]

    def unrope(x):
        return x * r.tab_v[:, 0:128] - turned(x) * r.tab_v[:, 128:256]

    def swap(x):
        return pltpu.roll(x, HD, 1)

    def blocks(width):
        return [(b, b * 128, min(128, width - b * 128)) for b in range(-(-width // 128))]

    def head_row(i):
        return i // GQ, (i % GQ) * rows

    def store_t(dst, src):
        for b, lo, w in blocks(d):
            dst[lo : lo + w, :] = src[:, lo : lo + w].T

    gain_a = lambda: r.gains_v[0:1, :]
    gain_f = lambda: r.gains_v[1:2, :]

    loads.tab.wait()
    loads.gains.wait()
    loads.hid.wait()
    for b, lo, w in blocks(d):
        r.res[0, :, lo : lo + w] = r.hid_v[lo : lo + w, :].astype(F32).T

    def gather(e, src, dst, by_owner=False):
        def hop(k, ref, to, j):
            return remote(ref, to, r.ag_ss.at[e, k], r.ag_rs.at[e, k], j)

        at = (lambda j, near, x: dst(near, x)) if by_owner else (lambda j, near, x: dst(j, x))
        first = [hop(0, src(0), at(1, 0, 0), 1), hop(3, src(1), at(2, 0, 1), 2), hop(1, src(1), at(1, 0, 1), 1),
                 hop(2, src(0), at(2, 0, 0), 2)]
        relay = [hop(4, dst(1, 0), at(3, 1, 0), 2), hop(5, dst(2, 1), at(3, 2, 1), 1)]
        for cp in first:
            cp.start()

        def hand_on():
            first[0].wait_recv()
            relay[0].start()
            first[1].wait_recv()
            relay[1].start()

        def wait(j):
            for cp in ((first[2],), (first[3],), relay)[j - 1]:
                cp.wait_recv()

        def drain():
            for cp in first + relay:
                cp.wait_send()

        return SimpleNamespace(hand_on=hand_on, wait=wait, drain=drain)

    def halves(ref):
        n = ref.shape[0] // 2
        return lambda x: ref.at[pl.ds(x * n, n)]

    def forward(p):
        x = r.res[p]
        na = rms(x, gain_a()).astype(BF16)
        store_t(r.nat.at[:, p * rows : (p + 1) * rows], na)
        if p == 0:
            loads.wk.wait()
            loads.wv.wait()
        r.wide2[:, : KV * HD] = nt(na, r.wk_v[...])
        r.wide3[:, : KV * HD] = nt(na, r.wv_v[...])
        for b in range(-(-KV // 2)):
            kb = rope(r.wide2[:, b * 128 : (b + 1) * 128])
            vb = r.wide3[:, b * 128 : (b + 1) * 128]
            r.kv[p, 2 * b, 0:rows, :] = jnp.where(low, kb, swap(vb)).astype(BF16)
            if 2 * b + 1 < KV:
                r.kv[p, 2 * b + 1, 0:rows, :] = jnp.where(low, swap(kb), vb).astype(BF16)

        def to_peer(j, g):
            return remote(
                r.kv.at[p, g, pl.ds(0, rows)], r.kv.at[p, g, pl.ds(j * rows, rows)],
                r.kv_ss.at[p, g], r.kv_rs.at[p, g], j,
            )

        def to_partner(j, g):
            return across(
                r.kv.at[p, g, pl.ds(j * rows, rows)], r.kv.at[p, g, pl.ds(half + j * rows, rows)],
                r.kvc_ss.at[p, g], r.kvc_rs.at[p, g],
            )

        def all_peers(g):
            span = r.kv.at[p, g, pl.ds(rows, 3 * rows)]
            return remote(span, span, r.kv_ss.at[p, g], r.kv_rs.at[p, g], 1)

        def all_partner(g):
            span = r.kv.at[p, g, pl.ds(half, half)]
            return across(span, span, r.kvc_ss.at[p, g], r.kvc_rs.at[p, g])

        for g in range(KV):
            for j in (1, 2, 3):
                to_peer(j, g).start()

            @pl.when(c == 0)
            def _():
                to_partner(0, g).start()

        def arrive(g):
            all_peers(g).wait_recv()

            @pl.when(c == 0)
            def _():
                for j in (1, 2, 3):
                    to_partner(j, g).start()

        if p == 0:
            loads.wq.wait()
        r.wide[:, :d] = nn(na, r.wq_v[...])
        for b, lo, w in blocks(d):
            y = rope(r.wide[:, lo : lo + 128]).astype(BF16).astype(F32) * HD ** (-0.5)
            g, o = head_row(2 * b)
            r.ql[p, g, o : o + rows, :] = jnp.where(low, y, 0.0).astype(BF16)
            if 2 * b + 1 < QH:
                g, o = head_row(2 * b + 1)
                r.ql[p, g, o : o + rows, :] = jnp.where(low, swap(y), 0.0).astype(BF16)

        arrive(0)

        @pl.loop(0, KV)
        def _(g):
            @pl.when(g < KV - 1)
            def _():
                arrive(g + 1)

            @pl.when(c == 1)
            def _():
                all_partner(g).wait_recv()

            kv = r.kv[p, g]
            for k in range(GQ):
                s = nt(r.ql[p, g, k * rows : (k + 1) * rows, :], kv)
                s = jnp.where(r.bias[...] < 0.0, NEG, s)
                m = jnp.max(s, axis=-1, keepdims=True)
                e = jnp.exp(s - m)
                t = jnp.sum(e, axis=-1, keepdims=True)
                r.lse[p] += jnp.where(lane == g * GQ + k, m + jnp.log(t), 0.0)
                r.heads[g * GQ + k] = nn((e / t).astype(BF16), kv)

        mine = pl.ds(p * rows, rows)
        for g in range(KV):
            o0, o1, o2 = (r.heads[g * GQ + k] for k in range(GQ))
            r.aog[g, mine, 0:128] = jnp.where(low, 0.0, o0).astype(BF16)
            r.aog[g, mine, 128:256] = jnp.where(low, swap(o1), o2).astype(BF16)
        for b, lo, w in blocks(d):
            first = swap(r.heads[2 * b])
            both = jnp.where(low, first, r.heads[2 * b + 1]) if 2 * b + 1 < QH else first
            r.at[:, lo : lo + w] = both[:, :w].astype(BF16)
        if p == 0:
            loads.wo.wait()
        mid = r.res[p] + nn(r.at[...], r.wo_v[...])
        r.mid[p] = mid
        r.nf[p, 0] = rms(mid, gain_f()).astype(BF16)
        ag = gather(p, halves(r.nf.at[p, 0]), lambda j, x: halves(r.nf.at[p, j])(x))
        if p == 0:
            loads.wg.wait()
            loads.wu.wait()
            loads.wd.wait()
        rs = []
        for j in range(HEADS):
            if j == 1:
                ag.hand_on()
            if j:
                ag.wait(j)
            nf = r.nf[p, j]
            gate = nn(nf, wg_v[...])
            up = nn(nf, wu_v[...])
            r.gate[p, j] = gate
            r.up[p, j] = up
            act = (gate / (1.0 + jnp.exp(-gate)) * up).astype(BF16)
            part = nt(act, wd_v[...])
            if j == 0:
                r.part[...] = part
            else:
                r.psend[j - 1] = part.astype(BF16)
                cp = remote(r.psend.at[j - 1], r.precv.at[p, j - 1], r.p_ss.at[p, j], r.p_rs.at[p, j], j)
                cp.start()
                rs.append(cp)
        total = r.part[...].astype(BF16).astype(F32)
        for j in (1, 2, 3):
            rs[j - 1].wait_recv()
            total = total + r.precv[p, j - 1].astype(F32)
        result = valid * (r.mid[p] + total)
        if p == 0:
            r.res[1] = result
        else:
            r.d_res[...] = result
        ag.drain()
        for cp in rs:
            cp.wait_send()

        @pl.loop(0, KV)
        def _(g):
            all_peers(g).wait_send()

            @pl.when(c == 0)
            def _():
                all_partner(g).wait_send()

    def finish(k, value, out):
        store_t(r.fin.at[k], value.astype(BF16))
        own = pltpu.make_async_copy(r.fin.at[k], out.at[:, my_rows], r.loc_sem.at[k])
        own.start()

        def there(j, x):
            at = pl.ds(pl.multiple_of(peer_of(h, j) * rows, rows), rows)
            return out.at[pl.ds(x * hd2, hd2), at]

        return own, gather(3 + k, halves(r.fin.at[k]), there, True)

    low_side = z < nb // 2
    middle = (z == nb // 2 - 1) | (z == nb // 2)
    handed = (z > 0) & (z < nb - 1)
    inwards = jnp.where(low_side, 1, -1)

    def zcopy(src, dst, ss, rs, dz):
        return copy_to(src, dst, ss, rs, dict(batch=z + dz))

    def to_next(i):
        return zcopy(r.zs.at[i], r.zu.at[i], r.z_s0.at[i], r.z_ur.at[i], inwards)

    def to_middle(i):
        return zcopy(r.zs.at[i], r.zb.at[i], r.z_s0.at[i], r.z_br.at[i], inwards)

    def to_outer(i, src):
        return zcopy(src.at[i], r.zb.at[i], r.z_s1.at[i], r.z_br.at[i], -inwards)

    def inward(i, own):
        @pl.when(handed)
        def _():
            to_next(i).wait_recv()
            r.zs[i] = (own() + r.zu[i].astype(F32)).astype(BF16)

        @pl.when(jnp.logical_not(handed))
        def _():
            r.zs[i] = own().astype(BF16)

        @pl.when(middle)
        def _():
            to_middle(i).start()

        @pl.when(jnp.logical_not(middle))
        def _():
            to_next(i).start()

    def og_local(i, src):
        return pltpu.make_async_copy(src.at[i], r.og.at[i // 4, c, i % 4], r.og_loc.at[i])

    def og_across(i, src):
        return across(src.at[i], r.og.at[i // 4, c, i % 4], r.og_ss.at[i], r.og_rs.at[i])

    def ex_local(q, src):
        return pltpu.make_async_copy(src.at[12 + q, :, pl.ds(512, 128)], r.ex.at[h, c, q], r.ex_loc.at[q])

    def ex_plane(q, src, j, x):
        return copy_to(
            src.at[12 + q, :, pl.ds(512, 128)], r.ex.at[h, c, q],
            r.ex_ss.at[q, 2 * j + x], r.ex_rs.at[q, 2 * j + x], plane_id(j, x),
        )

    def outward(i):
        def place(src):
            @pl.when(handed)
            def _():
                to_outer(i, src).start()

            og_local(i, src).start()
            og_across(i, src).start()
            if isinstance(i, int) and i >= 12:
                ex_local(i - 12, src).start()
                for j, x in plane:
                    ex_plane(i - 12, src, j, x).start()

        to_middle(i).wait_recv()

        @pl.when(middle)
        def _():
            to_middle(i).wait_send()
            r.zs[i] = (r.zs[i].astype(F32) + r.zb[i].astype(F32)).astype(BF16)
            place(r.zs)

        @pl.when(jnp.logical_not(middle))
        def _():
            place(r.zb)

    def ffn_half(t):
        sl = pl.ds(4 * t, 4)
        return across(r.sf.at[sl], r.rf.at[sl], r.f_ss.at[t], r.f_rs.at[t])

    def ffn_piece(i):
        @pl.when(i % 4 == 0)
        def _():
            ffn_half(i // 4).wait_recv()

        inward(i, lambda: r.gown[i] + r.rf[i].astype(F32))

    def within(i, cond, do):
        if isinstance(i, int) and not 0 <= i < 12:
            return

        @pl.when((i >= 0) & (i < 12) & cond)
        def _():
            do(i)

    def slot(k):
        within(k, jnp.logical_not(handed), ffn_piece)
        within(k - 2, handed, ffn_piece)
        within(k - 4, middle, outward)
        within(k - 6, jnp.logical_not(middle), outward)

    forward(0)
    forward(1)
    out_own, out_ag = finish(0, r.d_res[...], r.out)

    def norm_bwd(x, gain, dn):
        inv = lax.rsqrt(jnp.mean(x * x, axis=-1, keepdims=True) + EPS)
        u = gain * dn
        dx = inv * u - x * (inv * inv * inv) * jnp.mean(x * u, axis=-1, keepdims=True)
        return dx, jnp.sum(dn * x * inv, axis=0, keepdims=True)

    mine_half = pl.ds(pl.multiple_of(c * hd2, hd2), hd2)
    other_half = pl.ds(pl.multiple_of((1 - c) * hd2, hd2), hd2)

    def backward(p):
        if p == 1:
            loads.cot.wait()
            for j in range(HEADS):
                pr = pl.ds(pl.multiple_of(peer_of(h, j) * rows, rows), rows)
                pos = c * half + peer_of(h, j) * rows + lax.broadcasted_iota(jnp.int32, (rows, 1), 0)
                ok = (pos < length).astype(F32)
                for b, lo, w in blocks(d):
                    block = r.cot_v[lo : lo + w, pr].astype(F32).T * ok
                    r.df[p, j, :, lo : lo + w] = block.astype(BF16)
                    if j == 0:
                        r.d_res[:, lo : lo + w] = block
        else:
            block = r.d_res[...] * valid
            r.d_res[...] = block
            r.df[p, 0] = block.astype(BF16)
        if p == 0:
            ag = gather(2, halves(r.df.at[p, 0]), lambda j, x: halves(r.df.at[p, j])(x))
        rs = []
        e = 3 - p
        for j in (1, 2, 3, 0) if p == 1 else (0, 1, 2, 3):
            if p == 0 and j == 1:
                ag.hand_on()
            if p == 0 and j:
                ag.wait(j)
            d_act = nn(r.df[p, j], wd_v[...])
            gate, up = r.gate[p, j], r.up[p, j]
            s = 1.0 / (1.0 + jnp.exp(-gate))
            dg = (d_act * up * s * (1.0 + gate * (1.0 - s))).astype(BF16)
            du = (d_act * (gate * s)).astype(BF16)
            r.act[j] = (gate * s * up).astype(BF16)
            r.dg[j] = dg
            r.du[j] = du
            part = nt(dg, wg_v[...]) + nt(du, wu_v[...])
            if j == 0:
                r.part[...] = part
            else:
                r.psend[j - 1] = part.astype(BF16)
                cp = remote(r.psend.at[j - 1], r.precv.at[1 - p, j - 1], r.p_ss.at[e, j], r.p_rs.at[e, j], j)
                cp.start()
                rs.append(cp)
        for t, rhs in ((0, r.dg), (1, r.du), (2, r.act)):
            if t != 1:
                src = r.nf if t == 0 else r.df
                for j in range(HEADS):
                    store_t(lhs.at[:, j * rows : (j + 1) * rows], src[p, j])
            right = rhs[...].reshape(half, ff)
            theirs = nn(lhs[other_half, :], right)
            for q in range(4):
                v = theirs[q * cr : (q + 1) * cr]
                if p == 0:
                    v = v + r.sf[4 * t + q].astype(F32)
                r.sf[4 * t + q] = v.astype(BF16)
            if p == 0:
                ffn_half(t).start()
            ours = nn(lhs[mine_half, :], right)
            for q in range(4):
                v = ours[q * cr : (q + 1) * cr]
                if p == 0:
                    v = v + r.gown[4 * t + q]
                r.gown[4 * t + q] = v
        dn = r.part[...].astype(BF16).astype(F32)
        for j in (1, 2, 3):
            rs[j - 1].wait_recv()
            dn = dn + r.precv[1 - p, j - 1].astype(F32)
        dx, dgain = norm_bwd(r.mid[p], gain_f(), dn)
        d_mid = r.d_res[...] + dx
        r.d_mid[...] = d_mid
        if p == 1:
            r.gain_v[1:2, :] = dgain
        else:
            r.gain_v[1:2, :] += dgain
        da = d_mid.astype(BF16)
        store_t(r.dat.at[:, p * rows : (p + 1) * rows], da)
        r.wide[:, :d] = nt(da, r.wo_v[...])
        for b, lo, w in blocks(d):
            y = r.wide[:, lo : lo + 128]
            g, o = head_row(2 * b)
            r.ou[g, o : o + rows, :] = jnp.where(low, 0.0, swap(y)).astype(BF16)
            if 2 * b + 1 < QH:
                g, o = head_row(2 * b + 1)
                r.ou[g, o : o + rows, :] = jnp.where(low, 0.0, y).astype(BF16)

        def hop(g):
            return across(r.dkv_ctx.at[g], r.dkv_ctx_r.at[p, g], r.dc_ss.at[p, g], r.dc_rs.at[p, g])

        def to_owner(j, g):
            return remote(
                r.dkv_s.at[g, j - 1], r.dkv_r.at[g, j - 1], r.dkv_ss.at[p, g], r.dkv_rs.at[p, g], j
            )

        def all_owners(g):
            return remote(r.dkv_s.at[g], r.dkv_r.at[g], r.dkv_ss.at[p, g], r.dkv_rs.at[p, g], 1)

        def pass_on(g):
            @pl.when(c == 0)
            def _():
                hop(g).wait_recv()
                r.dkv[g] += r.dkv_ctx_r[p, g].astype(F32)

            for j in (1, 2, 3):
                r.dkv_s[g, j - 1] = r.dkv[g, :, j * rows : (j + 1) * rows].astype(BF16)
                to_owner(j, g).start()

        @pl.loop(0, KV)
        def _(g):
            kv = r.kv[p, g]
            acc = None
            for k in range(GQ):
                q = r.ql[p, g, k * rows : (k + 1) * rows, :]
                o = r.ou[g, k * rows : (k + 1) * rows, :]
                s = nt(q, kv)
                s = jnp.where(r.bias[...] < 0.0, NEG, s)
                lse = jnp.sum(jnp.where(lane == g * GQ + k, r.lse[p], 0.0), axis=-1, keepdims=True)
                pr = jnp.exp(s - lse)
                dpr = nt(o, kv)
                delta = jnp.sum(pr * dpr, axis=-1, keepdims=True)
                ds = (pr * (dpr - delta)).astype(BF16)
                r.heads[g * GQ + k] = unrope(nn(ds, kv) * HD ** (-0.5))
                t = nn(o.T, pr.astype(BF16)) + nn(q.T, ds)
                acc = t if acc is None else acc + t
            r.dkv[g] = acc[:, :half]
            r.dkv_ctx[g] = acc[:, half:].astype(BF16)

            @pl.when(c == 1)
            def _():
                hop(g).start()

            @pl.when(g > 0)
            def _():
                pass_on(g - 1)

            if p == 0:
                slot(g)

        pass_on(KV - 1)
        mine = pl.ds(p * rows, rows)
        for b, lo, w in blocks(d):
            y = r.heads[2 * b]
            if 2 * b + 1 < QH:
                y = jnp.where(low, y, swap(r.heads[2 * b + 1]))
            r.dq[:, lo : lo + w] = y[:, :w].astype(BF16)
        for g in range(KV):
            both = jnp.where(low, r.heads[g * GQ], swap(r.heads[g * GQ + 1]))
            r.dpg[g, mine, 0:128] = both.astype(BF16)

        r.wide[:, :d] = nt(r.dq[...], r.wq_v[...])
        if p == 0:
            slot(KV)
        keys, vals = [], []
        for g in range(KV):
            t = r.dkv[g, :, 0:rows]
            all_owners(g).wait_recv()
            for j in range(3):
                t = t + r.dkv_r[g, j].astype(F32)
            t = t.T
            kt, vt = unrope(t), swap(t)
            keys.append(kt)
            vals.append(t)
            r.dpg[g, mine, 128:256] = jnp.where(low, r.heads[g * GQ + 2], swap(kt)).astype(BF16)
            r.dpg[g, mine, 256:384] = jnp.where(low, vt, 0.0).astype(BF16)
        for b, lo, w in blocks(KV * HD):
            kb, vb = keys[2 * b], swap(vals[2 * b])
            if 2 * b + 1 < KV:
                kb = jnp.where(low, kb, swap(keys[2 * b + 1]))
                vb = jnp.where(low, vb, vals[2 * b + 1])
            r.dk[:, lo : lo + w] = kb[:, :w].astype(BF16)
            r.dv[:, lo : lo + w] = vb[:, :w].astype(BF16)
        dna = r.wide[:, :d] + nn(r.dk[...], r.wk_v[...]) + nn(r.dv[...], r.wv_v[...])
        dx, dgain = norm_bwd(r.res[p], gain_a(), dna)
        r.d_res[...] = r.d_mid[...] + dx
        if p == 1:
            r.gain_v[0:1, :] = dgain
        else:
            r.gain_v[0:1, :] += dgain
        if p == 0:
            ag.drain()
        for cp in rs:
            cp.wait_send()

        @pl.loop(0, KV)
        def _(g):
            all_owners(g).wait_send()

            @pl.when(c == 1)
            def _():
                hop(g).wait_send()

    backward(1)
    out_ag.hand_on()
    backward(0)
    gin_own, gin_ag = finish(1, r.d_res[...], r.gin)

    me = 2 * h + c
    r.gain_p[me] = r.gain_v[...]
    gp = [copy_to(r.gain_p.at[me], r.gain_p.at[me], r.gp_ss.at[2 * j + x], r.gp_rs.at[2 * j + x], plane_id(j, x))
          for j, x in plane]
    for cp in gp:
        cp.start()

    def a_half(g):
        src = r.wf.at[pl.ds(pl.multiple_of(g * hd2, hd2), hd2), pl.ds(0, 512)]
        return across(src, r.ra.at[g], r.a_ss.at[g], r.a_rs.at[g])

    @pl.loop(0, KV)
    def _(g):
        def product(rows_of):
            first = nn(r.nat[rows_of, :], r.dpg[g])
            second = nn(r.dat[rows_of, :], r.aog[g])
            return first[:, :256], first[:, 256:] + second[:, :128], second[:, 128:]

        def put(dst, parts):
            dst[:, 0:256] = parts[0].astype(BF16)
            dst[:, 256:384] = parts[1].astype(BF16)
            dst[:, 384:512] = parts[2].astype(BF16)

        put(r.wf.at[pl.ds(pl.multiple_of(g * hd2, hd2), hd2)], product(other_half))
        a_half(g).start()
        put(r.ha.at[g], product(mine_half))
        slot(KV + 1 + g)

        @pl.when(g == 1)
        def _():
            gin_ag.hand_on()

    for cp in gp:
        cp.wait_recv()
    total = r.gain_p[0]
    for k in range(1, 2 * HEADS):
        total = total + r.gain_p[k]
    r.gain_z[z] = total
    gz = [copy_to(r.gain_z.at[z], r.gain_z.at[z], r.gz_ss.at[k], r.gz_rs.at[k], dict(batch=(z + k) % nb))
          for k in range(1, nb)]
    for cp in gz:
        cp.start()

    @pl.loop(0, KV)
    def _(g):
        a_half(g).wait_recv()

    def own_share(to, q):
        at = pl.ds(q * cr, cr)
        g0, g1 = r.gid[to], r.gid[HEADS]
        first = r.ha[g0, at, :].astype(F32) + r.ra[g0, at, :].astype(F32)
        cols = pl.ds(pl.multiple_of(to * 128, 128), 128)
        second = r.ha[g1, at, cols].astype(F32) + r.ra[g1, at, cols].astype(F32)
        return jnp.concatenate([first, second], axis=1)

    for t in range(3):
        ffn_half(t).wait_send()

    def head_share(j):
        sl = pl.ds(4 * (j - 1), 4)
        return remote(r.sf.at[sl], r.rf2.at[sl], r.h_ss.at[j], r.h_rs.at[j], j)

    for j in (1, 2, 3):
        for q in range(4):
            r.sf[4 * (j - 1) + q] = own_share(peer_of(h, j), q).astype(BF16)
        head_share(j).start()

    @pl.loop(2 * KV + 1, 18)
    def _(k):
        slot(k)

    for j in (1, 2, 3):
        head_share(j).wait_recv()

    for q in range(4):
        def own(q=q):
            v = own_share(h, q)
            for j in range(3):
                v = v + r.rf2[4 * j + q].astype(F32)
            return v

        inward(12 + q, own)
    for q in range(4):
        outward(12 + q)

    for cp in gz:
        cp.wait_recv()
    total = r.gain_z[0]
    for k in range(1, nb):
        total = total + r.gain_z[k]
    r.gain_v[...] = total
    gains_out = pltpu.make_async_copy(r.gain_v, r.gains_out, r.loc_sem.at[2])
    gains_out.start()

    gains_out.wait()
    for cp in gp + gz:
        cp.wait_send()
    for j in (1, 2, 3):
        head_share(j).wait_send()

    @pl.loop(0, KV)
    def _(g):
        a_half(g).wait_send()

    @pl.loop(0, 16)
    def _(i):
        og_local(i, r.zs).wait()
        og_across(i, r.zs).wait_send()
        og_across(i, r.zs).wait_recv()

        @pl.when(jnp.logical_not(middle))
        def _():
            to_next(i).wait_send()

        @pl.when(handed)
        def _():
            to_outer(i, r.zs).wait_send()

    for q in range(4):
        ex_local(q, r.zs).wait()
        for j, x in plane:
            ex_plane(q, r.zs, j, x).wait_send()
            ex_plane(q, r.zs, j, x).wait_recv()
    for own, ag in ((out_own, out_ag), (gin_own, gin_ag)):
        own.wait()
        for j in (1, 2, 3):
            ag.wait(j)
        ag.drain()


def body(nb, hidden_in, cotangent, lengths, owners, w_query, w_key, w_value, w_output, gate_weight, up_weight, down_weight,
         gain_attn, gain_ffn):
    half, d = hidden_in.shape[1:]
    ff = gate_weight.shape[1]
    rows = half // HEADS
    cr = d // 8
    scratch = scratch_of(rows, d, ff, nb)
    anyspec = pl.BlockSpec(memory_space=pl.ANY)
    smem = pl.BlockSpec(memory_space=pltpu.SMEM)
    sd = jax.ShapeDtypeStruct
    ins = dict(
        hid=anyspec, cot=anyspec, len=smem, gid=smem, gains=anyspec, tab=anyspec,
        wq=anyspec, wk=anyspec, wv=anyspec, wo=anyspec, wg=anyspec, wu=anyspec, wd=anyspec,
    )
    outs = dict(
        out=sd((d, half), BF16), gin=sd((d, half), BF16),
        og=sd((4, 2, 4, cr, ff), BF16), ex=sd((HEADS, 2, 4, cr, 128), BF16), gains_out=sd((2, d), F32),
    )
    names = tuple(ins) + tuple(outs) + tuple(scratch)
    owned = (owners[None, :] == jnp.arange(HEADS, dtype=jnp.int32)[:, None]).astype(jnp.int32)
    group = jnp.arange(KV, dtype=jnp.int32)
    first = jnp.min(jnp.where(owned == 1, group[None, :], KV), axis=1)
    last = jnp.max(jnp.where(owned == 1, group[None, :], -1), axis=1)
    second = jnp.max(jnp.where(last != first, last, -1))
    gid = jnp.concatenate([first, second[None]]).astype(jnp.int32)
    o, gin, og, ex, gains = pl.pallas_call(
        functools.partial(step_kernel, names, rows, d, ff, nb),
        out_shape=tuple(outs.values()),
        in_specs=list(ins.values()),
        out_specs=(anyspec,) * len(outs),
        scratch_shapes=list(scratch.values()),
        compiler_params=pltpu.CompilerParams(
            collective_id=0, has_side_effects=True, vmem_limit_bytes=67043328
        ),
    )(
        hidden_in[0].T, cotangent[0].T, lengths, gid, jnp.stack([gain_attn, gain_ffn]),
        jnp.asarray(rope_table(2 * half)), w_query, w_key.T, w_value.T, w_output, gate_weight, up_weight, down_weight.T,
    )
    og = og.reshape(4, d, ff)
    has_second = jnp.sum(owned[lax.axis_index("head")]) > 1
    slot0 = og[3, :, :512]
    slot1 = ex.reshape(HEADS, d, 128).transpose(1, 0, 2).reshape(d, 512)
    slot1 = jnp.where(has_second, slot1, jnp.zeros_like(slot1))
    gw = GQ * HD
    pair = lambda lo, hi: jnp.concatenate([slot0[:, lo:hi], slot1[:, lo:hi]], axis=1).astype(F32)
    gq, gk, gv, go = pair(0, gw), pair(gw, gw + HD), pair(gw + HD, gw + 2 * HD), pair(gw + 2 * HD, 512)
    return (
        o.T[None], gin.T.astype(F32)[None], gq, gk, gv, go.T,
        og[0].astype(F32), og[1].astype(F32), og[2].astype(F32).T, gains[0], gains[1],
    )


def solution(mesh):
    rep = P()
    io = P("batch", "ctx", None)
    in_specs = (io, io, P("batch"), rep, rep, rep, rep, rep, P(None, "head"), P(None, "head"), P("head", None), rep, rep)
    out_specs = (io, io, P(None, "head"), P(None, "head"), P(None, "head"), P("head", None), P(None, "head"),
                 P(None, "head"), P("head", None), rep, rep)
    return jax.shard_map(
        functools.partial(body, mesh.shape["batch"]), mesh=mesh, in_specs=in_specs, out_specs=out_specs, check_vma=False
    )
```

```python
import functools
import math
from types import SimpleNamespace

import jax
import jax.numpy as jnp
import numpy as np
from jax import lax
from jax.experimental import pallas as pl
from jax.experimental.pallas import tpu as pltpu
from jax.sharding import PartitionSpec as P

KV = 5
HD = 64
GQ = 3
QH = KV * GQ
HEADS = 4
EPS = 1e-05
NEG = -1e30
MESH = pl.DeviceIdType.MESH
F32 = jnp.float32
BF16 = jnp.bfloat16


def nn(a, b):
    return lax.dot_general(a, b, (((1,), (0,)), ((), ())), preferred_element_type=F32)


def nt(a, b):
    return lax.dot_general(a, b, (((1,), (1,)), ((), ())), preferred_element_type=F32)


def tn(a, b):
    return lax.dot_general(a, b, (((0,), (0,)), ((), ())), preferred_element_type=F32)


def rope_table(slots):
    inverse = np.exp(np.arange(HD // 2, dtype=np.float32) * np.float32(-2.0 * math.log(10000.0) / HD))
    angles = np.arange(slots, dtype=np.float32)[:, None] * inverse[None, :].astype(np.float32)
    cos, sin = np.cos(angles).astype(np.float32), np.sin(angles).astype(np.float32)
    return np.concatenate([cos, sin] * 2, axis=1)


def peer_of(h, j):
    return (h, h + 1 - 2 * (h % 2), (h + 2) % 4, 3 - h)[j]


def scratch_of(rows, d, ff, nb):
    n = HEADS
    half = n * rows
    keys = 2 * half
    dp = -(-d // 128) * 128
    cr = d // 8
    v = pltpu.VMEM
    dma = pltpu.SemaphoreType.DMA
    return dict(
        cot_v=v((d, half), BF16),
        tab_v=v((rows, 256), F32),
        gains_v=v((2, 1, d), F32),
        wq_v=v((d, QH * HD), BF16),
        wk_v=v((KV * HD, d), BF16),
        wv_v=v((KV * HD, d), BF16),
        wo_v=v((QH * HD, d), BF16),
        wf=v((3 * d, ff), BF16),
        res=v((2, rows, d), F32),
        mid=v((2, rows, d), F32),
        nat=v((2, d, rows), BF16),
        dat=v((2, d, rows), BF16),
        ql=v((2, KV, GQ * rows, 128), BF16),
        kv=v((2, KV, keys, 128), BF16),
        lse=v((2, rows, 128), F32),
        at=v((rows, d), BF16),
        nf=v((2, n, rows, d), BF16),
        gate=v((2, n, rows, ff), F32),
        up=v((2, n, rows, ff), F32),
        act=v((n, rows, ff), BF16),
        bias=v((rows, keys), F32),
        wide=v((rows, dp), F32),
        heads=v((QH, rows, 128), F32),
        part=v((2, rows, d), BF16),
        psend=v((2, 3, rows, d), BF16),
        precv=v((2, 3, rows, d), BF16),
        d_res=v((rows, d), F32),
        d_mid=v((rows, d), F32),
        df=v((2, n, rows, d), BF16),
        dg=v((n, rows, ff), BF16),
        du=v((n, rows, ff), BF16),
        ou=v((KV, GQ * rows, 128), BF16),
        dk=v((rows, KV * HD), BF16),
        dv=v((rows, KV * HD), BF16),
        dpg=v((KV, 2 * rows, 384), BF16),
        aog=v((KV, 2 * rows, 256), BF16),
        dkv=v((KV, 128, half), F32),
        dkv_ctx=v((KV, 128, half), BF16),
        dkv_ctx_r=v((2, KV, 128, half), BF16),
        dkv_s=v((KV, 3, 128, rows), BF16),
        dkv_r=v((KV, 3, 128, rows), BF16),
        fin=v((2, d, rows), BF16),
        gown=v((12, cr, ff), F32),
        sf=v((12, cr, ff), BF16),
        rf=v((12, cr, ff), BF16),
        rf2=v((12, cr, ff), BF16),
        zs=v((16, cr, ff), BF16),
        zu=v((16, cr, ff), BF16),
        zb=v((16, cr, ff), BF16),
        ha=v((KV, d // 2, 512), BF16),
        ra=v((KV, d // 2, 512), BF16),
        gain_v=v((2, 1, d), F32),
        gain_p=v((2 * n, 2, 1, d), F32),
        gain_z=v((nb, 2, 1, d), F32),
        in_sem=dma((12,)),
        loc_sem=dma((8,)),
        kv_ss=dma((2, KV)),
        kv_rs=dma((2, KV)),
        kvc_ss=dma((2, KV)),
        kvc_rs=dma((2, KV)),
        ag_ss=dma((5, 6)),
        ag_rs=dma((5, 6)),
        p_ss=dma((4, 4)),
        p_rs=dma((4, 4)),
        dc_ss=dma((2, KV)),
        dc_rs=dma((2, KV)),
        dkv_ss=dma((2, KV)),
        dkv_rs=dma((2, KV)),
        f_ss=dma((3,)),
        f_rs=dma((3,)),
        z_s0=dma((16,)),
        z_s1=dma((16,)),
        z_ur=dma((16,)),
        z_br=dma((16,)),
        og_loc=dma((16,)),
        og_ss=dma((16,)),
        og_rs=dma((16,)),
        a_ss=dma((KV,)),
        a_rs=dma((KV,)),
        h_ss=dma((4, 4)),
        h_rs=dma((4, 4)),
        ex_loc=dma((4,)),
        ex_ss=dma((4, 8)),
        ex_rs=dma((4, 8)),
        gp_ss=dma((8,)),
        gp_rs=dma((8,)),
        gz_ss=dma((nb,)),
        gz_rs=dma((nb,)),
    )


def step_kernel(names, rows, d, ff, nb, *refs):
    r = SimpleNamespace(**dict(zip(names, refs)))
    wg_v, wu_v, wd_v = (r.wf.at[pl.ds(t * d, d)] for t in range(3))
    lhs, hid_v = r.cot_v, r.fin.at[1]
    h = lax.axis_index("head")
    c = lax.axis_index("ctx")
    z = lax.axis_index("batch")
    half = HEADS * rows
    hd2 = d // 2
    cr = d // 8
    lane = lax.broadcasted_iota(jnp.int32, (rows, 128), 1)
    low = lane < HD
    quarter = (lane % HD) < HD // 2

    def copy_to(src, dst, ss, rs, where):
        return pltpu.make_async_remote_copy(
            src_ref=src, dst_ref=dst, send_sem=ss, recv_sem=rs, device_id=where, device_id_type=MESH
        )

    def remote(src, dst, ss, rs, j):
        return copy_to(src, dst, ss, rs, dict(head=peer_of(h, j)))

    def across(src, dst, ss, rs):
        return copy_to(src, dst, ss, rs, dict(ctx=1 - c))

    def load(k, src, dst):
        return pltpu.make_async_copy(src, dst, r.in_sem.at[k])

    my_rows = pl.ds(pl.multiple_of(h * rows, rows), rows)
    my_pos = pl.ds(pl.multiple_of(c * half + h * rows, rows), rows)
    loads = SimpleNamespace(
        hid=load(0, r.hid.at[:, my_rows], hid_v),
        ga=load(1, r.ga, r.gains_v.at[0]),
        gf=load(11, r.gf, r.gains_v.at[1]),
        wk=load(3, r.wk, r.wk_v),
        wv=load(4, r.wv, r.wv_v),
        tab=load(5, r.tab.at[my_pos], r.tab_v.at[:, pl.ds(0, 128)]),
        wq=load(2, r.wq, r.wq_v),
        wo=load(6, r.wo, r.wo_v),
        wg=load(7, r.wg, wg_v),
        wu=load(8, r.wu, wu_v),
        wd=load(9, r.wd, wd_v),
        cot=load(10, r.cot, r.cot_v),
    )
    for cp in vars(loads).values():
        cp.start()

    plane = [(j, x) for j in range(HEADS) for x in range(2) if (j, x) != (0, 0)]

    def plane_id(j, x):
        return dict(head=peer_of(h, j), ctx=1 - c if x else c)

    barrier = pltpu.get_barrier_semaphore()
    for j, x in plane:
        pl.semaphore_signal(barrier, inc=1, device_id=plane_id(j, x), device_id_type=MESH)
    for k in range(1, nb):
        pl.semaphore_signal(barrier, inc=1, device_id=dict(batch=(z + k) % nb), device_id_type=MESH)
    pl.semaphore_wait(barrier, len(plane) + nb - 1)

    length = r.len[0]
    row_pos = c * half + h * rows + lax.broadcasted_iota(jnp.int32, (rows, 1), 0)
    valid = (row_pos < length).astype(F32)

    zero_w = jnp.zeros((rows, 128), F32)
    r.wide[...] = jnp.zeros(r.wide.shape, F32)
    vlo = r.wide.shape[1] // 2
    r.lse[0] = zero_w
    r.lse[1] = zero_w

    @pl.when(c == 0)
    def _():
        for p in range(2):
            r.kv[p, :, half:, :] = jnp.zeros((KV, half, 128), BF16)

    def fill_mask():
        for blk in range(2 * HEADS):
            own = blk < HEADS
            base = (c if own else 1 - c) * half + peer_of(h, blk % HEADS) * rows
            kp = base + lax.broadcasted_iota(jnp.int32, (rows, rows), 1)
            qp = c * half + h * rows + lax.broadcasted_iota(jnp.int32, (rows, rows), 0)
            ok = (kp <= qp) & (kp < length)
            r.bias[:, blk * rows : (blk + 1) * rows] = jnp.where(ok, 0.0, NEG)

    def fill_cotangent():
        for j in range(HEADS):
            pr = pl.ds(pl.multiple_of(peer_of(h, j) * rows, rows), rows)
            pos = c * half + peer_of(h, j) * rows + lax.broadcasted_iota(jnp.int32, (rows, 1), 0)
            ok = (pos < length).astype(F32)
            for b, lo, w in blocks(d):
                block = r.cot_v[lo : lo + w, pr].astype(F32).T * ok
                r.df[1, j, :, lo : lo + w] = block.astype(BF16)
                if j == 0:
                    r.d_res[:, lo : lo + w] = block

    def clear_sums():
        @pl.loop(0, 12)
        def _(i):
            r.gown[i] = jnp.zeros((cr, ff), F32)
            r.sf[i] = jnp.zeros((cr, ff), BF16)

        r.gain_v[...] = jnp.zeros((2, 1, d), F32)

    def share(k, e, j):
        return remote(r.psend.at[k, j - 1], r.precv.at[k, j - 1], r.p_ss.at[e, j], r.p_rs.at[e, j], j)

    def summed(k, e):
        total = r.part[k].astype(F32)
        for j in (1, 2, 3):
            share(k, e, j).wait_recv()
            total = total + r.precv[k, j - 1].astype(F32)
        return total

    def sent(k, e):
        for j in (1, 2, 3):
            share(k, e, j).wait_send()

    def rms(x, gain):
        inv = lax.rsqrt(jnp.mean(x * x, axis=-1, keepdims=True) + EPS)
        return x * inv * gain

    def turned(x):
        return jnp.where(quarter, -pltpu.roll(x, 128 - HD // 2, 1), pltpu.roll(x, HD // 2, 1))

    def rope(x):
        return x * r.tab_v[:, 0:128] + turned(x) * r.tab_v[:, 128:256]

    def unrope(x):
        return x * r.tab_v[:, 0:128] - turned(x) * r.tab_v[:, 128:256]

    def swap(x):
        return pltpu.roll(x, HD, 1)

    def blocks(width):
        return [(b, b * 128, min(128, width - b * 128)) for b in range(-(-width // 128))]

    def head_row(i):
        return i // GQ, (i % GQ) * rows

    def store_t(dst, src):
        for b, lo, w in blocks(d):
            dst[lo : lo + w, :] = src[:, lo : lo + w].T

    gain_a = lambda: r.gains_v[0]
    gain_f = lambda: r.gains_v[1]

    loads.tab.wait()
    both = r.tab_v[:, 0:128]
    r.tab_v[:, 128:256] = jnp.where(quarter, pltpu.roll(both, 128 - HD // 2, 1), both)
    r.tab_v[:, 0:128] = jnp.where(quarter, both, pltpu.roll(both, HD // 2, 1))
    loads.ga.wait()
    loads.gf.wait()
    loads.hid.wait()
    for b, lo, w in blocks(d):
        r.res[0, :, lo : lo + w] = hid_v[lo : lo + w, :].astype(F32).T

    def gather(e, src, dst, by_owner=False):
        def hop(k, ref, to, j):
            return remote(ref, to, r.ag_ss.at[e, k], r.ag_rs.at[e, k], j)

        at = (lambda j, near, x: dst(near, x)) if by_owner else (lambda j, near, x: dst(j, x))
        first = [hop(0, src(0), at(1, 0, 0), 1), hop(3, src(1), at(2, 0, 1), 2), hop(1, src(1), at(1, 0, 1), 1),
                 hop(2, src(0), at(2, 0, 0), 2)]
        relay = [hop(4, dst(1, 0), at(3, 1, 0), 2), hop(5, dst(2, 1), at(3, 2, 1), 1)]
        def start():
            for cp in first:
                cp.start()

        def hand_on():
            first[0].wait_recv()
            relay[0].start()
            first[1].wait_recv()
            relay[1].start()

        def wait(j):
            for cp in ((first[2],), (first[3],), relay)[j - 1]:
                cp.wait_recv()

        def drain():
            for cp in first + relay:
                cp.wait_send()

        return SimpleNamespace(start=start, hand_on=hand_on, wait=wait, drain=drain)

    def halves(ref):
        n = ref.shape[0] // 2
        return lambda x: ref.at[pl.ds(x * n, n)]

    @pl.loop(0, 2)
    def _(p):
        x = r.res[p]
        na = rms(x, gain_a()).astype(BF16)
        store_t(r.nat.at[p], na)

        @pl.when(p == 0)
        def _():
            loads.wk.wait()
            loads.wv.wait()

        r.wide[:, : KV * HD] = nt(na, r.wk_v[...])
        r.wide[:, vlo : vlo + KV * HD] = nt(na, r.wv_v[...])
        for b in range(-(-KV // 2)):
            kb = rope(r.wide[:, b * 128 : (b + 1) * 128])
            vb = r.wide[:, vlo + b * 128 : vlo + (b + 1) * 128]
            r.kv[p, 2 * b, 0:rows, :] = jnp.where(low, kb, swap(vb)).astype(BF16)
            if 2 * b + 1 < KV:
                r.kv[p, 2 * b + 1, 0:rows, :] = jnp.where(low, swap(kb), vb).astype(BF16)

        def to_peer(j, g):
            return remote(
                r.kv.at[p, g, pl.ds(0, rows)], r.kv.at[p, g, pl.ds(j * rows, rows)],
                r.kv_ss.at[p, g], r.kv_rs.at[p, g], j,
            )

        def to_partner(j, g):
            return across(
                r.kv.at[p, g, pl.ds(j * rows, rows)], r.kv.at[p, g, pl.ds(half + j * rows, rows)],
                r.kvc_ss.at[p, g], r.kvc_rs.at[p, g],
            )

        def all_peers(g):
            span = r.kv.at[p, g, pl.ds(rows, 3 * rows)]
            return remote(span, span, r.kv_ss.at[p, g], r.kv_rs.at[p, g], 1)

        def all_partner(g):
            span = r.kv.at[p, g, pl.ds(half, half)]
            return across(span, span, r.kvc_ss.at[p, g], r.kvc_rs.at[p, g])

        for g in range(KV):
            for j in (1, 2, 3):
                to_peer(j, g).start()

            @pl.when(c == 0)
            def _():
                to_partner(0, g).start()

        def arrive(g):
            all_peers(g).wait_recv()

            @pl.when(c == 0)
            def _():
                for j in (1, 2, 3):
                    to_partner(j, g).start()

        @pl.when(p == 0)
        def _():
            fill_mask()
            loads.wq.wait()

        r.wide[:, :d] = nn(na, r.wq_v[...])
        for b, lo, w in blocks(d):
            y = rope(r.wide[:, lo : lo + 128]).astype(BF16).astype(F32) * HD ** (-0.5)
            g, o = head_row(2 * b)
            r.ql[p, g, o : o + rows, :] = jnp.where(low, y, 0.0).astype(BF16)
            if 2 * b + 1 < QH:
                g, o = head_row(2 * b + 1)
                r.ql[p, g, o : o + rows, :] = jnp.where(low, swap(y), 0.0).astype(BF16)

        arrive(0)

        @pl.loop(0, KV)
        def _(g):
            @pl.when(g < KV - 1)
            def _():
                arrive(g + 1)

            @pl.when(c == 1)
            def _():
                all_partner(g).wait_recv()

            kv = r.kv[p, g]
            for k in range(GQ):
                s = nt(r.ql[p, g, k * rows : (k + 1) * rows, :], kv)
                s = jnp.where(r.bias[...] < 0.0, NEG, s)
                m = jnp.max(s, axis=-1, keepdims=True)
                e = jnp.exp(s - m)
                t = jnp.sum(e, axis=-1, keepdims=True)
                r.lse[p] += jnp.where(lane == g * GQ + k, m + jnp.log(t), 0.0)
                r.heads[g * GQ + k] = nn((e / t).astype(BF16), kv)

        mine = pl.ds(pl.multiple_of(p * rows, rows), rows)
        for g in range(KV):
            o0, o1, o2 = (r.heads[g * GQ + k] for k in range(GQ))
            r.aog[g, mine, 0:128] = jnp.where(low, 0.0, o0).astype(BF16)
            r.aog[g, mine, 128:256] = jnp.where(low, swap(o1), o2).astype(BF16)
        for b, lo, w in blocks(d):
            first = swap(r.heads[2 * b])
            both = jnp.where(low, first, r.heads[2 * b + 1]) if 2 * b + 1 < QH else first
            r.at[:, lo : lo + w] = both[:, :w].astype(BF16)

        @pl.when(p == 0)
        def _():
            loads.wo.wait()

        mid = r.res[p] + nn(r.at[...], r.wo_v[...])
        r.mid[p] = mid
        r.nf[p, 0] = rms(mid, gain_f()).astype(BF16)
        ag = gather(p, halves(r.nf.at[p, 0]), lambda j, x: halves(r.nf.at[p, j])(x))
        ag.start()

        @pl.when(p == 0)
        def _():
            loads.wg.wait()
            loads.wu.wait()
            loads.wd.wait()

        for j in range(HEADS):
            if j == 1:
                ag.hand_on()
            if j:
                ag.wait(j)
            nf = r.nf[p, j]
            gate = nn(nf, wg_v[...])
            up = nn(nf, wu_v[...])
            r.gate[p, j] = gate
            r.up[p, j] = up
            act = (gate / (1.0 + jnp.exp(-gate)) * up).astype(BF16)
            part = nt(act, wd_v[...])
            if j == 0:
                r.part[p] = part.astype(BF16)
            else:
                r.psend[p, j - 1] = part.astype(BF16)
                share(p, p, j).start()
        ag.drain()

        @pl.when(p == 0)
        def _():
            loads.cot.wait()
            fill_cotangent()
            clear_sums()
            r.res[1] = valid * (r.mid[0] + summed(0, 0))
            sent(0, 0)

        @pl.loop(0, KV)
        def _(g):
            all_peers(g).wait_send()

            @pl.when(c == 0)
            def _():
                all_partner(g).wait_send()

    def final(k, out):
        def there(j, x):
            at = pl.ds(pl.multiple_of(peer_of(h, j) * rows, rows), rows)
            return out.at[pl.ds(x * hd2, hd2), at]

        own = pltpu.make_async_copy(r.fin.at[k], out.at[:, my_rows], r.loc_sem.at[k])
        ag = gather(3 + k, halves(r.fin.at[k]), there, True)

        def send(value):
            store_t(r.fin.at[k], value.astype(BF16))
            own.start()
            ag.start()

        return SimpleNamespace(send=send, own=own, hand_on=ag.hand_on, wait=ag.wait, drain=ag.drain)

    low_side = z < nb // 2
    middle = (z == nb // 2 - 1) | (z == nb // 2)
    handed = (z > 0) & (z < nb - 1)
    inwards = jnp.where(low_side, 1, -1)

    def zcopy(src, dst, ss, rs, dz):
        return copy_to(src, dst, ss, rs, dict(batch=z + dz))

    def to_next(i):
        return zcopy(r.zs.at[i], r.zu.at[i], r.z_s0.at[i], r.z_ur.at[i], inwards)

    def to_middle(i):
        return zcopy(r.zs.at[i], r.zb.at[i], r.z_s0.at[i], r.z_br.at[i], inwards)

    def to_outer(i, src):
        return zcopy(src.at[i], r.zb.at[i], r.z_s1.at[i], r.z_br.at[i], -inwards)

    def inward(i, own):
        @pl.when(handed)
        def _():
            to_next(i).wait_recv()
            r.zs[i] = (own() + r.zu[i].astype(F32)).astype(BF16)

        @pl.when(jnp.logical_not(handed))
        def _():
            r.zs[i] = own().astype(BF16)

        @pl.when(middle)
        def _():
            to_middle(i).start()

        @pl.when(jnp.logical_not(middle))
        def _():
            to_next(i).start()

    def og_local(i, src):
        return pltpu.make_async_copy(src.at[i], r.og.at[i // 4, c, i % 4], r.og_loc.at[i])

    def og_across(i, src):
        return across(src.at[i], r.og.at[i // 4, c, i % 4], r.og_ss.at[i], r.og_rs.at[i])

    def ex_local(q, src):
        return pltpu.make_async_copy(src.at[12 + q, :, pl.ds(512, 128)], r.ex.at[h, c, q], r.ex_loc.at[q])

    def ex_plane(q, src, j, x):
        return copy_to(
            src.at[12 + q, :, pl.ds(512, 128)], r.ex.at[h, c, q],
            r.ex_ss.at[q, 2 * j + x], r.ex_rs.at[q, 2 * j + x], plane_id(j, x),
        )

    def outward(i):
        def place(src):
            @pl.when(handed)
            def _():
                to_outer(i, src).start()

            og_local(i, src).start()
            og_across(i, src).start()
            if isinstance(i, int) and i >= 12:
                ex_local(i - 12, src).start()
                for j, x in plane:
                    ex_plane(i - 12, src, j, x).start()

        to_middle(i).wait_recv()

        @pl.when(middle)
        def _():
            to_middle(i).wait_send()
            r.zs[i] = (r.zs[i].astype(F32) + r.zb[i].astype(F32)).astype(BF16)
            place(r.zs)

        @pl.when(jnp.logical_not(middle))
        def _():
            place(r.zb)

    def ffn_half(t):
        sl = pl.ds(4 * t, 4)
        return across(r.sf.at[sl], r.rf.at[sl], r.f_ss.at[t], r.f_rs.at[t])

    def ffn_piece(i):
        @pl.when(i % 4 == 0)
        def _():
            ffn_half(i // 4).wait_recv()

        inward(i, lambda: r.gown[i] + r.rf[i].astype(F32))

    def within(i, cond, do):
        if isinstance(i, int) and not 0 <= i < 16:
            return

        @pl.when((i >= 0) & (i < 16) & cond)
        def _():
            do(i)

    def slot(k):
        piece = lambda i: (attention_piece if isinstance(i, int) and i >= 12 else ffn_piece)(i)
        within(k, jnp.logical_not(handed), piece)
        within(k - 2, handed, piece)
        within(k - 4, middle, outward)
        within(k - 6, jnp.logical_not(middle), outward)

    def norm_bwd(x, gain, dn):
        inv = lax.rsqrt(jnp.mean(x * x, axis=-1, keepdims=True) + EPS)
        u = gain * dn
        dx = inv * u - x * (inv * inv * inv) * jnp.mean(x * u, axis=-1, keepdims=True)
        return dx, jnp.sum(dn * x * inv, axis=0, keepdims=True)

    mine_half = pl.ds(pl.multiple_of(c * hd2, hd2), hd2)
    other_half = pl.ds(pl.multiple_of((1 - c) * hd2, hd2), hd2)

    def a_half(g):
        src = r.wf.at[pl.ds(pl.multiple_of(g * hd2, hd2), hd2), pl.ds(0, 512)]
        return across(src, r.ra.at[g], r.a_ss.at[g], r.a_rs.at[g])

    def first_group(to):
        g = jnp.int32(KV - 1)
        for k in reversed(range(KV - 1)):
            g = jnp.where(r.own[k] == to, k, g)
        return g

    g1 = jnp.int32(0)
    for k in range(1, KV):
        for i in range(k):
            g1 = jnp.where(r.own[k] == r.own[i], k, g1)

    def own_share(to, q):
        at = pl.ds(q * cr, cr)
        g0 = first_group(to)
        first = r.ha[g0, at, :].astype(F32) + r.ra[g0, at, :].astype(F32)
        cols = pl.ds(pl.multiple_of(to * 128, 128), 128)
        second = r.ha[g1, at, cols].astype(F32) + r.ra[g1, at, cols].astype(F32)
        return jnp.concatenate([first, second], axis=1)

    def head_share(j, q):
        i = 4 * (j - 1) + q
        return remote(r.sf.at[i], r.rf2.at[i], r.h_ss.at[j, q], r.h_rs.at[j, q], j)

    def attention_sums():
        @pl.loop(0, KV)
        def _(g):
            def product(rows_of):
                first = nn(jnp.concatenate([r.nat[0, rows_of, :], r.nat[1, rows_of, :]], axis=1), r.dpg[g])
                second = nn(jnp.concatenate([r.dat[0, rows_of, :], r.dat[1, rows_of, :]], axis=1), r.aog[g])
                return first[:, :256], first[:, 256:] + second[:, :128], second[:, 128:]

            def put(dst, parts):
                dst[:, 0:256] = parts[0].astype(BF16)
                dst[:, 256:384] = parts[1].astype(BF16)
                dst[:, 384:512] = parts[2].astype(BF16)

            put(r.wf.at[pl.ds(pl.multiple_of(g * hd2, hd2), hd2)], product(other_half))
            a_half(g).start()
            put(r.ha.at[g], product(mine_half))
            slot(KV + 1 + g)

        @pl.loop(0, KV)
        def _(g):
            a_half(g).wait_recv()

        for t in range(3):
            ffn_half(t).wait_send()
        for q in range(4):
            for j in (3, 1, 2):
                r.sf[4 * (j - 1) + q] = own_share(peer_of(h, j), q).astype(BF16)
                head_share(j, q).start()

    def attention_piece(i):
        q = i - 12

        def own():
            v = own_share(h, q)
            for j in (1, 2, 3):
                head_share(j, q).wait_recv()
                v = v + r.rf2[4 * (j - 1) + q].astype(F32)
            return v

        inward(i, own)

    @pl.loop(0, 2)
    def _(turn):
        p = 1 - turn
        ag = gather(2, halves(r.df.at[0, 0]), lambda j, x: halves(r.df.at[0, j])(x))

        @pl.when(p == 0)
        def _():
            block = r.d_res[...] * valid
            r.d_res[...] = block
            r.df[0, 0] = block.astype(BF16)
            ag.start()

        for j in range(HEADS):
            if j:
                @pl.when(p == 0)
                def _():
                    if j == 1:
                        ag.hand_on()
                    ag.wait(j)

            d_act = nn(r.df[p, j], wd_v[...])
            gate, up = r.gate[p, j], r.up[p, j]
            s = 1.0 / (1.0 + jnp.exp(-gate))
            dg = (d_act * up * s * (1.0 + gate * (1.0 - s))).astype(BF16)
            du = (d_act * (gate * s)).astype(BF16)
            r.act[j] = (gate * s * up).astype(BF16)
            r.dg[j] = dg
            r.du[j] = du
            part = nt(dg, wg_v[...]) + nt(du, wu_v[...])
            if j == 0:
                r.part[1 - p] = part.astype(BF16)
            else:
                r.psend[1 - p, j - 1] = part.astype(BF16)
                share(1 - p, 3 - p, j).start()
        for t, rhs in ((0, r.dg), (1, r.du), (2, r.act)):
            if t != 1:
                src = r.nf if t == 0 else r.df
                for j in range(HEADS):
                    store_t(lhs.at[:, j * rows : (j + 1) * rows], src[p, j])
            right = rhs[...].reshape(half, ff)
            theirs = nn(lhs[other_half, :], right)
            for q in range(4):
                v = theirs[q * cr : (q + 1) * cr] + r.sf[4 * t + q].astype(F32)
                r.sf[4 * t + q] = v.astype(BF16)

            @pl.when(p == 0)
            def _():
                ffn_half(t).start()

            ours = nn(lhs[mine_half, :], right)
            for q in range(4):
                r.gown[4 * t + q] += ours[q * cr : (q + 1) * cr]

        @pl.when(p == 1)
        def _():
            final(0, r.out).send(valid * (r.mid[1] + summed(1, 1)))
            sent(1, 1)

        dn = summed(1 - p, 3 - p)
        dx, dgain = norm_bwd(r.mid[p], gain_f(), dn)
        d_mid = r.d_res[...] + dx
        r.d_mid[...] = d_mid
        r.gain_v[1] += dgain
        da = d_mid.astype(BF16)
        store_t(r.dat.at[p], da)
        r.wide[:, :d] = nt(da, r.wo_v[...])
        for b, lo, w in blocks(d):
            y = r.wide[:, lo : lo + 128]
            g, o = head_row(2 * b)
            r.ou[g, o : o + rows, :] = jnp.where(low, 0.0, swap(y)).astype(BF16)
            if 2 * b + 1 < QH:
                g, o = head_row(2 * b + 1)
                r.ou[g, o : o + rows, :] = jnp.where(low, 0.0, y).astype(BF16)

        def hop(g):
            return across(r.dkv_ctx.at[g], r.dkv_ctx_r.at[p, g], r.dc_ss.at[p, g], r.dc_rs.at[p, g])

        def to_owner(j, g):
            return remote(
                r.dkv_s.at[g, j - 1], r.dkv_r.at[g, j - 1], r.dkv_ss.at[p, g], r.dkv_rs.at[p, g], j
            )

        def all_owners(g):
            return remote(r.dkv_s.at[g], r.dkv_r.at[g], r.dkv_ss.at[p, g], r.dkv_rs.at[p, g], 1)

        def pass_on(g):
            @pl.when(c == 0)
            def _():
                hop(g).wait_recv()
                r.dkv[g] += r.dkv_ctx_r[p, g].astype(F32)

            for j in (1, 2, 3):
                r.dkv_s[g, j - 1] = r.dkv[g, :, j * rows : (j + 1) * rows].astype(BF16)
                to_owner(j, g).start()

        @pl.loop(0, KV)
        def _(g):
            kv = r.kv[p, g]
            acc = None
            for k in range(GQ):
                q = r.ql[p, g, k * rows : (k + 1) * rows, :]
                o = r.ou[g, k * rows : (k + 1) * rows, :]
                s = nt(q, kv)
                s = jnp.where(r.bias[...] < 0.0, NEG, s)
                lse = jnp.sum(jnp.where(lane == g * GQ + k, r.lse[p], 0.0), axis=-1, keepdims=True)
                pr = jnp.exp(s - lse)
                dpr = nt(o, kv)
                delta = jnp.sum(pr * dpr, axis=-1, keepdims=True)
                ds = (pr * (dpr - delta)).astype(BF16)
                r.heads[g * GQ + k] = unrope(nn(ds, kv) * HD ** (-0.5))
                t = nn(o.T, pr.astype(BF16)) + nn(q.T, ds)
                acc = t if acc is None else acc + t
            r.dkv[g] = acc[:, :half]
            r.dkv_ctx[g] = acc[:, half:].astype(BF16)

            @pl.when(c == 1)
            def _():
                hop(g).start()

            @pl.when(g > 0)
            def _():
                pass_on(g - 1)

            @pl.when(p == 0)
            def _():
                slot(g)

        pass_on(KV - 1)
        mine = pl.ds(pl.multiple_of(p * rows, rows), rows)
        for b, lo, w in blocks(d):
            y = r.heads[2 * b]
            if 2 * b + 1 < QH:
                y = jnp.where(low, y, swap(r.heads[2 * b + 1]))
            r.at[:, lo : lo + w] = y[:, :w].astype(BF16)
        for g in range(KV):
            both = jnp.where(low, r.heads[g * GQ], swap(r.heads[g * GQ + 1]))
            r.dpg[g, mine, 0:128] = both.astype(BF16)

        r.wide[:, :d] = nt(r.at[...], r.wq_v[...])

        @pl.when(p == 0)
        def _():
            slot(KV)

        keys, vals = [], []
        for g in range(KV):
            t = r.dkv[g, :, 0:rows]
            all_owners(g).wait_recv()
            for j in range(3):
                t = t + r.dkv_r[g, j].astype(F32)
            t = t.T
            kt, vt = unrope(t), swap(t)
            keys.append(kt)
            vals.append(t)
            r.dpg[g, mine, 128:256] = jnp.where(low, r.heads[g * GQ + 2], swap(kt)).astype(BF16)
            r.dpg[g, mine, 256:384] = jnp.where(low, vt, 0.0).astype(BF16)
        for b, lo, w in blocks(KV * HD):
            kb, vb = keys[2 * b], swap(vals[2 * b])
            if 2 * b + 1 < KV:
                kb = jnp.where(low, kb, swap(keys[2 * b + 1]))
                vb = jnp.where(low, vb, vals[2 * b + 1])
            r.dk[:, lo : lo + w] = kb[:, :w].astype(BF16)
            r.dv[:, lo : lo + w] = vb[:, :w].astype(BF16)
        @pl.when(p == 0)
        def _():
            attention_sums()

        dna = r.wide[:, :d] + nn(r.dk[...], r.wk_v[...]) + nn(r.dv[...], r.wv_v[...])
        dx, dgain = norm_bwd(r.res[p], gain_a(), dna)
        r.d_res[...] = r.d_mid[...] + dx
        r.gain_v[0] += dgain
        sent(1 - p, 3 - p)

        @pl.when(p == 0)
        def _():
            ag.drain()

        @pl.when(p == 1)
        def _():
            final(0, r.out).hand_on()


        @pl.loop(0, KV)
        def _(g):
            all_owners(g).wait_send()

            @pl.when(c == 1)
            def _():
                hop(g).wait_send()

    final(1, r.gin).send(r.d_res[...])

    me = 2 * h + c
    r.gain_p[me] = r.gain_v[...]
    gp = [copy_to(r.gain_p.at[me], r.gain_p.at[me], r.gp_ss.at[2 * j + x], r.gp_rs.at[2 * j + x], plane_id(j, x))
          for j, x in plane]
    for cp in gp:
        cp.start()

    for cp in gp:
        cp.wait_recv()
    total = r.gain_p[0]
    for k in range(1, 2 * HEADS):
        total = total + r.gain_p[k]
    r.gain_z[z] = total
    gz = [copy_to(r.gain_z.at[z], r.gain_z.at[z], r.gz_ss.at[k], r.gz_rs.at[k], dict(batch=(z + k) % nb))
          for k in range(1, nb)]
    for cp in gz:
        cp.start()

    for k in range(2 * KV + 1, 22):
        slot(k)
        if k == 2 * KV + 1:
            final(1, r.gin).hand_on()

    for cp in gz:
        cp.wait_recv()
    total = r.gain_z[0]
    for k in range(1, nb):
        total = total + r.gain_z[k]
    r.gain_v[...] = total
    gains_out = pltpu.make_async_copy(r.gain_v, r.gains_out, r.loc_sem.at[2])
    gains_out.start()

    gains_out.wait()
    for cp in gp + gz:
        cp.wait_send()
    for j in (1, 2, 3):
        for q in range(4):
            head_share(j, q).wait_send()

    @pl.loop(0, KV)
    def _(g):
        a_half(g).wait_send()

    @pl.loop(0, 16)
    def _(i):
        og_local(i, r.zs).wait()
        og_across(i, r.zs).wait_send()
        og_across(i, r.zs).wait_recv()

        @pl.when(jnp.logical_not(middle))
        def _():
            to_next(i).wait_send()

        @pl.when(handed)
        def _():
            to_outer(i, r.zs).wait_send()

    for q in range(4):
        ex_local(q, r.zs).wait()
        for j, x in plane:
            ex_plane(q, r.zs, j, x).wait_send()
            ex_plane(q, r.zs, j, x).wait_recv()
    for k, out in ((0, r.out), (1, r.gin)):
        end = final(k, out)
        end.own.wait()
        for j in (1, 2, 3):
            end.wait(j)
        end.drain()


def put_kernel(own, o, gin, og, ex, ga, gf, o_out, gin_out, gq, gk, gv, go, gg, gu, gd, ga_out, gf_out):
    h = lax.axis_index("head")
    held = jnp.int32(0)
    for k in range(KV):
        held = held + jnp.where(own[k] == h, 1, 0)
    gw = GQ * HD
    o_out[...] = o[...]
    gin_out[...] = gin[...].astype(F32)
    gg[...] = og[0].astype(F32)
    gu[...] = og[1].astype(F32)
    gd[...] = og[2].astype(F32)
    ga_out[...] = ga[...]
    gf_out[...] = gf[...]
    first = og[3, :, 0:512].astype(F32)
    second = jnp.concatenate([ex[k].astype(F32) for k in range(HEADS)], axis=1)
    second = jnp.where(held > 1, second, 0.0)
    for out, lo, width in ((gq, 0, gw), (gk, gw, HD), (gv, gw + HD, HD), (go, gw + 2 * HD, gw)):
        out[...] = jnp.concatenate([first[:, lo : lo + width], second[:, lo : lo + width]], axis=1)


def body(nb, hidden_in, cotangent, lengths, owners, w_query, w_key, w_value, w_output, gate_weight, up_weight, down_weight,
         gain_attn, gain_ffn):
    half, d = hidden_in.shape[1:]
    ff = gate_weight.shape[1]
    rows = half // HEADS
    cr = d // 8
    scratch = scratch_of(rows, d, ff, nb)
    anyspec = pl.BlockSpec(memory_space=pl.ANY)
    smem = pl.BlockSpec(memory_space=pltpu.SMEM)
    sd = jax.ShapeDtypeStruct
    ins = dict(
        hid=anyspec, cot=anyspec, len=smem, own=smem, ga=anyspec, gf=anyspec, tab=anyspec,
        wq=anyspec, wk=anyspec, wv=anyspec, wo=anyspec, wg=anyspec, wu=anyspec, wd=anyspec,
    )
    outs = dict(
        out=sd((d, half), BF16), gin=sd((d, half), BF16),
        og=sd((4, 2, 4, cr, ff), BF16), ex=sd((HEADS, 2, 4, cr, 128), BF16), gains_out=sd((2, 1, d), F32),
    )
    names = tuple(ins) + tuple(outs) + tuple(scratch)
    o, gin, og, ex, gains = pl.pallas_call(
        functools.partial(step_kernel, names, rows, d, ff, nb),
        out_shape=tuple(outs.values()),
        in_specs=list(ins.values()),
        out_specs=(anyspec,) * len(outs),
        scratch_shapes=list(scratch.values()),
        compiler_params=pltpu.CompilerParams(
            collective_id=0, has_side_effects=True, vmem_limit_bytes=67043328
        ),
    )(
        hidden_in[0].T, cotangent[0].T, lengths, owners, gain_attn[None], gain_ffn[None],
        jnp.asarray(rope_table(2 * half)), w_query, w_key.T, w_value.T, w_output, gate_weight, up_weight, down_weight.T,
    )
    gw, block = GQ * HD, lambda *shape: (lambda index: pl.BlockSpec(shape, index))
    rowwise = lambda width: block(cr, width)(lambda i: (i, 0))
    gains_spec = lambda k: block(None, 1, d)(lambda i: (k, 0, 0))
    gain_out = block(1, d)(lambda i: (0, 0))
    o, gin, gq, gk, gv, go, gg, gu, gd, ga, gf = pl.pallas_call(
        put_kernel,
        grid=(8,),
        out_shape=(
            sd((d, half), BF16), sd((d, half), F32), sd((d, 2 * gw), F32), sd((d, 2 * HD), F32), sd((d, 2 * HD), F32),
            sd((d, 2 * gw), F32), sd((d, ff), F32), sd((d, ff), F32), sd((d, ff), F32), sd((1, d), F32), sd((1, d), F32),
        ),
        in_specs=[
            smem, rowwise(half), rowwise(half), block(4, None, None, cr, ff)(lambda i: (0, i // 4, i % 4, 0, 0)),
            block(HEADS, None, None, cr, 128)(lambda i: (0, i // 4, i % 4, 0, 0)), gains_spec(0), gains_spec(1),
        ],
        out_specs=(
            rowwise(half), rowwise(half), rowwise(2 * gw), rowwise(2 * HD), rowwise(2 * HD), rowwise(2 * gw),
            rowwise(ff), rowwise(ff), rowwise(ff), gain_out, gain_out,
        ),
    )(owners, o, gin, og, ex, gains, gains)
    return o.T[None], gin.T[None], gq, gk, gv, go.T, gg, gu, gd.T, ga[0], gf[0]


def solution(mesh):
    rep = P()
    io = P("batch", "ctx", None)
    in_specs = (io, io, P("batch"), rep, rep, rep, rep, rep, P(None, "head"), P(None, "head"), P("head", None), rep, rep)
    out_specs = (io, io, P(None, "head"), P(None, "head"), P(None, "head"), P("head", None), P(None, "head"),
                 P(None, "head"), P("head", None), rep, rep)
    return jax.shard_map(
        functools.partial(body, mesh.shape["batch"]), mesh=mesh, in_specs=in_specs, out_specs=out_specs, check_vma=False
    )
```

```python
import functools
import math
from types import SimpleNamespace

import jax
import jax.numpy as jnp
import numpy as np
from jax import lax
from jax.experimental import pallas as pl
from jax.experimental.pallas import tpu as pltpu
from jax.sharding import PartitionSpec as P

KV = 5
HD = 64
GQ = 3
QH = KV * GQ
HEADS = 4
EPS = 1e-05
NEG = -1e30
MESH = pl.DeviceIdType.MESH
F32 = jnp.float32
BF16 = jnp.bfloat16


def nn(a, b):
    return lax.dot_general(a, b, (((1,), (0,)), ((), ())), preferred_element_type=F32)


def nt(a, b):
    return lax.dot_general(a, b, (((1,), (1,)), ((), ())), preferred_element_type=F32)


def tn(a, b):
    return lax.dot_general(a, b, (((0,), (0,)), ((), ())), preferred_element_type=F32)


def rope_table(slots):
    inverse = np.exp(np.arange(HD // 2, dtype=np.float32) * np.float32(-2.0 * math.log(10000.0) / HD))
    angles = np.arange(slots, dtype=np.float32)[:, None] * inverse[None, :].astype(np.float32)
    cos, sin = np.cos(angles).astype(np.float32), np.sin(angles).astype(np.float32)
    return np.concatenate([cos, sin] * 2, axis=1)


def peer_of(h, j):
    return (h, h + 1 - 2 * (h % 2), (h + 2) % 4, 3 - h)[j]


def scratch_of(rows, d, ff, nb):
    n = HEADS
    half = n * rows
    keys = 2 * half
    dp = -(-d // 128) * 128
    cr = d // 8
    v = pltpu.VMEM
    dma = pltpu.SemaphoreType.DMA
    return dict(
        cot_v=v((d, half), BF16),
        tab_v=v((rows, 256), F32),
        gains_v=v((2, 1, d), F32),
        wq_v=v((d, QH * HD), BF16),
        wk_v=v((KV * HD, d), BF16),
        wv_v=v((KV * HD, d), BF16),
        wo_v=v((QH * HD, d), BF16),
        wf=v((3 * d, ff), BF16),
        res=v((2, rows, d), F32),
        mid=v((2, rows, d), F32),
        nat=v((2, d, rows), BF16),
        dat=v((2, d, rows), BF16),
        ql=v((2, KV, GQ * rows, 128), BF16),
        kv=v((2, KV, keys, 128), BF16),
        lse=v((2, rows, 128), F32),
        at=v((rows, d), BF16),
        nf=v((2, n, rows, d), BF16),
        gate=v((2, n, rows, ff), F32),
        up=v((2, n, rows, ff), F32),
        act=v((n, rows, ff), BF16),
        bias=v((rows, keys), F32),
        wide=v((rows, dp), F32),
        heads=v((QH, rows, 128), F32),
        part=v((2, rows, d), BF16),
        psend=v((2, 3, rows, d), BF16),
        precv=v((2, 3, rows, d), BF16),
        d_res=v((rows, d), F32),
        d_mid=v((rows, d), F32),
        df=v((2, n, rows, d), BF16),
        dg=v((n, rows, ff), BF16),
        du=v((n, rows, ff), BF16),
        ou=v((KV, GQ * rows, 128), BF16),
        dk=v((rows, KV * HD), BF16),
        dv=v((rows, KV * HD), BF16),
        dpg=v((KV, 2 * rows, 384), BF16),
        aog=v((KV, 2 * rows, 256), BF16),
        dkv=v((KV, 128, half), F32),
        dkv_ctx=v((KV, 128, half), BF16),
        dkv_ctx_r=v((2, KV, 128, half), BF16),
        dkv_s=v((KV, 3, 128, rows), BF16),
        dkv_r=v((KV, 3, 128, rows), BF16),
        fin=v((2, d, rows), BF16),
        gown=v((12, cr, ff), F32),
        sf=v((12, cr, ff), BF16),
        rf=v((12, cr, ff), BF16),
        rf2=v((12, cr, ff), BF16),
        zs=v((16, cr, ff), BF16),
        zu=v((16, cr, ff), BF16),
        zb=v((16, cr, ff), BF16),
        ha=v((KV, d // 2, 512), BF16),
        ra=v((KV, d // 2, 512), BF16),
        gain_v=v((2, 1, d), F32),
        gain_p=v((2 * n, 2, 1, d), F32),
        gain_z=v((nb, 2, 1, d), F32),
        in_sem=dma((12,)),
        loc_sem=dma((8,)),
        kv_ss=dma((2, KV)),
        kv_rs=dma((2, KV)),
        kvc_ss=dma((2, KV)),
        kvc_rs=dma((2, KV)),
        ag_ss=dma((5, 6)),
        ag_rs=dma((5, 6)),
        p_ss=dma((4, 4)),
        p_rs=dma((4, 4)),
        dc_ss=dma((2, KV)),
        dc_rs=dma((2, KV)),
        dkv_ss=dma((2, KV)),
        dkv_rs=dma((2, KV)),
        f_ss=dma((3,)),
        f_rs=dma((3,)),
        z_s0=dma((16,)),
        z_s1=dma((16,)),
        z_ur=dma((16,)),
        z_br=dma((16,)),
        og_loc=dma((16,)),
        og_ss=dma((16,)),
        og_rs=dma((16,)),
        a_ss=dma((KV,)),
        a_rs=dma((KV,)),
        h_ss=dma((4, 4)),
        h_rs=dma((4, 4)),
        ex_loc=dma((4,)),
        ex_ss=dma((4, 8)),
        ex_rs=dma((4, 8)),
        gp_ss=dma((8,)),
        gp_rs=dma((8,)),
        gz_ss=dma((nb,)),
        gz_rs=dma((nb,)),
    )


def step_kernel(names, rows, d, ff, nb, *refs):
    r = SimpleNamespace(**dict(zip(names, refs)))
    wg_v, wu_v, wd_v = (r.wf.at[pl.ds(t * d, d)] for t in range(3))
    lhs, hid_v = r.cot_v, r.fin.at[1]
    h = lax.axis_index("head")
    c = lax.axis_index("ctx")
    z = lax.axis_index("batch")
    half = HEADS * rows
    hd2 = d // 2
    cr = d // 8
    lane = lax.broadcasted_iota(jnp.int32, (rows, 128), 1)
    low = lane < HD
    quarter = (lane % HD) < HD // 2

    def copy_to(src, dst, ss, rs, where):
        return pltpu.make_async_remote_copy(
            src_ref=src, dst_ref=dst, send_sem=ss, recv_sem=rs, device_id=where, device_id_type=MESH
        )

    def remote(src, dst, ss, rs, j):
        return copy_to(src, dst, ss, rs, dict(head=peer_of(h, j)))

    def across(src, dst, ss, rs):
        return copy_to(src, dst, ss, rs, dict(ctx=1 - c))

    def load(k, src, dst):
        return pltpu.make_async_copy(src, dst, r.in_sem.at[k])

    my_rows = pl.ds(pl.multiple_of(h * rows, rows), rows)
    my_pos = pl.ds(pl.multiple_of(c * half + h * rows, rows), rows)
    loads = SimpleNamespace(
        hid=load(0, r.hid.at[:, my_rows], hid_v),
        ga=load(1, r.ga, r.gains_v.at[0]),
        gf=load(11, r.gf, r.gains_v.at[1]),
        wk=load(3, r.wk, r.wk_v),
        wv=load(4, r.wv, r.wv_v),
        tab=load(5, r.tab.at[my_pos], r.tab_v.at[:, pl.ds(0, 128)]),
        wq=load(2, r.wq, r.wq_v),
        wo=load(6, r.wo, r.wo_v),
        wg=load(7, r.wg, wg_v),
        wu=load(8, r.wu, wu_v),
        wd=load(9, r.wd, wd_v),
        cot=load(10, r.cot, r.cot_v),
    )
    for cp in vars(loads).values():
        cp.start()

    plane = [(j, x) for j in range(HEADS) for x in range(2) if (j, x) != (0, 0)]

    def plane_id(j, x):
        return dict(head=peer_of(h, j), ctx=1 - c if x else c)

    barrier = pltpu.get_barrier_semaphore()
    for j, x in plane:
        pl.semaphore_signal(barrier, inc=1, device_id=plane_id(j, x), device_id_type=MESH)
    for k in range(1, nb):
        pl.semaphore_signal(barrier, inc=1, device_id=dict(batch=(z + k) % nb), device_id_type=MESH)
    pl.semaphore_wait(barrier, len(plane) + nb - 1)

    length = r.len[0]
    row_pos = c * half + h * rows + lax.broadcasted_iota(jnp.int32, (rows, 1), 0)
    valid = (row_pos < length).astype(F32)

    zero_w = jnp.zeros((rows, 128), F32)
    r.wide[...] = jnp.zeros(r.wide.shape, F32)
    vlo = r.wide.shape[1] // 2
    r.lse[0] = zero_w
    r.lse[1] = zero_w

    @pl.when(c == 0)
    def _():
        for p in range(2):
            r.kv[p, :, half:, :] = jnp.zeros((KV, half, 128), BF16)

    def fill_mask():
        for blk in range(2 * HEADS):
            own = blk < HEADS
            base = (c if own else 1 - c) * half + peer_of(h, blk % HEADS) * rows
            kp = base + lax.broadcasted_iota(jnp.int32, (rows, rows), 1)
            qp = c * half + h * rows + lax.broadcasted_iota(jnp.int32, (rows, rows), 0)
            ok = (kp <= qp) & (kp < length)
            r.bias[:, blk * rows : (blk + 1) * rows] = jnp.where(ok, 0.0, NEG)

    def fill_cotangent():
        for j in range(HEADS):
            pr = pl.ds(pl.multiple_of(peer_of(h, j) * rows, rows), rows)
            pos = c * half + peer_of(h, j) * rows + lax.broadcasted_iota(jnp.int32, (rows, 1), 0)
            ok = (pos < length).astype(F32)
            for b, lo, w in blocks(d):
                block = r.cot_v[lo : lo + w, pr].astype(F32).T * ok
                r.df[1, j, :, lo : lo + w] = block.astype(BF16)
                if j == 0:
                    r.d_res[:, lo : lo + w] = block

    def clear_sums():
        @pl.loop(0, 12)
        def _(i):
            r.gown[i] = jnp.zeros((cr, ff), F32)
            r.sf[i] = jnp.zeros((cr, ff), BF16)

        r.gain_v[...] = jnp.zeros((2, 1, d), F32)

    def share(k, e, j):
        return remote(r.psend.at[k, j - 1], r.precv.at[k, j - 1], r.p_ss.at[e, j], r.p_rs.at[e, j], j)

    def summed(k, e):
        total = r.part[k].astype(F32)
        for j in (1, 2, 3):
            share(k, e, j).wait_recv()
            total = total + r.precv[k, j - 1].astype(F32)
        return total

    def sent(k, e):
        for j in (1, 2, 3):
            share(k, e, j).wait_send()

    def rms(x, gain):
        inv = lax.rsqrt(jnp.mean(x * x, axis=-1, keepdims=True) + EPS)
        return x * inv * gain

    def turned(x):
        return jnp.where(quarter, -pltpu.roll(x, 128 - HD // 2, 1), pltpu.roll(x, HD // 2, 1))

    def rope(x):
        return x * r.tab_v[:, 0:128] + turned(x) * r.tab_v[:, 128:256]

    def unrope(x):
        return x * r.tab_v[:, 0:128] - turned(x) * r.tab_v[:, 128:256]

    def swap(x):
        return pltpu.roll(x, HD, 1)

    def blocks(width):
        return [(b, b * 128, min(128, width - b * 128)) for b in range(-(-width // 128))]

    def head_row(i):
        return i // GQ, (i % GQ) * rows

    def store_t(dst, src):
        for b, lo, w in blocks(d):
            dst[lo : lo + w, :] = src[:, lo : lo + w].T

    gain_a = lambda: r.gains_v[0]
    gain_f = lambda: r.gains_v[1]

    loads.tab.wait()
    both = r.tab_v[:, 0:128]
    r.tab_v[:, 128:256] = jnp.where(quarter, pltpu.roll(both, 128 - HD // 2, 1), both)
    r.tab_v[:, 0:128] = jnp.where(quarter, both, pltpu.roll(both, HD // 2, 1))
    loads.ga.wait()
    loads.gf.wait()
    loads.hid.wait()
    for b, lo, w in blocks(d):
        r.res[0, :, lo : lo + w] = hid_v[lo : lo + w, :].astype(F32).T

    def gather(e, src, dst, by_owner=False):
        def hop(k, ref, to, j):
            return remote(ref, to, r.ag_ss.at[e, k], r.ag_rs.at[e, k], j)

        at = (lambda j, near, x: dst(near, x)) if by_owner else (lambda j, near, x: dst(j, x))
        first = [hop(0, src(0), at(1, 0, 0), 1), hop(3, src(1), at(2, 0, 1), 2), hop(1, src(1), at(1, 0, 1), 1),
                 hop(2, src(0), at(2, 0, 0), 2)]
        relay = [hop(4, dst(1, 0), at(3, 1, 0), 2), hop(5, dst(2, 1), at(3, 2, 1), 1)]
        def start():
            for cp in first:
                cp.start()

        def hand_on():
            first[0].wait_recv()
            relay[0].start()
            first[1].wait_recv()
            relay[1].start()

        def wait(j):
            for cp in ((first[2],), (first[3],), relay)[j - 1]:
                cp.wait_recv()

        def drain():
            for cp in first + relay:
                cp.wait_send()

        return SimpleNamespace(start=start, hand_on=hand_on, wait=wait, drain=drain)

    def halves(ref):
        n = ref.shape[0] // 2
        return lambda x: ref.at[pl.ds(x * n, n)]

    @pl.loop(0, 2)
    def _(p):
        x = r.res[p]
        na = rms(x, gain_a()).astype(BF16)
        store_t(r.nat.at[p], na)

        @pl.when(p == 0)
        def _():
            loads.wk.wait()
            loads.wv.wait()

        r.wide[:, : KV * HD] = nt(na, r.wk_v[...])
        r.wide[:, vlo : vlo + KV * HD] = nt(na, r.wv_v[...])
        for b in range(-(-KV // 2)):
            kb = rope(r.wide[:, b * 128 : (b + 1) * 128])
            vb = r.wide[:, vlo + b * 128 : vlo + (b + 1) * 128]
            r.kv[p, 2 * b, 0:rows, :] = jnp.where(low, kb, swap(vb)).astype(BF16)
            if 2 * b + 1 < KV:
                r.kv[p, 2 * b + 1, 0:rows, :] = jnp.where(low, swap(kb), vb).astype(BF16)

        def to_peer(j, g):
            return remote(
                r.kv.at[p, g, pl.ds(0, rows)], r.kv.at[p, g, pl.ds(j * rows, rows)],
                r.kv_ss.at[p, g], r.kv_rs.at[p, g], j,
            )

        def to_partner(j, g):
            return across(
                r.kv.at[p, g, pl.ds(j * rows, rows)], r.kv.at[p, g, pl.ds(half + j * rows, rows)],
                r.kvc_ss.at[p, g], r.kvc_rs.at[p, g],
            )

        def all_peers(g):
            span = r.kv.at[p, g, pl.ds(rows, 3 * rows)]
            return remote(span, span, r.kv_ss.at[p, g], r.kv_rs.at[p, g], 1)

        def all_partner(g):
            span = r.kv.at[p, g, pl.ds(half, half)]
            return across(span, span, r.kvc_ss.at[p, g], r.kvc_rs.at[p, g])

        for g in range(KV):
            for j in (1, 2, 3):
                to_peer(j, g).start()

            @pl.when(c == 0)
            def _():
                to_partner(0, g).start()

        def arrive(g):
            all_peers(g).wait_recv()

            @pl.when(c == 0)
            def _():
                for j in (1, 2, 3):
                    to_partner(j, g).start()

        @pl.when(p == 0)
        def _():
            fill_mask()
            loads.wq.wait()

        r.wide[:, :d] = nn(na, r.wq_v[...])
        for b, lo, w in blocks(d):
            y = rope(r.wide[:, lo : lo + 128]).astype(BF16).astype(F32) * HD ** (-0.5)
            g, o = head_row(2 * b)
            r.ql[p, g, o : o + rows, :] = jnp.where(low, y, 0.0).astype(BF16)
            if 2 * b + 1 < QH:
                g, o = head_row(2 * b + 1)
                r.ql[p, g, o : o + rows, :] = jnp.where(low, swap(y), 0.0).astype(BF16)

        arrive(0)

        @pl.loop(0, KV)
        def _(g):
            @pl.when(g < KV - 1)
            def _():
                arrive(g + 1)

            @pl.when(c == 1)
            def _():
                all_partner(g).wait_recv()

            kv = r.kv[p, g]
            for k in range(GQ):
                s = nt(r.ql[p, g, k * rows : (k + 1) * rows, :], kv)
                s = jnp.where(r.bias[...] < 0.0, NEG, s)
                m = jnp.max(s, axis=-1, keepdims=True)
                e = jnp.exp(s - m)
                t = jnp.sum(e, axis=-1, keepdims=True)
                r.lse[p] += jnp.where(lane == g * GQ + k, m + jnp.log(t), 0.0)
                r.heads[g * GQ + k] = nn((e / t).astype(BF16), kv)

        mine = pl.ds(pl.multiple_of(p * rows, rows), rows)
        for g in range(KV):
            o0, o1, o2 = (r.heads[g * GQ + k] for k in range(GQ))
            r.aog[g, mine, 0:128] = jnp.where(low, 0.0, o0).astype(BF16)
            r.aog[g, mine, 128:256] = jnp.where(low, swap(o1), o2).astype(BF16)
        for b, lo, w in blocks(d):
            first = swap(r.heads[2 * b])
            both = jnp.where(low, first, r.heads[2 * b + 1]) if 2 * b + 1 < QH else first
            r.at[:, lo : lo + w] = both[:, :w].astype(BF16)

        @pl.when(p == 0)
        def _():
            loads.wo.wait()

        mid = r.res[p] + nn(r.at[...], r.wo_v[...])
        r.mid[p] = mid
        r.nf[p, 0] = rms(mid, gain_f()).astype(BF16)
        ag = gather(p, halves(r.nf.at[p, 0]), lambda j, x: halves(r.nf.at[p, j])(x))
        ag.start()

        @pl.when(p == 0)
        def _():
            loads.wg.wait()
            loads.wu.wait()
            loads.wd.wait()

        for j in range(HEADS):
            if j == 1:
                ag.hand_on()
            if j:
                ag.wait(j)
            nf = r.nf[p, j]
            gate = nn(nf, wg_v[...])
            up = nn(nf, wu_v[...])
            r.gate[p, j] = gate
            r.up[p, j] = up
            act = (gate / (1.0 + jnp.exp(-gate)) * up).astype(BF16)
            part = nt(act, wd_v[...])
            if j == 0:
                r.part[p] = part.astype(BF16)
            else:
                r.psend[p, j - 1] = part.astype(BF16)
                share(p, p, j).start()
        ag.drain()

        @pl.when(p == 0)
        def _():
            loads.cot.wait()
            fill_cotangent()
            clear_sums()
            r.res[1] = valid * (r.mid[0] + summed(0, 0))
            sent(0, 0)

        @pl.loop(0, KV)
        def _(g):
            all_peers(g).wait_send()

            @pl.when(c == 0)
            def _():
                all_partner(g).wait_send()

    def final(k, out):
        def there(j, x):
            at = pl.ds(pl.multiple_of(peer_of(h, j) * rows, rows), rows)
            return out.at[pl.ds(x * hd2, hd2), at]

        own = pltpu.make_async_copy(r.fin.at[k], out.at[:, my_rows], r.loc_sem.at[k])
        ag = gather(3 + k, halves(r.fin.at[k]), there, True)

        def put(value):
            store_t(r.fin.at[k], value.astype(BF16))
            own.start()

        return SimpleNamespace(put=put, own=own, send=ag.start, hand_on=ag.hand_on, wait=ag.wait, drain=ag.drain)

    low_side = z < nb // 2
    middle = (z == nb // 2 - 1) | (z == nb // 2)
    handed = (z > 0) & (z < nb - 1)
    inwards = jnp.where(low_side, 1, -1)

    def zcopy(src, dst, ss, rs, dz):
        return copy_to(src, dst, ss, rs, dict(batch=z + dz))

    def to_next(i):
        return zcopy(r.zs.at[i], r.zu.at[i], r.z_s0.at[i], r.z_ur.at[i], inwards)

    def to_middle(i):
        return zcopy(r.zs.at[i], r.zb.at[i], r.z_s0.at[i], r.z_br.at[i], inwards)

    def to_outer(i, src):
        return zcopy(src.at[i], r.zb.at[i], r.z_s1.at[i], r.z_br.at[i], -inwards)

    def inward(i, own):
        @pl.when(handed)
        def _():
            to_next(i).wait_recv()
            r.zs[i] = (own() + r.zu[i].astype(F32)).astype(BF16)

        @pl.when(jnp.logical_not(handed))
        def _():
            r.zs[i] = own().astype(BF16)

        @pl.when(middle)
        def _():
            to_middle(i).start()

        @pl.when(jnp.logical_not(middle))
        def _():
            to_next(i).start()

    def og_local(i, src):
        return pltpu.make_async_copy(src.at[i], r.og.at[i // 4, c, i % 4], r.og_loc.at[i])

    def og_across(i, src):
        return across(src.at[i], r.og.at[i // 4, c, i % 4], r.og_ss.at[i], r.og_rs.at[i])

    def ex_local(q, src):
        return pltpu.make_async_copy(src.at[12 + q, :, pl.ds(512, 128)], r.ex.at[h, c, q], r.ex_loc.at[q])

    def ex_plane(q, src, j, x):
        return copy_to(
            src.at[12 + q, :, pl.ds(512, 128)], r.ex.at[h, c, q],
            r.ex_ss.at[q, 2 * j + x], r.ex_rs.at[q, 2 * j + x], plane_id(j, x),
        )

    def ex_hand_on(q, j):
        at = r.ex.at[peer_of(h, j), c, q]
        return across(at, at, r.ex_ss.at[q, 2 * j + 1], r.ex_rs.at[q, 2 * j + 1])

    def ex_arrive(q):
        for j in (1, 2, 3):
            ex_plane(q, r.zs, j, 0).wait_send()
            ex_plane(q, r.zs, j, 0).wait_recv()
            ex_hand_on(q, j).start()

    def outward(i):
        def place(src):
            @pl.when(handed)
            def _():
                to_outer(i, src).start()

            og_local(i, src).start()
            og_across(i, src).start()
            if isinstance(i, int) and i >= 12:
                ex_local(i - 12, src).start()
                for j, x in ((3, 0), (1, 0), (2, 0), (0, 1)):
                    ex_plane(i - 12, src, j, x).start()

        to_middle(i).wait_recv()

        @pl.when(middle)
        def _():
            to_middle(i).wait_send()
            r.zs[i] = (r.zs[i].astype(F32) + r.zb[i].astype(F32)).astype(BF16)
            place(r.zs)

        @pl.when(jnp.logical_not(middle))
        def _():
            place(r.zb)

    def ffn_half(t):
        sl = pl.ds(4 * t, 4)
        return across(r.sf.at[sl], r.rf.at[sl], r.f_ss.at[t], r.f_rs.at[t])

    def ffn_piece(i):
        @pl.when(i % 4 == 0)
        def _():
            ffn_half(i // 4).wait_recv()

        inward(i, lambda: r.gown[i] + r.rf[i].astype(F32))

    def within(i, cond, do):
        if isinstance(i, int) and not 0 <= i < 16:
            return

        @pl.when((i >= 0) & (i < 16) & cond)
        def _():
            do(i)

    outer = jnp.logical_not(handed)

    def outer_pieces(lo, hi):
        @pl.when(outer)
        def _():
            pl.loop(lo, hi)(ffn_piece)

    def turn(m):
        piece = lambda i: (attention_piece if isinstance(i, int) and i >= 12 else ffn_piece)(i)
        within(m, handed, piece)
        if isinstance(m, int) and m in (9, 11, 13, 15):
            within(12 + (m - 9) // 2, outer, piece)
        if not isinstance(m, int) or m <= 13:
            within(m - 2, middle, outward)
        if isinstance(m, int) and m >= 13:
            within(m - 1, middle, outward)
        within(m - 5, jnp.logical_not(middle), outward)

    def norm_bwd(x, gain, dn):
        inv = lax.rsqrt(jnp.mean(x * x, axis=-1, keepdims=True) + EPS)
        u = gain * dn
        dx = inv * u - x * (inv * inv * inv) * jnp.mean(x * u, axis=-1, keepdims=True)
        return dx, jnp.sum(dn * x * inv, axis=0, keepdims=True)

    mine_half = pl.ds(pl.multiple_of(c * hd2, hd2), hd2)
    other_half = pl.ds(pl.multiple_of((1 - c) * hd2, hd2), hd2)

    def a_half(g):
        src = r.wf.at[pl.ds(pl.multiple_of(g * hd2, hd2), hd2), pl.ds(0, 512)]
        return across(src, r.ra.at[g], r.a_ss.at[g], r.a_rs.at[g])

    def first_group(to):
        g = jnp.int32(KV - 1)
        for k in reversed(range(KV - 1)):
            g = jnp.where(r.own[k] == to, k, g)
        return g

    g1 = jnp.int32(0)
    for k in range(1, KV):
        for i in range(k):
            g1 = jnp.where(r.own[k] == r.own[i], k, g1)

    def own_share(to, q):
        at = pl.ds(q * cr, cr)
        g0 = first_group(to)
        first = r.ha[g0, at, :].astype(F32) + r.ra[g0, at, :].astype(F32)
        cols = pl.ds(pl.multiple_of(to * 128, 128), 128)
        second = r.ha[g1, at, cols].astype(F32) + r.ra[g1, at, cols].astype(F32)
        return jnp.concatenate([first, second], axis=1)

    def head_share(j, q):
        i = 4 * (j - 1) + q
        return remote(r.sf.at[i], r.rf2.at[i], r.h_ss.at[j, q], r.h_rs.at[j, q], j)

    def attention_sums():
        @pl.loop(0, KV)
        def _(g):
            def product(rows_of):
                first = nn(jnp.concatenate([r.nat[0, rows_of, :], r.nat[1, rows_of, :]], axis=1), r.dpg[g])
                second = nn(jnp.concatenate([r.dat[0, rows_of, :], r.dat[1, rows_of, :]], axis=1), r.aog[g])
                return first[:, :256], first[:, 256:] + second[:, :128], second[:, 128:]

            def put(dst, parts):
                dst[:, 0:256] = parts[0].astype(BF16)
                dst[:, 256:384] = parts[1].astype(BF16)
                dst[:, 384:512] = parts[2].astype(BF16)

            put(r.wf.at[pl.ds(pl.multiple_of(g * hd2, hd2), hd2)], product(other_half))
            a_half(g).start()
            put(r.ha.at[g], product(mine_half))

            @pl.when(g % 3 == 1)
            def _():
                turn(KV + g // 3)

        @pl.loop(0, KV)
        def _(g):
            a_half(g).wait_recv()

        for t in range(3):
            ffn_half(t).wait_send()
        for q in range(4):
            for j in (3, 1, 2):
                r.sf[4 * (j - 1) + q] = own_share(peer_of(h, j), q).astype(BF16)
                head_share(j, q).start()
        turn(KV + 2)

    def attention_piece(i):
        q = i - 12

        def own():
            v = own_share(h, q)
            for j in (1, 2, 3):
                head_share(j, q).wait_recv()
                v = v + r.rf2[4 * (j - 1) + q].astype(F32)
            return v

        inward(i, own)

    @pl.loop(0, 2)
    def _(back):
        p = 1 - back
        ag = gather(2, halves(r.df.at[0, 0]), lambda j, x: halves(r.df.at[0, j])(x))

        @pl.when(p == 0)
        def _():
            block = r.d_res[...] * valid
            r.d_res[...] = block
            r.df[0, 0] = block.astype(BF16)
            ag.start()

        for j in range(HEADS):
            if j:
                @pl.when(p == 0)
                def _():
                    if j == 1:
                        ag.hand_on()
                    ag.wait(j)

            d_act = nn(r.df[p, j], wd_v[...])
            gate, up = r.gate[p, j], r.up[p, j]
            s = 1.0 / (1.0 + jnp.exp(-gate))
            dg = (d_act * up * s * (1.0 + gate * (1.0 - s))).astype(BF16)
            du = (d_act * (gate * s)).astype(BF16)
            r.act[j] = (gate * s * up).astype(BF16)
            r.dg[j] = dg
            r.du[j] = du
            part = nt(dg, wg_v[...]) + nt(du, wu_v[...])
            if j == 0:
                r.part[1 - p] = part.astype(BF16)
            else:
                r.psend[1 - p, j - 1] = part.astype(BF16)
                share(1 - p, 3 - p, j).start()
        for t, rhs in ((0, r.dg), (1, r.du), (2, r.act)):
            if t != 1:
                src = r.nf if t == 0 else r.df
                for j in range(HEADS):
                    store_t(lhs.at[:, j * rows : (j + 1) * rows], src[p, j])
            right = rhs[...].reshape(half, ff)
            theirs = nn(lhs[other_half, :], right)
            for q in range(4):
                v = theirs[q * cr : (q + 1) * cr] + r.sf[4 * t + q].astype(F32)
                r.sf[4 * t + q] = v.astype(BF16)

            @pl.when(p == 0)
            def _():
                ffn_half(t).start()

            ours = nn(lhs[mine_half, :], right)
            for q in range(4):
                r.gown[4 * t + q] += ours[q * cr : (q + 1) * cr]

        @pl.when(p == 0)
        def _():
            outer_pieces(0, 8)

        @pl.when(p == 1)
        def _():
            final(0, r.out).put(valid * (r.mid[1] + summed(1, 1)))
            final(0, r.out).send()
            sent(1, 1)

        dn = summed(1 - p, 3 - p)
        dx, dgain = norm_bwd(r.mid[p], gain_f(), dn)
        d_mid = r.d_res[...] + dx
        r.d_mid[...] = d_mid
        r.gain_v[1] += dgain
        da = d_mid.astype(BF16)
        store_t(r.dat.at[p], da)
        r.wide[:, :d] = nt(da, r.wo_v[...])
        for b, lo, w in blocks(d):
            y = r.wide[:, lo : lo + 128]
            g, o = head_row(2 * b)
            r.ou[g, o : o + rows, :] = jnp.where(low, 0.0, swap(y)).astype(BF16)
            if 2 * b + 1 < QH:
                g, o = head_row(2 * b + 1)
                r.ou[g, o : o + rows, :] = jnp.where(low, 0.0, y).astype(BF16)

        def hop(g):
            return across(r.dkv_ctx.at[g], r.dkv_ctx_r.at[p, g], r.dc_ss.at[p, g], r.dc_rs.at[p, g])

        def to_owner(j, g):
            return remote(
                r.dkv_s.at[g, j - 1], r.dkv_r.at[g, j - 1], r.dkv_ss.at[p, g], r.dkv_rs.at[p, g], j
            )

        def all_owners(g):
            return remote(r.dkv_s.at[g], r.dkv_r.at[g], r.dkv_ss.at[p, g], r.dkv_rs.at[p, g], 1)

        def pass_on(g):
            @pl.when(c == 0)
            def _():
                hop(g).wait_recv()
                r.dkv[g] += r.dkv_ctx_r[p, g].astype(F32)

            for j in (1, 2, 3):
                r.dkv_s[g, j - 1] = r.dkv[g, :, j * rows : (j + 1) * rows].astype(BF16)
                to_owner(j, g).start()

        @pl.loop(0, KV)
        def _(g):
            kv = r.kv[p, g]
            acc = None
            for k in range(GQ):
                q = r.ql[p, g, k * rows : (k + 1) * rows, :]
                o = r.ou[g, k * rows : (k + 1) * rows, :]
                s = nt(q, kv)
                s = jnp.where(r.bias[...] < 0.0, NEG, s)
                lse = jnp.sum(jnp.where(lane == g * GQ + k, r.lse[p], 0.0), axis=-1, keepdims=True)
                pr = jnp.exp(s - lse)
                dpr = nt(o, kv)
                delta = jnp.sum(pr * dpr, axis=-1, keepdims=True)
                ds = (pr * (dpr - delta)).astype(BF16)
                r.heads[g * GQ + k] = unrope(nn(ds, kv) * HD ** (-0.5))
                t = nn(o.T, pr.astype(BF16)) + nn(q.T, ds)
                acc = t if acc is None else acc + t
            r.dkv[g] = acc[:, :half]
            r.dkv_ctx[g] = acc[:, half:].astype(BF16)

            @pl.when(c == 1)
            def _():
                hop(g).start()

            @pl.when(g > 0)
            def _():
                pass_on(g - 1)

            @pl.when((p == 0) & (g == 0))
            def _():
                outer_pieces(8, 12)

            @pl.when((p == 0) & (g > 0))
            def _():
                turn(g - 1)

        pass_on(KV - 1)
        mine = pl.ds(pl.multiple_of(p * rows, rows), rows)
        for b, lo, w in blocks(d):
            y = r.heads[2 * b]
            if 2 * b + 1 < QH:
                y = jnp.where(low, y, swap(r.heads[2 * b + 1]))
            r.at[:, lo : lo + w] = y[:, :w].astype(BF16)
        for g in range(KV):
            both = jnp.where(low, r.heads[g * GQ], swap(r.heads[g * GQ + 1]))
            r.dpg[g, mine, 0:128] = both.astype(BF16)

        r.wide[:, :d] = nt(r.at[...], r.wq_v[...])

        @pl.when(p == 0)
        def _():
            turn(KV - 1)

        keys, vals = [], []
        for g in range(KV):
            t = r.dkv[g, :, 0:rows]
            all_owners(g).wait_recv()
            for j in range(3):
                t = t + r.dkv_r[g, j].astype(F32)
            t = t.T
            kt, vt = unrope(t), swap(t)
            keys.append(kt)
            vals.append(t)
            r.dpg[g, mine, 128:256] = jnp.where(low, r.heads[g * GQ + 2], swap(kt)).astype(BF16)
            r.dpg[g, mine, 256:384] = jnp.where(low, vt, 0.0).astype(BF16)
        for b, lo, w in blocks(KV * HD):
            kb, vb = keys[2 * b], swap(vals[2 * b])
            if 2 * b + 1 < KV:
                kb = jnp.where(low, kb, swap(keys[2 * b + 1]))
                vb = jnp.where(low, vb, vals[2 * b + 1])
            r.dk[:, lo : lo + w] = kb[:, :w].astype(BF16)
            r.dv[:, lo : lo + w] = vb[:, :w].astype(BF16)
        @pl.when(p == 0)
        def _():
            attention_sums()

        dna = r.wide[:, :d] + nn(r.dk[...], r.wk_v[...]) + nn(r.dv[...], r.wv_v[...])
        dx, dgain = norm_bwd(r.res[p], gain_a(), dna)
        r.d_res[...] = r.d_mid[...] + dx
        r.gain_v[0] += dgain
        sent(1 - p, 3 - p)

        @pl.when(p == 0)
        def _():
            ag.drain()

        @pl.when(p == 1)
        def _():
            final(0, r.out).hand_on()


        @pl.loop(0, KV)
        def _(g):
            all_owners(g).wait_send()

            @pl.when(c == 1)
            def _():
                hop(g).wait_send()

    final(1, r.gin).put(r.d_res[...])

    me = 2 * h + c
    r.gain_p[me] = r.gain_v[...]
    gp = [copy_to(r.gain_p.at[me], r.gain_p.at[me], r.gp_ss.at[2 * j + x], r.gp_rs.at[2 * j + x], plane_id(j, x))
          for j, x in plane]
    for cp in gp:
        cp.start()

    for cp in gp:
        cp.wait_recv()
    total = r.gain_p[0]
    for k in range(1, 2 * HEADS):
        total = total + r.gain_p[k]
    r.gain_z[z] = total
    gz = [copy_to(r.gain_z.at[z], r.gain_z.at[z], r.gz_ss.at[k], r.gz_rs.at[k], dict(batch=(z + k) % nb))
          for k in range(1, nb)]
    for cp in gz:
        cp.start()

    for m in range(KV + 3, 21):
        turn(m)
        if m == 15:
            final(1, r.gin).send()
        if m == 18:
            final(1, r.gin).hand_on()

    for cp in gz:
        cp.wait_recv()
    total = r.gain_z[0]
    for k in range(1, nb):
        total = total + r.gain_z[k]
    r.gain_v[...] = total
    gains_out = pltpu.make_async_copy(r.gain_v, r.gains_out, r.loc_sem.at[2])
    gains_out.start()

    for q in range(4):
        ex_arrive(q)

    gains_out.wait()
    for cp in gp + gz:
        cp.wait_send()
    for j in (1, 2, 3):
        for q in range(4):
            head_share(j, q).wait_send()

    @pl.loop(0, KV)
    def _(g):
        a_half(g).wait_send()

    @pl.loop(0, 16)
    def _(i):
        og_local(i, r.zs).wait()
        og_across(i, r.zs).wait_send()
        og_across(i, r.zs).wait_recv()

        @pl.when(jnp.logical_not(middle))
        def _():
            to_next(i).wait_send()

        @pl.when(handed)
        def _():
            to_outer(i, r.zs).wait_send()

    for q in range(4):
        ex_local(q, r.zs).wait()
        ex_plane(q, r.zs, 0, 1).wait()
        for j in (1, 2, 3):
            ex_hand_on(q, j).wait()
    for k, out in ((0, r.out), (1, r.gin)):
        end = final(k, out)
        end.own.wait()
        for j in (1, 2, 3):
            end.wait(j)
        end.drain()


def put_kernel(own, o, gin, og, ex, ga, gf, o_out, gin_out, gq, gk, gv, go, gg, gu, gd, ga_out, gf_out):
    h = lax.axis_index("head")
    held = jnp.int32(0)
    for k in range(KV):
        held = held + jnp.where(own[k] == h, 1, 0)
    gw = GQ * HD
    o_out[...] = o[...]
    gin_out[...] = gin[...].astype(F32)
    gg[...] = og[0].astype(F32)
    gu[...] = og[1].astype(F32)
    gd[...] = og[2].astype(F32)
    ga_out[...] = ga[...]
    gf_out[...] = gf[...]
    first = og[3, :, 0:512].astype(F32)
    second = jnp.concatenate([ex[k].astype(F32) for k in range(HEADS)], axis=1)
    second = jnp.where(held > 1, second, 0.0)
    for out, lo, width in ((gq, 0, gw), (gk, gw, HD), (gv, gw + HD, HD), (go, gw + 2 * HD, gw)):
        out[...] = jnp.concatenate([first[:, lo : lo + width], second[:, lo : lo + width]], axis=1)


def body(nb, hidden_in, cotangent, lengths, owners, w_query, w_key, w_value, w_output, gate_weight, up_weight, down_weight,
         gain_attn, gain_ffn):
    half, d = hidden_in.shape[1:]
    ff = gate_weight.shape[1]
    rows = half // HEADS
    cr = d // 8
    scratch = scratch_of(rows, d, ff, nb)
    anyspec = pl.BlockSpec(memory_space=pl.ANY)
    smem = pl.BlockSpec(memory_space=pltpu.SMEM)
    sd = jax.ShapeDtypeStruct
    ins = dict(
        hid=anyspec, cot=anyspec, len=smem, own=smem, ga=anyspec, gf=anyspec, tab=anyspec,
        wq=anyspec, wk=anyspec, wv=anyspec, wo=anyspec, wg=anyspec, wu=anyspec, wd=anyspec,
    )
    outs = dict(
        out=sd((d, half), BF16), gin=sd((d, half), BF16),
        og=sd((4, 2, 4, cr, ff), BF16), ex=sd((HEADS, 2, 4, cr, 128), BF16), gains_out=sd((2, 1, d), F32),
    )
    names = tuple(ins) + tuple(outs) + tuple(scratch)
    o, gin, og, ex, gains = pl.pallas_call(
        functools.partial(step_kernel, names, rows, d, ff, nb),
        out_shape=tuple(outs.values()),
        in_specs=list(ins.values()),
        out_specs=(anyspec,) * len(outs),
        scratch_shapes=list(scratch.values()),
        compiler_params=pltpu.CompilerParams(
            collective_id=0, has_side_effects=True, vmem_limit_bytes=67043328
        ),
    )(
        hidden_in[0].T, cotangent[0].T, lengths, owners, gain_attn[None], gain_ffn[None],
        jnp.asarray(rope_table(2 * half)), w_query, w_key.T, w_value.T, w_output, gate_weight, up_weight, down_weight.T,
    )
    gw, block = GQ * HD, lambda *shape: (lambda index: pl.BlockSpec(shape, index))
    rowwise = lambda width: block(cr, width)(lambda i: (i, 0))
    gains_spec = lambda k: block(None, 1, d)(lambda i: (k, 0, 0))
    gain_out = block(1, d)(lambda i: (0, 0))
    o, gin, gq, gk, gv, go, gg, gu, gd, ga, gf = pl.pallas_call(
        put_kernel,
        grid=(8,),
        out_shape=(
            sd((d, half), BF16), sd((d, half), F32), sd((d, 2 * gw), F32), sd((d, 2 * HD), F32), sd((d, 2 * HD), F32),
            sd((d, 2 * gw), F32), sd((d, ff), F32), sd((d, ff), F32), sd((d, ff), F32), sd((1, d), F32), sd((1, d), F32),
        ),
        in_specs=[
            smem, rowwise(half), rowwise(half), block(4, None, None, cr, ff)(lambda i: (0, i // 4, i % 4, 0, 0)),
            block(HEADS, None, None, cr, 128)(lambda i: (0, i // 4, i % 4, 0, 0)), gains_spec(0), gains_spec(1),
        ],
        out_specs=(
            rowwise(half), rowwise(half), rowwise(2 * gw), rowwise(2 * HD), rowwise(2 * HD), rowwise(2 * gw),
            rowwise(ff), rowwise(ff), rowwise(ff), gain_out, gain_out,
        ),
    )(owners, o, gin, og, ex, gains, gains)
    return o.T[None], gin.T[None], gq, gk, gv, go.T, gg, gu, gd.T, ga[0], gf[0]


def solution(mesh):
    rep = P()
    io = P("batch", "ctx", None)
    in_specs = (io, io, P("batch"), rep, rep, rep, rep, rep, P(None, "head"), P(None, "head"), P("head", None), rep, rep)
    out_specs = (io, io, P(None, "head"), P(None, "head"), P(None, "head"), P("head", None), P(None, "head"),
                 P(None, "head"), P("head", None), rep, rep)
    return jax.shard_map(
        functools.partial(body, mesh.shape["batch"]), mesh=mesh, in_specs=in_specs, out_specs=out_specs, check_vma=False
    )
```

```python
import functools
import math
from types import SimpleNamespace

import jax
import jax.numpy as jnp
import numpy as np
from jax import lax
from jax.experimental import pallas as pl
from jax.experimental.pallas import tpu as pltpu
from jax.sharding import PartitionSpec as P

KV = 5
HD = 64
GQ = 3
QH = KV * GQ
HEADS = 4
EPS = 1e-05
NEG = -1e30
MESH = pl.DeviceIdType.MESH
F32 = jnp.float32
BF16 = jnp.bfloat16


def nn(a, b):
    return lax.dot_general(a, b, (((1,), (0,)), ((), ())), preferred_element_type=F32)


def nt(a, b):
    return lax.dot_general(a, b, (((1,), (1,)), ((), ())), preferred_element_type=F32)


def tn(a, b):
    return lax.dot_general(a, b, (((0,), (0,)), ((), ())), preferred_element_type=F32)


def rope_table(slots):
    inverse = np.exp(np.arange(HD // 2, dtype=np.float32) * np.float32(-2.0 * math.log(10000.0) / HD))
    angles = np.arange(slots, dtype=np.float32)[:, None] * inverse[None, :].astype(np.float32)
    cos, sin = np.cos(angles).astype(np.float32), np.sin(angles).astype(np.float32)
    return np.concatenate([cos, sin] * 2, axis=1)


def peer_of(h, j):
    return (h, h + 1 - 2 * (h % 2), (h + 2) % 4, 3 - h)[j]


def scratch_of(rows, d, ff, nb):
    n = HEADS
    half = n * rows
    keys = 2 * half
    dp = -(-d // 128) * 128
    cr = d // 8
    v = pltpu.VMEM
    dma = pltpu.SemaphoreType.DMA
    return dict(
        cot_v=v((d, half), BF16),
        tab_v=v((rows, 256), F32),
        gains_v=v((2, 1, d), F32),
        wq_v=v((d, QH * HD), BF16),
        wk_v=v((KV * HD, d), BF16),
        wv_v=v((KV * HD, d), BF16),
        wo_v=v((QH * HD, d), BF16),
        wf=v((3 * d, ff), BF16),
        res=v((2, rows, d), F32),
        mid=v((2, rows, d), F32),
        nat=v((2, d, rows), BF16),
        dat=v((2, d, rows), BF16),
        ql=v((2, KV, GQ * rows, 128), BF16),
        kv=v((2, KV, keys, 128), BF16),
        lse=v((2, rows, 128), F32),
        at=v((rows, d), BF16),
        nf=v((2, n, rows, d), BF16),
        gate=v((2, n, rows, ff), F32),
        up=v((2, n, rows, ff), F32),
        act=v((n, rows, ff), BF16),
        bias=v((rows, keys), F32),
        wide=v((rows, dp), F32),
        heads=v((QH, rows, 128), F32),
        part=v((2, rows, d), BF16),
        psend=v((2, 3, rows, d), BF16),
        precv=v((2, 3, rows, d), BF16),
        d_res=v((rows, d), F32),
        d_mid=v((rows, d), F32),
        df=v((2, n, rows, d), BF16),
        dg=v((n, rows, ff), BF16),
        du=v((n, rows, ff), BF16),
        ou=v((KV, GQ * rows, 128), BF16),
        dk=v((rows, KV * HD), BF16),
        dv=v((rows, KV * HD), BF16),
        dpg=v((KV, 2 * rows, 384), BF16),
        aog=v((KV, 2 * rows, 256), BF16),
        dkv=v((KV, 128, half), F32),
        dkv_ctx=v((KV, 128, half), BF16),
        dkv_ctx_r=v((2, KV, 128, half), BF16),
        dkv_s=v((KV, 3, 128, rows), BF16),
        dkv_r=v((KV, 3, 128, rows), BF16),
        fin=v((2, d, rows), BF16),
        gown=v((12, cr, ff), F32),
        sf=v((12, cr, ff), BF16),
        rf=v((12, cr, ff), BF16),
        rf2=v((12, cr, ff), BF16),
        zs=v((16, cr, ff), BF16),
        zu=v((16, cr, ff), BF16),
        zb=v((16, cr, ff), BF16),
        ha=v((KV, d // 2, 512), BF16),
        ra=v((KV, d // 2, 512), BF16),
        gain_v=v((2, 1, d), F32),
        gain_p=v((2 * n, 2, 1, d), F32),
        gain_z=v((nb, 2, 1, d), F32),
        in_sem=dma((12,)),
        loc_sem=dma((8,)),
        kv_ss=dma((2, KV)),
        kv_rs=dma((2, KV)),
        kvc_ss=dma((2, KV)),
        kvc_rs=dma((2, KV)),
        ag_ss=dma((5, 6)),
        ag_rs=dma((5, 6)),
        p_ss=dma((4, 4)),
        p_rs=dma((4, 4)),
        dc_ss=dma((2, KV)),
        dc_rs=dma((2, KV)),
        dkv_ss=dma((2, KV)),
        dkv_rs=dma((2, KV)),
        f_ss=dma((3,)),
        f_rs=dma((3,)),
        z_s0=dma((17,)),
        z_s1=dma((17,)),
        z_ur=dma((17,)),
        z_br=dma((17,)),
        og_loc=dma((17,)),
        og_ss=dma((17,)),
        og_rs=dma((17,)),
        a_ss=dma((KV,)),
        a_rs=dma((KV,)),
        h_ss=dma((4, 5)),
        h_rs=dma((4, 5)),
        ex_loc=dma((4,)),
        ex_ss=dma((4, 8)),
        ex_rs=dma((4, 8)),
        gp_ss=dma((8,)),
        gp_rs=dma((8,)),
        gz_ss=dma((nb,)),
        gz_rs=dma((nb,)),
    )


def step_kernel(names, rows, d, ff, nb, *refs):
    r = SimpleNamespace(**dict(zip(names, refs)))
    wg_v, wu_v, wd_v = (r.wf.at[pl.ds(t * d, d)] for t in range(3))
    lhs, hid_v = r.cot_v, r.fin.at[1]
    h = lax.axis_index("head")
    c = lax.axis_index("ctx")
    z = lax.axis_index("batch")
    half = HEADS * rows
    hd2 = d // 2
    cr = d // 8
    lane = lax.broadcasted_iota(jnp.int32, (rows, 128), 1)
    low = lane < HD
    quarter = (lane % HD) < HD // 2

    def copy_to(src, dst, ss, rs, where):
        return pltpu.make_async_remote_copy(
            src_ref=src, dst_ref=dst, send_sem=ss, recv_sem=rs, device_id=where, device_id_type=MESH
        )

    def remote(src, dst, ss, rs, j):
        return copy_to(src, dst, ss, rs, dict(head=peer_of(h, j)))

    def across(src, dst, ss, rs):
        return copy_to(src, dst, ss, rs, dict(ctx=1 - c))

    def load(k, src, dst):
        return pltpu.make_async_copy(src, dst, r.in_sem.at[k])

    my_rows = pl.ds(pl.multiple_of(h * rows, rows), rows)
    my_pos = pl.ds(pl.multiple_of(c * half + h * rows, rows), rows)
    loads = SimpleNamespace(
        hid=load(0, r.hid.at[:, my_rows], hid_v),
        ga=load(1, r.ga, r.gains_v.at[0]),
        gf=load(11, r.gf, r.gains_v.at[1]),
        wk=load(3, r.wk, r.wk_v),
        wv=load(4, r.wv, r.wv_v),
        tab=load(5, r.tab.at[my_pos], r.tab_v.at[:, pl.ds(0, 128)]),
        wq=load(2, r.wq, r.wq_v),
        wo=load(6, r.wo, r.wo_v),
        wg=load(7, r.wg, wg_v),
        wu=load(8, r.wu, wu_v),
        wd=load(9, r.wd, wd_v),
        cot=load(10, r.cot, r.cot_v),
    )
    for cp in vars(loads).values():
        cp.start()

    plane = [(j, x) for j in range(HEADS) for x in range(2) if (j, x) != (0, 0)]

    def plane_id(j, x):
        return dict(head=peer_of(h, j), ctx=1 - c if x else c)

    barrier = pltpu.get_barrier_semaphore()
    for j, x in plane:
        pl.semaphore_signal(barrier, inc=1, device_id=plane_id(j, x), device_id_type=MESH)
    for k in range(1, nb):
        pl.semaphore_signal(barrier, inc=1, device_id=dict(batch=(z + k) % nb), device_id_type=MESH)
    pl.semaphore_wait(barrier, len(plane) + nb - 1)

    length = r.len[0]
    row_pos = c * half + h * rows + lax.broadcasted_iota(jnp.int32, (rows, 1), 0)
    valid = (row_pos < length).astype(F32)

    zero_w = jnp.zeros((rows, 128), F32)
    r.wide[...] = jnp.zeros(r.wide.shape, F32)
    vlo = r.wide.shape[1] // 2
    r.lse[0] = zero_w
    r.lse[1] = zero_w

    @pl.when(c == 0)
    def _():
        for p in range(2):
            r.kv[p, :, half:, :] = jnp.zeros((KV, half, 128), BF16)

    def fill_mask():
        for blk in range(2 * HEADS):
            own = blk < HEADS
            base = (c if own else 1 - c) * half + peer_of(h, blk % HEADS) * rows
            kp = base + lax.broadcasted_iota(jnp.int32, (rows, rows), 1)
            qp = c * half + h * rows + lax.broadcasted_iota(jnp.int32, (rows, rows), 0)
            ok = (kp <= qp) & (kp < length)
            r.bias[:, blk * rows : (blk + 1) * rows] = jnp.where(ok, 0.0, NEG)

    def fill_cotangent():
        for j in range(HEADS):
            pr = pl.ds(pl.multiple_of(peer_of(h, j) * rows, rows), rows)
            pos = c * half + peer_of(h, j) * rows + lax.broadcasted_iota(jnp.int32, (rows, 1), 0)
            ok = (pos < length).astype(F32)
            for b, lo, w in blocks(d):
                block = r.cot_v[lo : lo + w, pr].astype(F32).T * ok
                r.df[1, j, :, lo : lo + w] = block.astype(BF16)
                if j == 0:
                    r.d_res[:, lo : lo + w] = block

    def clear_sums():
        @pl.loop(0, 12)
        def _(i):
            r.gown[i] = jnp.zeros((cr, ff), F32)
            r.sf[i] = jnp.zeros((cr, ff), BF16)

        r.gain_v[...] = jnp.zeros((2, 1, d), F32)

    def share(k, e, j):
        return remote(r.psend.at[k, j - 1], r.precv.at[k, j - 1], r.p_ss.at[e, j], r.p_rs.at[e, j], j)

    def summed(k, e):
        total = r.part[k].astype(F32)
        for j in (1, 2, 3):
            share(k, e, j).wait_recv()
            total = total + r.precv[k, j - 1].astype(F32)
        return total

    def sent(k, e):
        for j in (1, 2, 3):
            share(k, e, j).wait_send()

    def rms(x, gain):
        inv = lax.rsqrt(jnp.mean(x * x, axis=-1, keepdims=True) + EPS)
        return x * inv * gain

    def turned(x):
        return jnp.where(quarter, -pltpu.roll(x, 128 - HD // 2, 1), pltpu.roll(x, HD // 2, 1))

    def rope(x):
        return x * r.tab_v[:, 0:128] + turned(x) * r.tab_v[:, 128:256]

    def unrope(x):
        return x * r.tab_v[:, 0:128] - turned(x) * r.tab_v[:, 128:256]

    def swap(x):
        return pltpu.roll(x, HD, 1)

    def blocks(width):
        return [(b, b * 128, min(128, width - b * 128)) for b in range(-(-width // 128))]

    def head_row(i):
        return i // GQ, (i % GQ) * rows

    def store_t(dst, src):
        for b, lo, w in blocks(d):
            dst[lo : lo + w, :] = src[:, lo : lo + w].T

    gain_a = lambda: r.gains_v[0]
    gain_f = lambda: r.gains_v[1]

    loads.tab.wait()
    both = r.tab_v[:, 0:128]
    r.tab_v[:, 128:256] = jnp.where(quarter, pltpu.roll(both, 128 - HD // 2, 1), both)
    r.tab_v[:, 0:128] = jnp.where(quarter, both, pltpu.roll(both, HD // 2, 1))
    loads.ga.wait()
    loads.gf.wait()
    loads.hid.wait()
    for b, lo, w in blocks(d):
        r.res[0, :, lo : lo + w] = hid_v[lo : lo + w, :].astype(F32).T

    def gather(e, src, dst, by_owner=False):
        def hop(k, ref, to, j):
            return remote(ref, to, r.ag_ss.at[e, k], r.ag_rs.at[e, k], j)

        at = (lambda j, near, x: dst(near, x)) if by_owner else (lambda j, near, x: dst(j, x))
        first = [hop(0, src(0), at(1, 0, 0), 1), hop(3, src(1), at(2, 0, 1), 2), hop(1, src(1), at(1, 0, 1), 1),
                 hop(2, src(0), at(2, 0, 0), 2)]
        relay = [hop(4, dst(1, 0), at(3, 1, 0), 2), hop(5, dst(2, 1), at(3, 2, 1), 1)]
        def start():
            for cp in first:
                cp.start()

        def hand_on():
            first[0].wait_recv()
            relay[0].start()
            first[1].wait_recv()
            relay[1].start()

        def wait(j):
            for cp in ((first[2],), (first[3],), relay)[j - 1]:
                cp.wait_recv()

        def drain():
            for cp in first + relay:
                cp.wait_send()

        return SimpleNamespace(start=start, hand_on=hand_on, wait=wait, drain=drain)

    def halves(ref):
        n = ref.shape[0] // 2
        return lambda x: ref.at[pl.ds(x * n, n)]

    @pl.loop(0, 2)
    def _(p):
        x = r.res[p]
        na = rms(x, gain_a()).astype(BF16)
        store_t(r.nat.at[p], na)

        @pl.when(p == 0)
        def _():
            loads.wk.wait()
            loads.wv.wait()

        r.wide[:, : KV * HD] = nt(na, r.wk_v[...])
        r.wide[:, vlo : vlo + KV * HD] = nt(na, r.wv_v[...])
        for b in range(-(-KV // 2)):
            kb = rope(r.wide[:, b * 128 : (b + 1) * 128])
            vb = r.wide[:, vlo + b * 128 : vlo + (b + 1) * 128]
            r.kv[p, 2 * b, 0:rows, :] = jnp.where(low, kb, swap(vb)).astype(BF16)
            if 2 * b + 1 < KV:
                r.kv[p, 2 * b + 1, 0:rows, :] = jnp.where(low, swap(kb), vb).astype(BF16)

        def to_peer(j, g):
            return remote(
                r.kv.at[p, g, pl.ds(0, rows)], r.kv.at[p, g, pl.ds(j * rows, rows)],
                r.kv_ss.at[p, g], r.kv_rs.at[p, g], j,
            )

        def to_partner(j, g):
            return across(
                r.kv.at[p, g, pl.ds(j * rows, rows)], r.kv.at[p, g, pl.ds(half + j * rows, rows)],
                r.kvc_ss.at[p, g], r.kvc_rs.at[p, g],
            )

        def all_peers(g):
            span = r.kv.at[p, g, pl.ds(rows, 3 * rows)]
            return remote(span, span, r.kv_ss.at[p, g], r.kv_rs.at[p, g], 1)

        def all_partner(g):
            span = r.kv.at[p, g, pl.ds(half, half)]
            return across(span, span, r.kvc_ss.at[p, g], r.kvc_rs.at[p, g])

        for g in range(KV):
            for j in (1, 2, 3):
                to_peer(j, g).start()

            @pl.when(c == 0)
            def _():
                to_partner(0, g).start()

        def arrive(g):
            all_peers(g).wait_recv()

            @pl.when(c == 0)
            def _():
                for j in (1, 2, 3):
                    to_partner(j, g).start()

        @pl.when(p == 0)
        def _():
            fill_mask()
            loads.wq.wait()

        r.wide[:, :d] = nn(na, r.wq_v[...])
        for b, lo, w in blocks(d):
            y = rope(r.wide[:, lo : lo + 128]).astype(BF16).astype(F32) * HD ** (-0.5)
            g, o = head_row(2 * b)
            r.ql[p, g, o : o + rows, :] = jnp.where(low, y, 0.0).astype(BF16)
            if 2 * b + 1 < QH:
                g, o = head_row(2 * b + 1)
                r.ql[p, g, o : o + rows, :] = jnp.where(low, swap(y), 0.0).astype(BF16)

        arrive(0)

        @pl.loop(0, KV)
        def _(g):
            @pl.when(g < KV - 1)
            def _():
                arrive(g + 1)

            @pl.when(c == 1)
            def _():
                all_partner(g).wait_recv()

            kv = r.kv[p, g]
            for k in range(GQ):
                s = nt(r.ql[p, g, k * rows : (k + 1) * rows, :], kv)
                s = s + r.bias[...]
                m = jnp.max(s, axis=-1, keepdims=True)
                e = jnp.exp(s - m)
                t = jnp.sum(e, axis=-1, keepdims=True)
                r.lse[p] += jnp.where(lane == g * GQ + k, m + jnp.log(t), 0.0)
                r.heads[g * GQ + k] = nn((e * (1.0 / t)).astype(BF16), kv)

        mine = pl.ds(pl.multiple_of(p * rows, rows), rows)
        for g in range(KV):
            o0, o1, o2 = (r.heads[g * GQ + k] for k in range(GQ))
            r.aog[g, mine, 0:128] = jnp.where(low, 0.0, o0).astype(BF16)
            r.aog[g, mine, 128:256] = jnp.where(low, swap(o1), o2).astype(BF16)
        for b, lo, w in blocks(d):
            first = swap(r.heads[2 * b])
            both = jnp.where(low, first, r.heads[2 * b + 1]) if 2 * b + 1 < QH else first
            r.at[:, lo : lo + w] = both[:, :w].astype(BF16)

        @pl.when(p == 0)
        def _():
            loads.wo.wait()

        mid = r.res[p] + nn(r.at[...], r.wo_v[...])
        r.mid[p] = mid
        r.nf[p, 0] = rms(mid, gain_f()).astype(BF16)
        ag = gather(p, halves(r.nf.at[p, 0]), lambda j, x: halves(r.nf.at[p, j])(x))
        ag.start()

        @pl.when(p == 0)
        def _():
            loads.wg.wait()
            loads.wu.wait()
            loads.wd.wait()

        for j in range(HEADS):
            if j == 1:
                ag.hand_on()
            if j:
                ag.wait(j)
            nf = r.nf[p, j]
            gate = nn(nf, wg_v[...])
            up = nn(nf, wu_v[...])
            r.gate[p, j] = gate
            r.up[p, j] = up
            act = (gate / (1.0 + jnp.exp(-gate)) * up).astype(BF16)
            part = nt(act, wd_v[...])
            if j == 0:
                r.part[p] = part.astype(BF16)
            else:
                r.psend[p, j - 1] = part.astype(BF16)
                share(p, p, j).start()
        ag.drain()

        @pl.when(p == 0)
        def _():
            loads.cot.wait()
            fill_cotangent()
            clear_sums()
            r.res[1] = valid * (r.mid[0] + summed(0, 0))
            sent(0, 0)

        @pl.loop(0, KV)
        def _(g):
            all_peers(g).wait_send()

            @pl.when(c == 0)
            def _():
                all_partner(g).wait_send()

    def final(k, out):
        def there(j, x):
            at = pl.ds(pl.multiple_of(peer_of(h, j) * rows, rows), rows)
            return out.at[pl.ds(x * hd2, hd2), at]

        own = pltpu.make_async_copy(r.fin.at[k], out.at[:, my_rows], r.loc_sem.at[k])
        ag = gather(3 + k, halves(r.fin.at[k]), there, True)

        def put(value):
            store_t(r.fin.at[k], value.astype(BF16))
            own.start()

        return SimpleNamespace(put=put, own=own, send=ag.start, hand_on=ag.hand_on, wait=ag.wait, drain=ag.drain)

    low_side = z < nb // 2
    middle = (z == nb // 2 - 1) | (z == nb // 2)
    handed = (z > 0) & (z < nb - 1)
    inwards = jnp.where(low_side, 1, -1)

    def zcopy(src, dst, ss, rs, dz):
        return copy_to(src, dst, ss, rs, dict(batch=z + dz))

    def columns(i):
        return {15: (384, ff - 384), 16: (0, 384)}.get(i, (0, ff)) if isinstance(i, int) else (0, ff)

    def place(i):
        return min(i, 15) if isinstance(i, int) else i

    def view(ref, i):
        lo, n = columns(i)
        return ref.at[i] if n == ff else ref.at[place(i), :, pl.ds(lo, n)]

    def to_next(i):
        return zcopy(view(r.zs, i), view(r.zu, i), r.z_s0.at[i], r.z_ur.at[i], inwards)

    def to_middle(i):
        return zcopy(view(r.zs, i), view(r.zb, i), r.z_s0.at[i], r.z_br.at[i], inwards)

    def to_outer(i, src):
        return zcopy(view(src, i), view(r.zb, i), r.z_s1.at[i], r.z_br.at[i], -inwards)

    def inward(i, own):
        @pl.when(handed)
        def _():
            to_next(i).wait_recv()
            view(r.zs, i)[...] = (own() + view(r.zu, i)[...].astype(F32)).astype(BF16)

        @pl.when(jnp.logical_not(handed))
        def _():
            view(r.zs, i)[...] = own().astype(BF16)

        @pl.when(middle)
        def _():
            to_middle(i).start()

        @pl.when(jnp.logical_not(middle))
        def _():
            to_next(i).start()

    def og_view(i):
        lo, n = columns(i)
        k = place(i)
        at = r.og.at[k // 4, c, k % 4]
        return at if n == ff else at.at[:, pl.ds(lo, n)]

    def og_local(i, src):
        return pltpu.make_async_copy(view(src, i), og_view(i), r.og_loc.at[i])

    def og_across(i, src):
        return across(view(src, i), og_view(i), r.og_ss.at[i], r.og_rs.at[i])

    def ex_local(q, src):
        return pltpu.make_async_copy(src.at[12 + q, :, pl.ds(512, 128)], r.ex.at[h, c, q], r.ex_loc.at[q])

    def ex_plane(q, src, j, x):
        return copy_to(
            src.at[12 + q, :, pl.ds(512, 128)], r.ex.at[h, c, q],
            r.ex_ss.at[q, 2 * j + x], r.ex_rs.at[q, 2 * j + x], plane_id(j, x),
        )

    def ex_hand_on(q, j):
        at = r.ex.at[peer_of(h, j), c, q]
        return across(at, at, r.ex_ss.at[q, 2 * j + 1], r.ex_rs.at[q, 2 * j + 1])

    def ex_arrive(q):
        for j in (1, 2, 3):
            ex_plane(q, r.zs, j, 0).wait_send()
            ex_plane(q, r.zs, j, 0).wait_recv()
            ex_hand_on(q, j).start()

    def outward(i):
        def put(src):
            @pl.when(handed)
            def _():
                to_outer(i, src).start()

            og_local(i, src).start()
            og_across(i, src).start()
            if isinstance(i, int) and 12 <= i < 16:
                ex_local(i - 12, src).start()
                for j, x in ((3, 0), (1, 0), (2, 0), (0, 1)):
                    ex_plane(i - 12, src, j, x).start()

        to_middle(i).wait_recv()

        @pl.when(middle)
        def _():
            to_middle(i).wait_send()
            at = view(r.zs, i)
            at[...] = (at[...].astype(F32) + view(r.zb, i)[...].astype(F32)).astype(BF16)
            put(r.zs)

        @pl.when(jnp.logical_not(middle))
        def _():
            put(r.zb)

    def ffn_half(t):
        sl = pl.ds(4 * t, 4)
        return across(r.sf.at[sl], r.rf.at[sl], r.f_ss.at[t], r.f_rs.at[t])

    def ffn_piece(i):
        @pl.when(i % 4 == 0)
        def _():
            ffn_half(i // 4).wait_recv()

        inward(i, lambda: r.gown[i] + r.rf[i].astype(F32))

    def within(i, cond, do):
        if isinstance(i, int) and not 0 <= i < 17:
            return

        @pl.when((i >= 0) & (i < 17) & cond)
        def _():
            do(i)

    outer = jnp.logical_not(handed)

    def outer_pieces(lo, hi):
        @pl.when(outer)
        def _():
            pl.loop(lo, hi)(ffn_piece)

    def turn(m):
        piece = lambda i: (attention_piece if isinstance(i, int) and i >= 12 else ffn_piece)(i)
        within(m, handed, piece)
        if isinstance(m, int) and m in (9, 11, 13, 15, 16):
            within(12 + (m - 8) // 2, outer, piece)
        if not isinstance(m, int) or m <= 13:
            within(m - 2, middle, outward)
        if isinstance(m, int) and m >= 13:
            within(m - 1, middle, outward)
        within(m - 5, jnp.logical_not(middle), outward)

    def norm_bwd(x, gain, dn):
        inv = lax.rsqrt(jnp.mean(x * x, axis=-1, keepdims=True) + EPS)
        u = gain * dn
        dx = inv * u - x * (inv * inv * inv) * jnp.mean(x * u, axis=-1, keepdims=True)
        return dx, jnp.sum(dn * x * inv, axis=0, keepdims=True)

    mine_half = pl.ds(pl.multiple_of(c * hd2, hd2), hd2)
    other_half = pl.ds(pl.multiple_of((1 - c) * hd2, hd2), hd2)

    def a_half(g):
        src = r.wf.at[pl.ds(pl.multiple_of(g * hd2, hd2), hd2), pl.ds(0, 512)]
        return across(src, r.ra.at[g], r.a_ss.at[g], r.a_rs.at[g])

    def first_group(to):
        g = jnp.int32(KV - 1)
        for k in reversed(range(KV - 1)):
            g = jnp.where(r.own[k] == to, k, g)
        return g

    g1 = jnp.int32(0)
    for k in range(1, KV):
        for i in range(k):
            g1 = jnp.where(r.own[k] == r.own[i], k, g1)

    def own_share(to, i):
        lo, n = columns(i)
        q = place(i) - 12
        at = pl.ds(q * cr, cr)
        g0 = first_group(to)
        span = pl.ds(lo, min(n, 512 - lo))
        first = r.ha[g0, at, span].astype(F32) + r.ra[g0, at, span].astype(F32)
        if lo + n <= 512:
            return first
        cols = pl.ds(pl.multiple_of(to * 128, 128), 128)
        second = r.ha[g1, at, cols].astype(F32) + r.ra[g1, at, cols].astype(F32)
        return jnp.concatenate([first, second], axis=1)

    def share_slot(ref, j, i):
        lo, n = columns(i)
        return ref.at[4 * (j - 1) + place(i) - 12, :, pl.ds(lo, n)]

    def head_share(j, i):
        return remote(share_slot(r.sf, j, i), share_slot(r.rf2, j, i), r.h_ss.at[j, i - 12], r.h_rs.at[j, i - 12], j)

    def attention_sums():
        @pl.loop(0, KV)
        def _(g):
            def product(rows_of):
                first = nn(jnp.concatenate([r.nat[0, rows_of, :], r.nat[1, rows_of, :]], axis=1), r.dpg[g])
                second = nn(jnp.concatenate([r.dat[0, rows_of, :], r.dat[1, rows_of, :]], axis=1), r.aog[g])
                return first[:, :256], first[:, 256:] + second[:, :128], second[:, 128:]

            def put(dst, parts):
                dst[:, 0:256] = parts[0].astype(BF16)
                dst[:, 256:384] = parts[1].astype(BF16)
                dst[:, 384:512] = parts[2].astype(BF16)

            put(r.wf.at[pl.ds(pl.multiple_of(g * hd2, hd2), hd2)], product(other_half))
            a_half(g).start()
            put(r.ha.at[g], product(mine_half))

            @pl.when(g % 3 == 1)
            def _():
                turn(KV + g // 3)

        @pl.loop(0, KV)
        def _(g):
            a_half(g).wait_recv()

        for t in range(3):
            ffn_half(t).wait_send()
        for i in range(12, 17):
            for j in (3, 1, 2):
                share_slot(r.sf, j, i)[...] = own_share(peer_of(h, j), i).astype(BF16)
                head_share(j, i).start()
        turn(KV + 2)

    def attention_piece(i):
        def own():
            v = own_share(h, i)
            for j in (1, 2, 3):
                head_share(j, i).wait_recv()
                v = v + share_slot(r.rf2, j, i)[...].astype(F32)
            return v

        inward(i, own)

    @pl.loop(0, 2)
    def _(back):
        p = 1 - back
        ag = gather(2, halves(r.df.at[0, 0]), lambda j, x: halves(r.df.at[0, j])(x))

        @pl.when(p == 0)
        def _():
            block = r.d_res[...] * valid
            r.d_res[...] = block
            r.df[0, 0] = block.astype(BF16)
            ag.start()

        for j in range(HEADS):
            if j:
                @pl.when(p == 0)
                def _():
                    if j == 1:
                        ag.hand_on()
                    ag.wait(j)

            d_act = nn(r.df[p, j], wd_v[...])
            gate, up = r.gate[p, j], r.up[p, j]
            s = 1.0 / (1.0 + jnp.exp(-gate))
            dg = (d_act * up * s * (1.0 + gate * (1.0 - s))).astype(BF16)
            du = (d_act * (gate * s)).astype(BF16)
            r.act[j] = (gate * s * up).astype(BF16)
            r.dg[j] = dg
            r.du[j] = du
            part = nt(dg, wg_v[...]) + nt(du, wu_v[...])
            if j == 0:
                r.part[1 - p] = part.astype(BF16)
            else:
                r.psend[1 - p, j - 1] = part.astype(BF16)
                share(1 - p, 3 - p, j).start()
        for t, rhs in ((0, r.dg), (1, r.du), (2, r.act)):
            if t != 1:
                src = r.nf if t == 0 else r.df
                for j in range(HEADS):
                    store_t(lhs.at[:, j * rows : (j + 1) * rows], src[p, j])
            right = rhs[...].reshape(half, ff)
            theirs = nn(lhs[other_half, :], right)
            for q in range(4):
                v = theirs[q * cr : (q + 1) * cr] + r.sf[4 * t + q].astype(F32)
                r.sf[4 * t + q] = v.astype(BF16)

            @pl.when(p == 0)
            def _():
                ffn_half(t).start()

            ours = nn(lhs[mine_half, :], right)
            for q in range(4):
                r.gown[4 * t + q] += ours[q * cr : (q + 1) * cr]

        @pl.when(p == 0)
        def _():
            outer_pieces(0, 8)

        @pl.when(p == 1)
        def _():
            final(0, r.out).put(valid * (r.mid[1] + summed(1, 1)))
            final(0, r.out).send()
            sent(1, 1)

        dn = summed(1 - p, 3 - p)
        dx, dgain = norm_bwd(r.mid[p], gain_f(), dn)
        d_mid = r.d_res[...] + dx
        r.d_mid[...] = d_mid
        r.gain_v[1] += dgain
        da = d_mid.astype(BF16)
        store_t(r.dat.at[p], da)
        r.wide[:, :d] = nt(da, r.wo_v[...])
        for b, lo, w in blocks(d):
            y = r.wide[:, lo : lo + 128]
            g, o = head_row(2 * b)
            r.ou[g, o : o + rows, :] = jnp.where(low, 0.0, swap(y)).astype(BF16)
            if 2 * b + 1 < QH:
                g, o = head_row(2 * b + 1)
                r.ou[g, o : o + rows, :] = jnp.where(low, 0.0, y).astype(BF16)

        def hop(g):
            return across(r.dkv_ctx.at[g], r.dkv_ctx_r.at[p, g], r.dc_ss.at[p, g], r.dc_rs.at[p, g])

        def to_owner(j, g):
            return remote(
                r.dkv_s.at[g, j - 1], r.dkv_r.at[g, j - 1], r.dkv_ss.at[p, g], r.dkv_rs.at[p, g], j
            )

        def all_owners(g):
            return remote(r.dkv_s.at[g], r.dkv_r.at[g], r.dkv_ss.at[p, g], r.dkv_rs.at[p, g], 1)

        def pass_on(g):
            @pl.when(c == 0)
            def _():
                hop(g).wait_recv()
                r.dkv[g] += r.dkv_ctx_r[p, g].astype(F32)

            for j in (1, 2, 3):
                r.dkv_s[g, j - 1] = r.dkv[g, :, j * rows : (j + 1) * rows].astype(BF16)
                to_owner(j, g).start()

        @pl.loop(0, KV)
        def _(g):
            kv = r.kv[p, g]
            acc = None
            for k in range(GQ):
                q = r.ql[p, g, k * rows : (k + 1) * rows, :]
                o = r.ou[g, k * rows : (k + 1) * rows, :]
                s = nt(q, kv)
                s = s + r.bias[...]
                lse = jnp.sum(jnp.where(lane == g * GQ + k, r.lse[p], 0.0), axis=-1, keepdims=True)
                pr = jnp.exp(s - lse)
                dpr = nt(o, kv)
                delta = jnp.sum(pr * dpr, axis=-1, keepdims=True)
                ds = (pr * (dpr - delta)).astype(BF16)
                r.heads[g * GQ + k] = unrope(nn(ds, kv) * HD ** (-0.5))
                t = nn(o.T, pr.astype(BF16)) + nn(q.T, ds)
                acc = t if acc is None else acc + t
            r.dkv[g] = acc[:, :half]
            r.dkv_ctx[g] = acc[:, half:].astype(BF16)

            @pl.when(c == 1)
            def _():
                hop(g).start()

            @pl.when(g > 0)
            def _():
                pass_on(g - 1)

            @pl.when((p == 0) & (g == 0))
            def _():
                outer_pieces(8, 12)

            @pl.when((p == 0) & (g > 0))
            def _():
                turn(g - 1)

        pass_on(KV - 1)
        mine = pl.ds(pl.multiple_of(p * rows, rows), rows)
        for b, lo, w in blocks(d):
            y = r.heads[2 * b]
            if 2 * b + 1 < QH:
                y = jnp.where(low, y, swap(r.heads[2 * b + 1]))
            r.at[:, lo : lo + w] = y[:, :w].astype(BF16)
        for g in range(KV):
            both = jnp.where(low, r.heads[g * GQ], swap(r.heads[g * GQ + 1]))
            r.dpg[g, mine, 0:128] = both.astype(BF16)

        r.wide[:, :d] = nt(r.at[...], r.wq_v[...])

        @pl.when(p == 0)
        def _():
            turn(KV - 1)

        keys, vals = [], []
        for g in range(KV):
            t = r.dkv[g, :, 0:rows]
            all_owners(g).wait_recv()
            for j in range(3):
                t = t + r.dkv_r[g, j].astype(F32)
            t = t.T
            kt, vt = unrope(t), swap(t)
            keys.append(kt)
            vals.append(t)
            r.dpg[g, mine, 128:256] = jnp.where(low, r.heads[g * GQ + 2], swap(kt)).astype(BF16)
            r.dpg[g, mine, 256:384] = jnp.where(low, vt, 0.0).astype(BF16)
        for b, lo, w in blocks(KV * HD):
            kb, vb = keys[2 * b], swap(vals[2 * b])
            if 2 * b + 1 < KV:
                kb = jnp.where(low, kb, swap(keys[2 * b + 1]))
                vb = jnp.where(low, vb, vals[2 * b + 1])
            r.dk[:, lo : lo + w] = kb[:, :w].astype(BF16)
            r.dv[:, lo : lo + w] = vb[:, :w].astype(BF16)
        @pl.when(p == 0)
        def _():
            attention_sums()

        dna = r.wide[:, :d] + nn(r.dk[...], r.wk_v[...]) + nn(r.dv[...], r.wv_v[...])
        dx, dgain = norm_bwd(r.res[p], gain_a(), dna)
        r.d_res[...] = r.d_mid[...] + dx
        r.gain_v[0] += dgain
        sent(1 - p, 3 - p)

        @pl.when(p == 0)
        def _():
            ag.drain()

        @pl.when(p == 1)
        def _():
            final(0, r.out).hand_on()


        @pl.loop(0, KV)
        def _(g):
            all_owners(g).wait_send()

            @pl.when(c == 1)
            def _():
                hop(g).wait_send()

    final(1, r.gin).put(r.d_res[...])

    me = 2 * h + c
    r.gain_p[me] = r.gain_v[...]
    gp = [copy_to(r.gain_p.at[me], r.gain_p.at[me], r.gp_ss.at[2 * j + x], r.gp_rs.at[2 * j + x], plane_id(j, x))
          for j, x in plane]
    for cp in gp:
        cp.start()

    for cp in gp:
        cp.wait_recv()
    total = r.gain_p[0]
    for k in range(1, 2 * HEADS):
        total = total + r.gain_p[k]
    r.gain_z[z] = total
    gz = [copy_to(r.gain_z.at[z], r.gain_z.at[z], r.gz_ss.at[k], r.gz_rs.at[k], dict(batch=(z + k) % nb))
          for k in range(1, nb)]
    for cp in gz:
        cp.start()

    for m in range(KV + 3, 22):
        turn(m)
        if m == 15:
            final(1, r.gin).send()
        if m == 18:
            final(1, r.gin).hand_on()

    for cp in gz:
        cp.wait_recv()
    total = r.gain_z[0]
    for k in range(1, nb):
        total = total + r.gain_z[k]
    r.gain_v[...] = total
    gains_out = pltpu.make_async_copy(r.gain_v, r.gains_out, r.loc_sem.at[2])
    gains_out.start()

    for q in range(4):
        ex_arrive(q)

    gains_out.wait()
    for cp in gp + gz:
        cp.wait_send()
    for j in (1, 2, 3):
        for i in range(12, 17):
            head_share(j, i).wait_send()

    @pl.loop(0, KV)
    def _(g):
        a_half(g).wait_send()

    def settle(i):
        og_local(i, r.zs).wait()
        og_across(i, r.zs).wait_send()
        og_across(i, r.zs).wait_recv()

        @pl.when(jnp.logical_not(middle))
        def _():
            to_next(i).wait_send()

        @pl.when(handed)
        def _():
            to_outer(i, r.zs).wait_send()

    pl.loop(0, 12)(settle)
    for i in range(12, 17):
        settle(i)

    for q in range(4):
        ex_local(q, r.zs).wait()
        ex_plane(q, r.zs, 0, 1).wait()
        for j in (1, 2, 3):
            ex_hand_on(q, j).wait()
    for k, out in ((0, r.out), (1, r.gin)):
        end = final(k, out)
        end.own.wait()
        for j in (1, 2, 3):
            end.wait(j)
        end.drain()


def put_kernel(own, o, gin, og, ex, ga, gf, o_out, gin_out, gq, gk, gv, go, gg, gu, gd, ga_out, gf_out):
    h = lax.axis_index("head")
    held = jnp.int32(0)
    for k in range(KV):
        held = held + jnp.where(own[k] == h, 1, 0)
    gw = GQ * HD
    o_out[...] = o[...]
    gin_out[...] = gin[...].astype(F32)
    gg[...] = og[0].astype(F32)
    gu[...] = og[1].astype(F32)
    gd[...] = og[2].astype(F32)
    ga_out[...] = ga[...]
    gf_out[...] = gf[...]
    first = og[3, :, 0:512].astype(F32)
    second = jnp.concatenate([ex[k].astype(F32) for k in range(HEADS)], axis=1)
    second = jnp.where(held > 1, second, 0.0)
    for out, lo, width in ((gq, 0, gw), (gk, gw, HD), (gv, gw + HD, HD), (go, gw + 2 * HD, gw)):
        out[...] = jnp.concatenate([first[:, lo : lo + width], second[:, lo : lo + width]], axis=1)


def body(nb, hidden_in, cotangent, lengths, owners, w_query, w_key, w_value, w_output, gate_weight, up_weight, down_weight,
         gain_attn, gain_ffn):
    half, d = hidden_in.shape[1:]
    ff = gate_weight.shape[1]
    rows = half // HEADS
    cr = d // 8
    scratch = scratch_of(rows, d, ff, nb)
    anyspec = pl.BlockSpec(memory_space=pl.ANY)
    smem = pl.BlockSpec(memory_space=pltpu.SMEM)
    sd = jax.ShapeDtypeStruct
    ins = dict(
        hid=anyspec, cot=anyspec, len=smem, own=smem, ga=anyspec, gf=anyspec, tab=anyspec,
        wq=anyspec, wk=anyspec, wv=anyspec, wo=anyspec, wg=anyspec, wu=anyspec, wd=anyspec,
    )
    outs = dict(
        out=sd((d, half), BF16), gin=sd((d, half), BF16),
        og=sd((4, 2, 4, cr, ff), BF16), ex=sd((HEADS, 2, 4, cr, 128), BF16), gains_out=sd((2, 1, d), F32),
    )
    names = tuple(ins) + tuple(outs) + tuple(scratch)
    o, gin, og, ex, gains = pl.pallas_call(
        functools.partial(step_kernel, names, rows, d, ff, nb),
        out_shape=tuple(outs.values()),
        in_specs=list(ins.values()),
        out_specs=(anyspec,) * len(outs),
        scratch_shapes=list(scratch.values()),
        compiler_params=pltpu.CompilerParams(
            collective_id=0, has_side_effects=True, vmem_limit_bytes=67043328
        ),
    )(
        hidden_in[0].T, cotangent[0].T, lengths, owners, gain_attn[None], gain_ffn[None],
        jnp.asarray(rope_table(2 * half)), w_query, w_key.T, w_value.T, w_output, gate_weight, up_weight, down_weight.T,
    )
    gw, block = GQ * HD, lambda *shape: (lambda index: pl.BlockSpec(shape, index))
    rowwise = lambda width: block(cr, width)(lambda i: (i, 0))
    gains_spec = lambda k: block(None, 1, d)(lambda i: (k, 0, 0))
    gain_out = block(1, d)(lambda i: (0, 0))
    o, gin, gq, gk, gv, go, gg, gu, gd, ga, gf = pl.pallas_call(
        put_kernel,
        grid=(8,),
        out_shape=(
            sd((d, half), BF16), sd((d, half), F32), sd((d, 2 * gw), F32), sd((d, 2 * HD), F32), sd((d, 2 * HD), F32),
            sd((d, 2 * gw), F32), sd((d, ff), F32), sd((d, ff), F32), sd((d, ff), F32), sd((1, d), F32), sd((1, d), F32),
        ),
        in_specs=[
            smem, rowwise(half), rowwise(half), block(4, None, None, cr, ff)(lambda i: (0, i // 4, i % 4, 0, 0)),
            block(HEADS, None, None, cr, 128)(lambda i: (0, i // 4, i % 4, 0, 0)), gains_spec(0), gains_spec(1),
        ],
        out_specs=(
            rowwise(half), rowwise(half), rowwise(2 * gw), rowwise(2 * HD), rowwise(2 * HD), rowwise(2 * gw),
            rowwise(ff), rowwise(ff), rowwise(ff), gain_out, gain_out,
        ),
    )(owners, o, gin, og, ex, gains, gains)
    return o.T[None], gin.T[None], gq, gk, gv, go.T, gg, gu, gd.T, ga[0], gf[0]


def solution(mesh):
    rep = P()
    io = P("batch", "ctx", None)
    in_specs = (io, io, P("batch"), rep, rep, rep, rep, rep, P(None, "head"), P(None, "head"), P("head", None), rep, rep)
    out_specs = (io, io, P(None, "head"), P(None, "head"), P(None, "head"), P("head", None), P(None, "head"),
                 P(None, "head"), P("head", None), rep, rep)
    return jax.shard_map(
        functools.partial(body, mesh.shape["batch"]), mesh=mesh, in_specs=in_specs, out_specs=out_specs, check_vma=False
    )
```

```python
import functools
import math
from types import SimpleNamespace

import jax
import jax.numpy as jnp
import numpy as np
from jax import lax
from jax.experimental import pallas as pl
from jax.experimental.pallas import tpu as pltpu
from jax.sharding import PartitionSpec as P

KV = 5
HD = 64
GQ = 3
QH = KV * GQ
HEADS = 4
EPS = 1e-05
NEG = -1e30
MESH = pl.DeviceIdType.MESH
F32 = jnp.float32
BF16 = jnp.bfloat16


def nn(a, b):
    return lax.dot_general(a, b, (((1,), (0,)), ((), ())), preferred_element_type=F32)


def nt(a, b):
    return lax.dot_general(a, b, (((1,), (1,)), ((), ())), preferred_element_type=F32)


def tn(a, b):
    return lax.dot_general(a, b, (((0,), (0,)), ((), ())), preferred_element_type=F32)


def rope_table(slots):
    inverse = np.exp(np.arange(HD // 2, dtype=np.float32) * np.float32(-2.0 * math.log(10000.0) / HD))
    angles = np.arange(slots, dtype=np.float32)[:, None] * inverse[None, :].astype(np.float32)
    cos, sin = np.cos(angles).astype(np.float32), np.sin(angles).astype(np.float32)
    return np.concatenate([cos, sin] * 2, axis=1)


def peer_of(h, j):
    return (h, h + 1 - 2 * (h % 2), (h + 2) % 4, 3 - h)[j]


def scratch_of(rows, d, ff, nb):
    n = HEADS
    half = n * rows
    keys = 2 * half
    dp = -(-d // 128) * 128
    cr = d // 8
    v = pltpu.VMEM
    dma = pltpu.SemaphoreType.DMA
    return dict(
        cot_v=v((d, half), BF16),
        tab_v=v((rows, 256), F32),
        gains_v=v((2, 1, d), F32),
        wq_v=v((d, QH * HD), BF16),
        wk_v=v((KV * HD, d), BF16),
        wv_v=v((KV * HD, d), BF16),
        wo_v=v((QH * HD, d), BF16),
        wf=v((3 * d, ff), BF16),
        res=v((2, rows, d), F32),
        mid=v((2, rows, d), F32),
        nat=v((2, d, rows), BF16),
        dat=v((2, d, rows), BF16),
        ql=v((2, KV, GQ * rows, 128), BF16),
        kv=v((2, KV, keys, 128), BF16),
        lse=v((2, rows, 128), F32),
        at=v((rows, d), BF16),
        nf=v((2, n, rows, d), BF16),
        gate=v((2, n, rows, ff), F32),
        up=v((2, n, rows, ff), F32),
        act=v((n, rows, ff), BF16),
        bias=v((rows, keys), F32),
        wide=v((rows, dp), F32),
        heads=v((QH, rows, 128), F32),
        part=v((2, rows, d), BF16),
        psend=v((2, 3, rows, d), BF16),
        precv=v((2, 3, rows, d), BF16),
        d_res=v((rows, d), F32),
        d_mid=v((rows, d), F32),
        df=v((2, n, rows, d), BF16),
        dg=v((n, rows, ff), BF16),
        du=v((n, rows, ff), BF16),
        ou=v((KV, GQ * rows, 128), BF16),
        dk=v((rows, KV * HD), BF16),
        dv=v((rows, KV * HD), BF16),
        dpg=v((KV, 2 * rows, 384), BF16),
        aog=v((KV, 2 * rows, 256), BF16),
        dkv=v((KV, 128, half), F32),
        dkv_ctx=v((KV, 128, half), BF16),
        dkv_ctx_r=v((2, KV, 128, half), BF16),
        dkv_s=v((KV, 3, 128, rows), BF16),
        dkv_r=v((KV, 3, 128, rows), BF16),
        fin=v((2, d, rows), BF16),
        gown=v((12, cr, ff), F32),
        sf=v((12, cr, ff), BF16),
        rf=v((12, cr, ff), BF16),
        rf2=v((12, cr, ff), BF16),
        zs=v((16, cr, ff), BF16),
        zu=v((16, cr, ff), BF16),
        zb=v((16, cr, ff), BF16),
        ha=v((KV, d // 2, 512), BF16),
        ra=v((KV, d // 2, 512), BF16),
        gain_v=v((2, 1, d), F32),
        gain_p=v((2 * n, 2, 1, d), F32),
        gain_z=v((nb, 2, 1, d), F32),
        in_sem=dma((12,)),
        loc_sem=dma((8,)),
        kv_ss=dma((2, KV)),
        kv_rs=dma((2, KV)),
        kvc_ss=dma((2, KV)),
        kvc_rs=dma((2, KV)),
        ag_ss=dma((5, 6)),
        ag_rs=dma((5, 6)),
        p_ss=dma((4, 4)),
        p_rs=dma((4, 4)),
        dc_ss=dma((2, KV)),
        dc_rs=dma((2, KV)),
        dkv_ss=dma((2, KV)),
        dkv_rs=dma((2, KV)),
        f_ss=dma((3,)),
        f_rs=dma((3,)),
        z_s0=dma((17,)),
        z_s1=dma((17,)),
        z_ur=dma((17,)),
        z_br=dma((17,)),
        og_loc=dma((17,)),
        og_ss=dma((17,)),
        og_rs=dma((17,)),
        a_ss=dma((KV,)),
        a_rs=dma((KV,)),
        h_ss=dma((4, 5)),
        h_rs=dma((4, 5)),
        ex_loc=dma((4,)),
        ex_ss=dma((4, 8)),
        ex_rs=dma((4, 8)),
        gp_ss=dma((8,)),
        gp_rs=dma((8,)),
        gz_ss=dma((nb,)),
        gz_rs=dma((nb,)),
    )


def step_kernel(names, rows, d, ff, nb, *refs):
    r = SimpleNamespace(**dict(zip(names, refs)))
    wg_v, wu_v, wd_v = (r.wf.at[pl.ds(t * d, d)] for t in range(3))
    lhs, hid_v = r.cot_v, r.fin.at[1]
    h = lax.axis_index("head")
    c = lax.axis_index("ctx")
    z = lax.axis_index("batch")
    half = HEADS * rows
    hd2 = d // 2
    cr = d // 8
    lane = lax.broadcasted_iota(jnp.int32, (rows, 128), 1)
    low = lane < HD
    quarter = (lane % HD) < HD // 2

    def copy_to(src, dst, ss, rs, where):
        return pltpu.make_async_remote_copy(
            src_ref=src, dst_ref=dst, send_sem=ss, recv_sem=rs, device_id=where, device_id_type=MESH
        )

    def remote(src, dst, ss, rs, j):
        return copy_to(src, dst, ss, rs, dict(head=peer_of(h, j)))

    def across(src, dst, ss, rs):
        return copy_to(src, dst, ss, rs, dict(ctx=1 - c))

    def load(k, src, dst):
        return pltpu.make_async_copy(src, dst, r.in_sem.at[k])

    my_rows = pl.ds(pl.multiple_of(h * rows, rows), rows)
    my_pos = pl.ds(pl.multiple_of(c * half + h * rows, rows), rows)
    loads = SimpleNamespace(
        hid=load(0, r.hid.at[:, my_rows], hid_v),
        ga=load(1, r.ga, r.gains_v.at[0]),
        gf=load(11, r.gf, r.gains_v.at[1]),
        wk=load(3, r.wk, r.wk_v),
        wv=load(4, r.wv, r.wv_v),
        tab=load(5, r.tab.at[my_pos], r.tab_v.at[:, pl.ds(0, 128)]),
        wq=load(2, r.wq, r.wq_v),
        wo=load(6, r.wo, r.wo_v),
        wg=load(7, r.wg, wg_v),
        wu=load(8, r.wu, wu_v),
        wd=load(9, r.wd, wd_v),
        cot=load(10, r.cot, r.cot_v),
    )
    for cp in vars(loads).values():
        cp.start()

    plane = [(j, x) for j in range(HEADS) for x in range(2) if (j, x) != (0, 0)]

    def plane_id(j, x):
        return dict(head=peer_of(h, j), ctx=1 - c if x else c)

    barrier = pltpu.get_barrier_semaphore()
    for j, x in plane:
        pl.semaphore_signal(barrier, inc=1, device_id=plane_id(j, x), device_id_type=MESH)
    for k in range(1, nb):
        pl.semaphore_signal(barrier, inc=1, device_id=dict(batch=(z + k) % nb), device_id_type=MESH)
    pl.semaphore_wait(barrier, len(plane) + nb - 1)

    length = r.len[0]
    row_pos = c * half + h * rows + lax.broadcasted_iota(jnp.int32, (rows, 1), 0)
    valid = (row_pos < length).astype(F32)

    zero_w = jnp.zeros((rows, 128), F32)
    r.wide[...] = jnp.zeros(r.wide.shape, F32)
    vlo = r.wide.shape[1] // 2
    r.lse[0] = zero_w
    r.lse[1] = zero_w

    @pl.when(c == 0)
    def _():
        for p in range(2):
            r.kv[p, :, half:, :] = jnp.zeros((KV, half, 128), BF16)

    def fill_mask():
        for blk in range(2 * HEADS):
            own = blk < HEADS
            base = (c if own else 1 - c) * half + peer_of(h, blk % HEADS) * rows
            kp = base + lax.broadcasted_iota(jnp.int32, (rows, rows), 1)
            qp = c * half + h * rows + lax.broadcasted_iota(jnp.int32, (rows, rows), 0)
            ok = (kp <= qp) & (kp < length)
            r.bias[:, blk * rows : (blk + 1) * rows] = jnp.where(ok, 0.0, NEG)

    def fill_cotangent():
        for j in range(HEADS):
            pr = pl.ds(pl.multiple_of(peer_of(h, j) * rows, rows), rows)
            pos = c * half + peer_of(h, j) * rows + lax.broadcasted_iota(jnp.int32, (rows, 1), 0)
            ok = (pos < length).astype(F32)
            for b, lo, w in blocks(d):
                block = r.cot_v[lo : lo + w, pr].astype(F32).T * ok
                r.df[1, j, :, lo : lo + w] = block.astype(BF16)
                if j == 0:
                    r.d_res[:, lo : lo + w] = block

    def clear_sums():
        @pl.loop(0, 12)
        def _(i):
            r.gown[i] = jnp.zeros((cr, ff), F32)
            r.sf[i] = jnp.zeros((cr, ff), BF16)

        r.gain_v[...] = jnp.zeros((2, 1, d), F32)

    def share(k, e, j):
        return remote(r.psend.at[k, j - 1], r.precv.at[k, j - 1], r.p_ss.at[e, j], r.p_rs.at[e, j], j)

    def summed(k, e):
        total = r.part[k].astype(F32)
        for j in (1, 2, 3):
            share(k, e, j).wait_recv()
            total = total + r.precv[k, j - 1].astype(F32)
        return total

    def sent(k, e):
        for j in (1, 2, 3):
            share(k, e, j).wait_send()

    def rms(x, gain):
        inv = lax.rsqrt(jnp.mean(x * x, axis=-1, keepdims=True) + EPS)
        return x * inv * gain

    def turned(x):
        return jnp.where(quarter, -pltpu.roll(x, 128 - HD // 2, 1), pltpu.roll(x, HD // 2, 1))

    def rope(x):
        return x * r.tab_v[:, 0:128] + turned(x) * r.tab_v[:, 128:256]

    def unrope(x):
        return x * r.tab_v[:, 0:128] - turned(x) * r.tab_v[:, 128:256]

    def swap(x):
        return pltpu.roll(x, HD, 1)

    def blocks(width):
        return [(b, b * 128, min(128, width - b * 128)) for b in range(-(-width // 128))]

    def head_row(i):
        return i // GQ, (i % GQ) * rows

    def store_t(dst, src):
        for b, lo, w in blocks(d):
            dst[lo : lo + w, :] = src[:, lo : lo + w].T

    gain_a = lambda: r.gains_v[0]
    gain_f = lambda: r.gains_v[1]

    loads.tab.wait()
    both = r.tab_v[:, 0:128]
    r.tab_v[:, 128:256] = jnp.where(quarter, pltpu.roll(both, 128 - HD // 2, 1), both)
    r.tab_v[:, 0:128] = jnp.where(quarter, both, pltpu.roll(both, HD // 2, 1))
    loads.ga.wait()
    loads.gf.wait()
    loads.hid.wait()
    for b, lo, w in blocks(d):
        r.res[0, :, lo : lo + w] = hid_v[lo : lo + w, :].astype(F32).T

    def gather(e, src, dst, by_owner=False):
        def hop(k, ref, to, j):
            return remote(ref, to, r.ag_ss.at[e, k], r.ag_rs.at[e, k], j)

        at = (lambda j, near, x: dst(near, x)) if by_owner else (lambda j, near, x: dst(j, x))
        first = [hop(0, src(0), at(1, 0, 0), 1), hop(3, src(1), at(2, 0, 1), 2), hop(1, src(1), at(1, 0, 1), 1),
                 hop(2, src(0), at(2, 0, 0), 2)]
        relay = [hop(4, dst(1, 0), at(3, 1, 0), 2), hop(5, dst(2, 1), at(3, 2, 1), 1)]
        def start():
            for cp in first:
                cp.start()

        def hand_on():
            first[0].wait_recv()
            relay[0].start()
            first[1].wait_recv()
            relay[1].start()

        def wait(j):
            for cp in ((first[2],), (first[3],), relay)[j - 1]:
                cp.wait_recv()

        def drain():
            for cp in first + relay:
                cp.wait_send()

        return SimpleNamespace(start=start, hand_on=hand_on, wait=wait, drain=drain)

    def halves(ref):
        n = ref.shape[0] // 2
        return lambda x: ref.at[pl.ds(x * n, n)]

    @pl.loop(0, 2)
    def _(p):
        x = r.res[p]
        na = rms(x, gain_a()).astype(BF16)
        store_t(r.nat.at[p], na)

        @pl.when(p == 0)
        def _():
            loads.wk.wait()
            loads.wv.wait()

        r.wide[:, : KV * HD] = nt(na, r.wk_v[...])
        r.wide[:, vlo : vlo + KV * HD] = nt(na, r.wv_v[...])
        for b in range(-(-KV // 2)):
            kb = rope(r.wide[:, b * 128 : (b + 1) * 128])
            vb = r.wide[:, vlo + b * 128 : vlo + (b + 1) * 128]
            r.kv[p, 2 * b, 0:rows, :] = jnp.where(low, kb, swap(vb)).astype(BF16)
            if 2 * b + 1 < KV:
                r.kv[p, 2 * b + 1, 0:rows, :] = jnp.where(low, swap(kb), vb).astype(BF16)

        def to_peer(j, g):
            return remote(
                r.kv.at[p, g, pl.ds(0, rows)], r.kv.at[p, g, pl.ds(j * rows, rows)],
                r.kv_ss.at[p, g], r.kv_rs.at[p, g], j,
            )

        def to_partner(j, g):
            return across(
                r.kv.at[p, g, pl.ds(j * rows, rows)], r.kv.at[p, g, pl.ds(half + j * rows, rows)],
                r.kvc_ss.at[p, g], r.kvc_rs.at[p, g],
            )

        def all_peers(g):
            span = r.kv.at[p, g, pl.ds(rows, 3 * rows)]
            return remote(span, span, r.kv_ss.at[p, g], r.kv_rs.at[p, g], 1)

        def all_partner(g):
            span = r.kv.at[p, g, pl.ds(half, half)]
            return across(span, span, r.kvc_ss.at[p, g], r.kvc_rs.at[p, g])

        for g in range(KV):
            for j in (1, 2, 3):
                to_peer(j, g).start()

            @pl.when(c == 0)
            def _():
                to_partner(0, g).start()

        def arrive(g):
            all_peers(g).wait_recv()

            @pl.when(c == 0)
            def _():
                for j in (1, 2, 3):
                    to_partner(j, g).start()

        @pl.when(p == 0)
        def _():
            fill_mask()
            loads.wq.wait()

        r.wide[:, :d] = nn(na, r.wq_v[...])
        for b, lo, w in blocks(d):
            y = rope(r.wide[:, lo : lo + 128]).astype(BF16).astype(F32) * HD ** (-0.5)
            g, o = head_row(2 * b)
            r.ql[p, g, o : o + rows, :] = jnp.where(low, y, 0.0).astype(BF16)
            if 2 * b + 1 < QH:
                g, o = head_row(2 * b + 1)
                r.ql[p, g, o : o + rows, :] = jnp.where(low, swap(y), 0.0).astype(BF16)

        arrive(0)

        @pl.loop(0, KV)
        def _(g):
            @pl.when(g < KV - 1)
            def _():
                arrive(g + 1)

            @pl.when(c == 1)
            def _():
                all_partner(g).wait_recv()

            kv = r.kv[p, g]
            for k in range(GQ):
                s = nt(r.ql[p, g, k * rows : (k + 1) * rows, :], kv)
                s = s + r.bias[...]
                m = jnp.max(s, axis=-1, keepdims=True)
                e = jnp.exp(s - m)
                t = jnp.sum(e, axis=-1, keepdims=True)
                r.lse[p] += jnp.where(lane == g * GQ + k, m + jnp.log(t), 0.0)
                r.heads[g * GQ + k] = nn((e * (1.0 / t)).astype(BF16), kv)

        mine = pl.ds(pl.multiple_of(p * rows, rows), rows)
        for g in range(KV):
            o0, o1, o2 = (r.heads[g * GQ + k] for k in range(GQ))
            r.aog[g, mine, 0:128] = jnp.where(low, 0.0, o0).astype(BF16)
            r.aog[g, mine, 128:256] = jnp.where(low, swap(o1), o2).astype(BF16)
        for b, lo, w in blocks(d):
            first = swap(r.heads[2 * b])
            both = jnp.where(low, first, r.heads[2 * b + 1]) if 2 * b + 1 < QH else first
            r.at[:, lo : lo + w] = both[:, :w].astype(BF16)

        @pl.when(p == 0)
        def _():
            loads.wo.wait()

        mid = r.res[p] + nn(r.at[...], r.wo_v[...])
        r.mid[p] = mid
        r.nf[p, 0] = rms(mid, gain_f()).astype(BF16)
        ag = gather(p, halves(r.nf.at[p, 0]), lambda j, x: halves(r.nf.at[p, j])(x))
        ag.start()

        @pl.when(p == 0)
        def _():
            loads.wg.wait()
            loads.wu.wait()
            loads.wd.wait()

        for j in range(HEADS):
            if j == 1:
                ag.hand_on()
            if j:
                ag.wait(j)
            nf = r.nf[p, j]
            gate = nn(nf, wg_v[...])
            up = nn(nf, wu_v[...])
            r.gate[p, j] = gate
            r.up[p, j] = up
            act = (gate / (1.0 + jnp.exp(-gate)) * up).astype(BF16)
            part = nt(act, wd_v[...])
            if j == 0:
                r.part[p] = part.astype(BF16)
            else:
                r.psend[p, j - 1] = part.astype(BF16)
                share(p, p, j).start()
        ag.drain()

        @pl.when(p == 0)
        def _():
            loads.cot.wait()
            fill_cotangent()
            clear_sums()
            r.res[1] = valid * (r.mid[0] + summed(0, 0))
            sent(0, 0)

        @pl.loop(0, KV)
        def _(g):
            all_peers(g).wait_send()

            @pl.when(c == 0)
            def _():
                all_partner(g).wait_send()

    def final(k, out):
        def there(j, x):
            at = pl.ds(pl.multiple_of(peer_of(h, j) * rows, rows), rows)
            return out.at[pl.ds(x * hd2, hd2), at]

        own = pltpu.make_async_copy(r.fin.at[k], out.at[:, my_rows], r.loc_sem.at[k])
        ag = gather(3 + k, halves(r.fin.at[k]), there, True)

        def put(value):
            store_t(r.fin.at[k], value.astype(BF16))
            own.start()

        return SimpleNamespace(put=put, own=own, send=ag.start, hand_on=ag.hand_on, wait=ag.wait, drain=ag.drain)

    low_side = z < nb // 2
    middle = (z == nb // 2 - 1) | (z == nb // 2)
    handed = (z > 0) & (z < nb - 1)
    inwards = jnp.where(low_side, 1, -1)

    def zcopy(src, dst, ss, rs, dz):
        return copy_to(src, dst, ss, rs, dict(batch=z + dz))

    def columns(i):
        return {15: (384, ff - 384), 16: (0, 384)}.get(i, (0, ff)) if isinstance(i, int) else (0, ff)

    def place(i):
        return min(i, 15) if isinstance(i, int) else i

    def view(ref, i):
        lo, n = columns(i)
        return ref.at[i] if n == ff else ref.at[place(i), :, pl.ds(lo, n)]

    def to_next(i):
        return zcopy(view(r.zs, i), view(r.zu, i), r.z_s0.at[i], r.z_ur.at[i], inwards)

    def to_middle(i):
        return zcopy(view(r.zs, i), view(r.zb, i), r.z_s0.at[i], r.z_br.at[i], inwards)

    def to_outer(i, src):
        return zcopy(view(src, i), view(r.zb, i), r.z_s1.at[i], r.z_br.at[i], -inwards)

    def inward(i, own):
        @pl.when(handed)
        def _():
            to_next(i).wait_recv()
            view(r.zs, i)[...] = (own() + view(r.zu, i)[...].astype(F32)).astype(BF16)

        @pl.when(jnp.logical_not(handed))
        def _():
            view(r.zs, i)[...] = own().astype(BF16)

        @pl.when(middle)
        def _():
            to_middle(i).start()

        @pl.when(jnp.logical_not(middle))
        def _():
            to_next(i).start()

    def og_view(i):
        lo, n = columns(i)
        k = place(i)
        at = r.og.at[k // 4, c, k % 4]
        return at if n == ff else at.at[:, pl.ds(lo, n)]

    def og_local(i, src):
        return pltpu.make_async_copy(view(src, i), og_view(i), r.og_loc.at[i])

    def og_across(i, src):
        return across(view(src, i), og_view(i), r.og_ss.at[i], r.og_rs.at[i])

    def ex_local(q, src):
        return pltpu.make_async_copy(src.at[12 + q, :, pl.ds(512, 128)], r.ex.at[h, c, q], r.ex_loc.at[q])

    def ex_plane(q, src, j, x):
        return copy_to(
            src.at[12 + q, :, pl.ds(512, 128)], r.ex.at[h, c, q],
            r.ex_ss.at[q, 2 * j + x], r.ex_rs.at[q, 2 * j + x], plane_id(j, x),
        )

    def ex_hand_on(q, j):
        at = r.ex.at[peer_of(h, j), c, q]
        return across(at, at, r.ex_ss.at[q, 2 * j + 1], r.ex_rs.at[q, 2 * j + 1])

    def ex_arrive(q):
        for j in (1, 2, 3):
            ex_plane(q, r.zs, j, 0).wait_send()
            ex_plane(q, r.zs, j, 0).wait_recv()
            ex_hand_on(q, j).start()

    def outward(i):
        def put(src):
            @pl.when(handed)
            def _():
                to_outer(i, src).start()

            og_local(i, src).start()
            og_across(i, src).start()
            if isinstance(i, int) and 12 <= i < 16:
                ex_local(i - 12, src).start()
                for j, x in ((3, 0), (1, 0), (2, 0), (0, 1)):
                    ex_plane(i - 12, src, j, x).start()

        to_middle(i).wait_recv()

        @pl.when(middle)
        def _():
            to_middle(i).wait_send()
            at = view(r.zs, i)
            at[...] = (at[...].astype(F32) + view(r.zb, i)[...].astype(F32)).astype(BF16)
            put(r.zs)

        @pl.when(jnp.logical_not(middle))
        def _():
            put(r.zb)

    def ffn_half(t):
        sl = pl.ds(4 * t, 4)
        return across(r.sf.at[sl], r.rf.at[sl], r.f_ss.at[t], r.f_rs.at[t])

    def ffn_piece(i):
        @pl.when(i % 4 == 0)
        def _():
            ffn_half(i // 4).wait_recv()

        inward(i, lambda: r.gown[i] + r.rf[i].astype(F32))

    def within(i, cond, do):
        if isinstance(i, int) and not 0 <= i < 17:
            return

        @pl.when((i >= 0) & (i < 17) & cond)
        def _():
            do(i)

    outer = jnp.logical_not(handed)

    def outer_pieces(lo, hi):
        @pl.when(outer)
        def _():
            pl.loop(lo, hi)(ffn_piece)

    def turn(m):
        piece = lambda i: (attention_piece if isinstance(i, int) and i >= 12 else ffn_piece)(i)
        within(m, handed, piece)
        if isinstance(m, int) and m in (9, 11, 13, 15, 16):
            within(12 + (m - 8) // 2, outer, piece)
        if not isinstance(m, int) or m <= 13:
            within(m - 2, middle, outward)
        if isinstance(m, int) and m >= 13:
            within(m - 1, middle, outward)
        within(m - 5, jnp.logical_not(middle), outward)

    def norm_bwd(x, gain, dn):
        inv = lax.rsqrt(jnp.mean(x * x, axis=-1, keepdims=True) + EPS)
        u = gain * dn
        dx = inv * u - x * (inv * inv * inv) * jnp.mean(x * u, axis=-1, keepdims=True)
        return dx, jnp.sum(dn * x * inv, axis=0, keepdims=True)

    mine_half = pl.ds(pl.multiple_of(c * hd2, hd2), hd2)
    other_half = pl.ds(pl.multiple_of((1 - c) * hd2, hd2), hd2)

    def a_half(g):
        src = r.wf.at[pl.ds(pl.multiple_of(g * hd2, hd2), hd2), pl.ds(0, 512)]
        return across(src, r.ra.at[g], r.a_ss.at[g], r.a_rs.at[g])

    def first_group(to):
        g = jnp.int32(KV - 1)
        for k in reversed(range(KV - 1)):
            g = jnp.where(r.own[k] == to, k, g)
        return g

    g1 = jnp.int32(0)
    for k in range(1, KV):
        for i in range(k):
            g1 = jnp.where(r.own[k] == r.own[i], k, g1)

    def own_share(to, i):
        lo, n = columns(i)
        q = place(i) - 12
        at = pl.ds(q * cr, cr)
        g0 = first_group(to)
        span = pl.ds(lo, min(n, 512 - lo))
        first = r.ha[g0, at, span].astype(F32) + r.ra[g0, at, span].astype(F32)
        if lo + n <= 512:
            return first
        cols = pl.ds(pl.multiple_of(to * 128, 128), 128)
        second = r.ha[g1, at, cols].astype(F32) + r.ra[g1, at, cols].astype(F32)
        return jnp.concatenate([first, second], axis=1)

    def share_slot(ref, j, i):
        lo, n = columns(i)
        return ref.at[4 * (j - 1) + place(i) - 12, :, pl.ds(lo, n)]

    def head_share(j, i):
        return remote(share_slot(r.sf, j, i), share_slot(r.rf2, j, i), r.h_ss.at[j, i - 12], r.h_rs.at[j, i - 12], j)

    def attention_sums():
        @pl.loop(0, KV)
        def _(g):
            def product(rows_of):
                first = nn(jnp.concatenate([r.nat[0, rows_of, :], r.nat[1, rows_of, :]], axis=1), r.dpg[g])
                second = nn(jnp.concatenate([r.dat[0, rows_of, :], r.dat[1, rows_of, :]], axis=1), r.aog[g])
                return first[:, :256], first[:, 256:] + second[:, :128], second[:, 128:]

            def put(dst, parts):
                dst[:, 0:256] = parts[0].astype(BF16)
                dst[:, 256:384] = parts[1].astype(BF16)
                dst[:, 384:512] = parts[2].astype(BF16)

            put(r.wf.at[pl.ds(pl.multiple_of(g * hd2, hd2), hd2)], product(other_half))
            a_half(g).start()
            put(r.ha.at[g], product(mine_half))

            @pl.when(g % 3 == 1)
            def _():
                turn(KV + g // 3)

        @pl.loop(0, KV)
        def _(g):
            a_half(g).wait_recv()

        for t in range(3):
            ffn_half(t).wait_send()
        for i in range(12, 17):
            for j in (3, 1, 2):
                share_slot(r.sf, j, i)[...] = own_share(peer_of(h, j), i).astype(BF16)
                head_share(j, i).start()
        turn(KV + 2)

    def attention_piece(i):
        def own():
            v = own_share(h, i)
            for j in (1, 2, 3):
                head_share(j, i).wait_recv()
                v = v + share_slot(r.rf2, j, i)[...].astype(F32)
            return v

        inward(i, own)

    @pl.loop(0, 2)
    def _(back):
        p = 1 - back
        ag = gather(2, halves(r.df.at[0, 0]), lambda j, x: halves(r.df.at[0, j])(x))

        @pl.when(p == 0)
        def _():
            block = r.d_res[...] * valid
            r.d_res[...] = block
            r.df[0, 0] = block.astype(BF16)
            ag.start()

        for j in range(HEADS):
            if j:
                @pl.when(p == 0)
                def _():
                    if j == 1:
                        ag.hand_on()
                    ag.wait(j)

            d_act = nn(r.df[p, j], wd_v[...])
            gate, up = r.gate[p, j], r.up[p, j]
            s = 1.0 / (1.0 + jnp.exp(-gate))
            dg = (d_act * up * s * (1.0 + gate * (1.0 - s))).astype(BF16)
            du = (d_act * (gate * s)).astype(BF16)
            r.act[j] = (gate * s * up).astype(BF16)
            r.dg[j] = dg
            r.du[j] = du
            part = nt(dg, wg_v[...]) + nt(du, wu_v[...])
            if j == 0:
                r.part[1 - p] = part.astype(BF16)
            else:
                r.psend[1 - p, j - 1] = part.astype(BF16)
                share(1 - p, 3 - p, j).start()
        for t, rhs in ((0, r.dg), (1, r.du), (2, r.act)):
            if t != 1:
                src = r.nf if t == 0 else r.df
                for j in range(HEADS):
                    store_t(lhs.at[:, j * rows : (j + 1) * rows], src[p, j])
            right = rhs[...].reshape(half, ff)
            theirs = nn(lhs[other_half, :], right)
            for q in range(4):
                v = theirs[q * cr : (q + 1) * cr] + r.sf[4 * t + q].astype(F32)
                r.sf[4 * t + q] = v.astype(BF16)

            @pl.when(p == 0)
            def _():
                ffn_half(t).start()

            ours = nn(lhs[mine_half, :], right)
            for q in range(4):
                r.gown[4 * t + q] += ours[q * cr : (q + 1) * cr]

        @pl.when(p == 0)
        def _():
            outer_pieces(0, 8)

        @pl.when(p == 1)
        def _():
            final(0, r.out).put(valid * (r.mid[1] + summed(1, 1)))
            final(0, r.out).send()
            sent(1, 1)

        dn = summed(1 - p, 3 - p)
        dx, dgain = norm_bwd(r.mid[p], gain_f(), dn)
        d_mid = r.d_res[...] + dx
        r.d_mid[...] = d_mid
        r.gain_v[1] += dgain
        da = d_mid.astype(BF16)
        store_t(r.dat.at[p], da)
        r.wide[:, :d] = nt(da, r.wo_v[...])
        for b, lo, w in blocks(d):
            y = r.wide[:, lo : lo + 128]
            g, o = head_row(2 * b)
            r.ou[g, o : o + rows, :] = jnp.where(low, 0.0, swap(y)).astype(BF16)
            if 2 * b + 1 < QH:
                g, o = head_row(2 * b + 1)
                r.ou[g, o : o + rows, :] = jnp.where(low, 0.0, y).astype(BF16)

        def hop(g):
            return across(r.dkv_ctx.at[g], r.dkv_ctx_r.at[p, g], r.dc_ss.at[p, g], r.dc_rs.at[p, g])

        def to_owner(j, g):
            return remote(
                r.dkv_s.at[g, j - 1], r.dkv_r.at[g, j - 1], r.dkv_ss.at[p, g], r.dkv_rs.at[p, g], j
            )

        def all_owners(g):
            return remote(r.dkv_s.at[g], r.dkv_r.at[g], r.dkv_ss.at[p, g], r.dkv_rs.at[p, g], 1)

        def pass_on(g):
            @pl.when(c == 0)
            def _():
                hop(g).wait_recv()
                r.dkv[g] += r.dkv_ctx_r[p, g].astype(F32)

            for j in (1, 2, 3):
                r.dkv_s[g, j - 1] = r.dkv[g, :, j * rows : (j + 1) * rows].astype(BF16)
                to_owner(j, g).start()

        @pl.loop(0, KV)
        def _(g):
            kv = r.kv[p, g]
            acc = None
            for k in range(GQ):
                q = r.ql[p, g, k * rows : (k + 1) * rows, :]
                o = r.ou[g, k * rows : (k + 1) * rows, :]
                s = nt(q, kv)
                s = s + r.bias[...]
                lse = jnp.sum(jnp.where(lane == g * GQ + k, r.lse[p], 0.0), axis=-1, keepdims=True)
                pr = jnp.exp(s - lse)
                dpr = nt(o, kv)
                delta = jnp.sum(pr * dpr, axis=-1, keepdims=True)
                ds = (pr * (dpr - delta)).astype(BF16)
                r.heads[g * GQ + k] = unrope(nn(ds, kv) * HD ** (-0.5))
                t = nn(o.T, pr.astype(BF16)) + nn(q.T, ds)
                acc = t if acc is None else acc + t
            r.dkv[g] = acc[:, :half]
            r.dkv_ctx[g] = acc[:, half:].astype(BF16)

            @pl.when(c == 1)
            def _():
                hop(g).start()

            @pl.when(g > 0)
            def _():
                pass_on(g - 1)

            @pl.when((p == 0) & (g == 0))
            def _():
                outer_pieces(8, 12)

            @pl.when((p == 0) & (g > 0))
            def _():
                turn(g - 1)

        pass_on(KV - 1)
        mine = pl.ds(pl.multiple_of(p * rows, rows), rows)
        for b, lo, w in blocks(d):
            y = r.heads[2 * b]
            if 2 * b + 1 < QH:
                y = jnp.where(low, y, swap(r.heads[2 * b + 1]))
            r.at[:, lo : lo + w] = y[:, :w].astype(BF16)
        for g in range(KV):
            both = jnp.where(low, r.heads[g * GQ], swap(r.heads[g * GQ + 1]))
            r.dpg[g, mine, 0:128] = both.astype(BF16)

        r.wide[:, :d] = nt(r.at[...], r.wq_v[...])

        @pl.when(p == 0)
        def _():
            turn(KV - 1)

        keys, vals = [], []
        for g in range(KV):
            t = r.dkv[g, :, 0:rows]
            all_owners(g).wait_recv()
            for j in range(3):
                t = t + r.dkv_r[g, j].astype(F32)
            t = t.T
            kt, vt = unrope(t), swap(t)
            keys.append(kt)
            vals.append(t)
            r.dpg[g, mine, 128:256] = jnp.where(low, r.heads[g * GQ + 2], swap(kt)).astype(BF16)
            r.dpg[g, mine, 256:384] = jnp.where(low, vt, 0.0).astype(BF16)
        for b, lo, w in blocks(KV * HD):
            kb, vb = keys[2 * b], swap(vals[2 * b])
            if 2 * b + 1 < KV:
                kb = jnp.where(low, kb, swap(keys[2 * b + 1]))
                vb = jnp.where(low, vb, vals[2 * b + 1])
            r.dk[:, lo : lo + w] = kb[:, :w].astype(BF16)
            r.dv[:, lo : lo + w] = vb[:, :w].astype(BF16)
        @pl.when(p == 0)
        def _():
            attention_sums()

        dna = r.wide[:, :d] + nn(r.dk[...], r.wk_v[...]) + nn(r.dv[...], r.wv_v[...])
        dx, dgain = norm_bwd(r.res[p], gain_a(), dna)
        r.d_res[...] = r.d_mid[...] + dx
        r.gain_v[0] += dgain
        sent(1 - p, 3 - p)

        @pl.when(p == 0)
        def _():
            ag.drain()

        @pl.when(p == 1)
        def _():
            final(0, r.out).hand_on()


        @pl.loop(0, KV)
        def _(g):
            all_owners(g).wait_send()

            @pl.when(c == 1)
            def _():
                hop(g).wait_send()

    final(1, r.gin).put(r.d_res[...])

    me = 2 * h + c
    r.gain_p[me] = r.gain_v[...]
    gp = [copy_to(r.gain_p.at[me], r.gain_p.at[me], r.gp_ss.at[2 * j + x], r.gp_rs.at[2 * j + x], plane_id(j, x))
          for j, x in plane]
    for cp in gp:
        cp.start()

    for cp in gp:
        cp.wait_recv()
    total = r.gain_p[0]
    for k in range(1, 2 * HEADS):
        total = total + r.gain_p[k]
    r.gain_z[z] = total
    gz = [copy_to(r.gain_z.at[z], r.gain_z.at[z], r.gz_ss.at[k], r.gz_rs.at[k], dict(batch=(z + k) % nb))
          for k in range(1, nb)]
    for cp in gz:
        cp.start()

    for m in range(KV + 3, 22):
        turn(m)
        if m == 13:
            final(1, r.gin).send()
        if m == 16:
            final(1, r.gin).hand_on()

    for cp in gz:
        cp.wait_recv()
    total = r.gain_z[0]
    for k in range(1, nb):
        total = total + r.gain_z[k]
    r.gain_v[...] = total
    gains_out = pltpu.make_async_copy(r.gain_v, r.gains_out, r.loc_sem.at[2])
    gains_out.start()

    for q in range(4):
        ex_arrive(q)

    gains_out.wait()
    for cp in gp + gz:
        cp.wait_send()
    for j in (1, 2, 3):
        for i in range(12, 17):
            head_share(j, i).wait_send()

    @pl.loop(0, KV)
    def _(g):
        a_half(g).wait_send()

    def settle(i):
        og_local(i, r.zs).wait()
        og_across(i, r.zs).wait_send()
        og_across(i, r.zs).wait_recv()

        @pl.when(jnp.logical_not(middle))
        def _():
            to_next(i).wait_send()

        @pl.when(handed)
        def _():
            to_outer(i, r.zs).wait_send()

    pl.loop(0, 12)(settle)
    for i in range(12, 17):
        settle(i)

    for q in range(4):
        ex_local(q, r.zs).wait()
        ex_plane(q, r.zs, 0, 1).wait()
        for j in (1, 2, 3):
            ex_hand_on(q, j).wait()
    for k, out in ((0, r.out), (1, r.gin)):
        end = final(k, out)
        end.own.wait()
        for j in (1, 2, 3):
            end.wait(j)
        end.drain()


def put_kernel(own, o, gin, og, ex, ga, gf, o_out, gin_out, gq, gk, gv, go, gg, gu, gd, ga_out, gf_out):
    h = lax.axis_index("head")
    held = jnp.int32(0)
    for k in range(KV):
        held = held + jnp.where(own[k] == h, 1, 0)
    gw = GQ * HD
    o_out[...] = o[...]
    gin_out[...] = gin[...].astype(F32)
    wide = lambda x: x.astype(F32).reshape(-1, x.shape[-1])
    gg[...] = wide(og[0])
    gu[...] = wide(og[1])
    gd[...] = wide(og[2])
    ga_out[...] = ga[...]
    gf_out[...] = gf[...]
    first = wide(og[3])[:, 0:512]
    second = jnp.concatenate([wide(ex[k]) for k in range(HEADS)], axis=1)
    second = jnp.where(held > 1, second, 0.0)
    for out, lo, width in ((gq, 0, gw), (gk, gw, HD), (gv, gw + HD, HD), (go, gw + 2 * HD, gw)):
        out[...] = jnp.concatenate([first[:, lo : lo + width], second[:, lo : lo + width]], axis=1)


def body(nb, hidden_in, cotangent, lengths, owners, w_query, w_key, w_value, w_output, gate_weight, up_weight, down_weight,
         gain_attn, gain_ffn):
    half, d = hidden_in.shape[1:]
    ff = gate_weight.shape[1]
    rows = half // HEADS
    cr = d // 8
    scratch = scratch_of(rows, d, ff, nb)
    anyspec = pl.BlockSpec(memory_space=pl.ANY)
    smem = pl.BlockSpec(memory_space=pltpu.SMEM)
    sd = jax.ShapeDtypeStruct
    ins = dict(
        hid=anyspec, cot=anyspec, len=smem, own=smem, ga=anyspec, gf=anyspec, tab=anyspec,
        wq=anyspec, wk=anyspec, wv=anyspec, wo=anyspec, wg=anyspec, wu=anyspec, wd=anyspec,
    )
    outs = dict(
        out=sd((d, half), BF16), gin=sd((d, half), BF16),
        og=sd((4, 2, 4, cr, ff), BF16), ex=sd((HEADS, 2, 4, cr, 128), BF16), gains_out=sd((2, 1, d), F32),
    )
    names = tuple(ins) + tuple(outs) + tuple(scratch)
    o, gin, og, ex, gains = pl.pallas_call(
        functools.partial(step_kernel, names, rows, d, ff, nb),
        out_shape=tuple(outs.values()),
        in_specs=list(ins.values()),
        out_specs=(anyspec,) * len(outs),
        scratch_shapes=list(scratch.values()),
        compiler_params=pltpu.CompilerParams(
            collective_id=0, has_side_effects=True, vmem_limit_bytes=67043328
        ),
    )(
        hidden_in[0].T, cotangent[0].T, lengths, owners, gain_attn[None], gain_ffn[None],
        jnp.asarray(rope_table(2 * half)), w_query, w_key.T, w_value.T, w_output, gate_weight, up_weight, down_weight.T,
    )
    gw, block = GQ * HD, lambda *shape: (lambda index: pl.BlockSpec(shape, index))
    rowwise = lambda width: block(2 * cr, width)(lambda i: (i, 0))
    gains_spec = lambda k: block(None, 1, d)(lambda i: (k, 0, 0))
    gain_out = block(1, d)(lambda i: (0, 0))
    o, gin, gq, gk, gv, go, gg, gu, gd, ga, gf = pl.pallas_call(
        put_kernel,
        grid=(4,),
        out_shape=(
            sd((d, half), BF16), sd((d, half), F32), sd((d, 2 * gw), F32), sd((d, 2 * HD), F32), sd((d, 2 * HD), F32),
            sd((d, 2 * gw), F32), sd((d, ff), F32), sd((d, ff), F32), sd((d, ff), F32), sd((1, d), F32), sd((1, d), F32),
        ),
        in_specs=[
            smem, rowwise(half), rowwise(half), block(4, None, 2, cr, ff)(lambda i: (0, i // 2, i % 2, 0, 0)),
            block(HEADS, None, 2, cr, 128)(lambda i: (0, i // 2, i % 2, 0, 0)), gains_spec(0), gains_spec(1),
        ],
        out_specs=(
            rowwise(half), rowwise(half), rowwise(2 * gw), rowwise(2 * HD), rowwise(2 * HD), rowwise(2 * gw),
            rowwise(ff), rowwise(ff), rowwise(ff), gain_out, gain_out,
        ),
    )(owners, o, gin, og, ex, gains, gains)
    return o.T[None], gin.T[None], gq, gk, gv, go.T, gg, gu, gd.T, ga[0], gf[0]


def solution(mesh):
    rep = P()
    io = P("batch", "ctx", None)
    in_specs = (io, io, P("batch"), rep, rep, rep, rep, rep, P(None, "head"), P(None, "head"), P("head", None), rep, rep)
    out_specs = (io, io, P(None, "head"), P(None, "head"), P(None, "head"), P("head", None), P(None, "head"),
                 P(None, "head"), P("head", None), rep, rep)
    return jax.shard_map(
        functools.partial(body, mesh.shape["batch"]), mesh=mesh, in_specs=in_specs, out_specs=out_specs, check_vma=False
    )
```

```python
import functools
import math
from types import SimpleNamespace

import jax
import jax.numpy as jnp
import numpy as np
from jax import lax
from jax.experimental import pallas as pl
from jax.experimental.pallas import tpu as pltpu
from jax.sharding import PartitionSpec as P

KV = 5
HD = 64
GQ = 3
QH = KV * GQ
HEADS = 4
EPS = 1e-05
NEG = -1e30
MESH = pl.DeviceIdType.MESH
F32 = jnp.float32
BF16 = jnp.bfloat16


def nn(a, b):
    return lax.dot_general(a, b, (((1,), (0,)), ((), ())), preferred_element_type=F32)


def nt(a, b):
    return lax.dot_general(a, b, (((1,), (1,)), ((), ())), preferred_element_type=F32)


def tn(a, b):
    return lax.dot_general(a, b, (((0,), (0,)), ((), ())), preferred_element_type=F32)


def rope_table(slots):
    inverse = np.exp(np.arange(HD // 2, dtype=np.float32) * np.float32(-2.0 * math.log(10000.0) / HD))
    angles = np.arange(slots, dtype=np.float32)[:, None] * inverse[None, :].astype(np.float32)
    cos, sin = np.cos(angles).astype(np.float32), np.sin(angles).astype(np.float32)
    return np.concatenate([cos, sin] * 2, axis=1)


def peer_of(h, j):
    return (h, h + 1 - 2 * (h % 2), (h + 2) % 4, 3 - h)[j]


def scratch_of(rows, d, ff, nb):
    n = HEADS
    half = n * rows
    keys = 2 * half
    dp = -(-d // 128) * 128
    cr = d // 8
    v = pltpu.VMEM
    dma = pltpu.SemaphoreType.DMA
    return dict(
        cot_v=v((d, half), BF16),
        tab_v=v((rows, 256), F32),
        gains_v=v((2, 1, d), F32),
        wq_v=v((d, QH * HD), BF16),
        wk_v=v((KV * HD, d), BF16),
        wv_v=v((KV * HD, d), BF16),
        wo_v=v((QH * HD, d), BF16),
        wf=v((3 * d, ff), BF16),
        res=v((2, rows, d), F32),
        mid=v((2, rows, d), F32),
        nat=v((2, d, rows), BF16),
        dat=v((2, d, rows), BF16),
        ql=v((2, KV, GQ * rows, 128), BF16),
        kv=v((2, KV, keys, 128), BF16),
        lse=v((2, rows, 128), F32),
        at=v((rows, d), BF16),
        nf=v((2, n, rows, d), BF16),
        gate=v((2, n, rows, ff), F32),
        up=v((2, n, rows, ff), F32),
        act=v((n, rows, ff), BF16),
        bias=v((rows, keys), F32),
        wide=v((rows, dp), F32),
        heads=v((QH, rows, 128), F32),
        part=v((2, rows, d), BF16),
        psend=v((2, 3, rows, d), BF16),
        precv=v((2, 3, rows, d), BF16),
        d_res=v((rows, d), F32),
        d_mid=v((rows, d), F32),
        df=v((2, n, rows, d), BF16),
        dg=v((n, rows, ff), BF16),
        du=v((n, rows, ff), BF16),
        ou=v((KV, GQ * rows, 128), BF16),
        dk=v((rows, KV * HD), BF16),
        dv=v((rows, KV * HD), BF16),
        dpg=v((KV, 2 * rows, 384), BF16),
        aog=v((KV, 2 * rows, 256), BF16),
        dkv=v((KV, 128, half), F32),
        dkv_ctx=v((KV, 128, half), BF16),
        dkv_ctx_r=v((2, KV, 128, half), BF16),
        dkv_s=v((KV, 3, 128, rows), BF16),
        dkv_r=v((KV, 3, 128, rows), BF16),
        fin=v((2, d, rows), BF16),
        gown=v((12, cr, ff), F32),
        sf=v((12, cr, ff), BF16),
        rf=v((12, cr, ff), BF16),
        rf2=v((12, cr, ff), BF16),
        zs=v((16, cr, ff), BF16),
        zu=v((16, cr, ff), BF16),
        zb=v((16, cr, ff), BF16),
        ha=v((KV, d // 2, 512), BF16),
        ra=v((KV, d // 2, 512), BF16),
        gain_v=v((2, 1, d), F32),
        gain_p=v((2 * n, 2, 1, d), F32),
        gain_z=v((nb, 2, 1, d), F32),
        in_sem=dma((12,)),
        loc_sem=dma((8,)),
        kv_ss=dma((2, KV)),
        kv_rs=dma((2, KV)),
        kvc_ss=dma((2, KV)),
        kvc_rs=dma((2, KV)),
        ag_ss=dma((5, 6)),
        ag_rs=dma((5, 6)),
        p_ss=dma((4, 4)),
        p_rs=dma((4, 4)),
        dc_ss=dma((2, KV)),
        dc_rs=dma((2, KV)),
        dkv_ss=dma((2, KV)),
        dkv_rs=dma((2, KV)),
        f_ss=dma((3,)),
        f_rs=dma((3,)),
        z_s0=dma((17,)),
        z_s1=dma((17,)),
        z_ur=dma((17,)),
        z_br=dma((17,)),
        og_loc=dma((17,)),
        og_ss=dma((17,)),
        og_rs=dma((17,)),
        a_ss=dma((KV,)),
        a_rs=dma((KV,)),
        h_ss=dma((4, 5)),
        h_rs=dma((4, 5)),
        ex_loc=dma((4,)),
        ex_ss=dma((4, 8)),
        ex_rs=dma((4, 8)),
        gp_ss=dma((8,)),
        gp_rs=dma((8,)),
        gz_ss=dma((nb,)),
        gz_rs=dma((nb,)),
    )


def step_kernel(names, rows, d, ff, nb, *refs):
    r = SimpleNamespace(**dict(zip(names, refs)))
    wg_v, wu_v, wd_v = (r.wf.at[pl.ds(t * d, d)] for t in range(3))
    lhs, hid_v = r.cot_v, r.fin.at[1]
    h = lax.axis_index("head")
    c = lax.axis_index("ctx")
    z = lax.axis_index("batch")
    half = HEADS * rows
    hd2 = d // 2
    cr = d // 8
    lane = lax.broadcasted_iota(jnp.int32, (rows, 128), 1)
    low = lane < HD
    quarter = (lane % HD) < HD // 2

    def copy_to(src, dst, ss, rs, where):
        return pltpu.make_async_remote_copy(
            src_ref=src, dst_ref=dst, send_sem=ss, recv_sem=rs, device_id=where, device_id_type=MESH
        )

    def remote(src, dst, ss, rs, j):
        return copy_to(src, dst, ss, rs, dict(head=peer_of(h, j)))

    def across(src, dst, ss, rs):
        return copy_to(src, dst, ss, rs, dict(ctx=1 - c))

    def load(k, src, dst):
        return pltpu.make_async_copy(src, dst, r.in_sem.at[k])

    my_rows = pl.ds(pl.multiple_of(h * rows, rows), rows)
    my_pos = pl.ds(pl.multiple_of(c * half + h * rows, rows), rows)
    loads = SimpleNamespace(
        hid=load(0, r.hid.at[:, my_rows], hid_v),
        ga=load(1, r.ga, r.gains_v.at[0]),
        gf=load(11, r.gf, r.gains_v.at[1]),
        wk=load(3, r.wk, r.wk_v),
        wv=load(4, r.wv, r.wv_v),
        tab=load(5, r.tab.at[my_pos], r.tab_v.at[:, pl.ds(0, 128)]),
        wq=load(2, r.wq, r.wq_v),
        wo=load(6, r.wo, r.wo_v),
        wg=load(7, r.wg, wg_v),
        wu=load(8, r.wu, wu_v),
        wd=load(9, r.wd, wd_v),
        cot=load(10, r.cot, r.cot_v),
    )
    for cp in vars(loads).values():
        cp.start()

    plane = [(j, x) for j in range(HEADS) for x in range(2) if (j, x) != (0, 0)]

    def plane_id(j, x):
        return dict(head=peer_of(h, j), ctx=1 - c if x else c)

    barrier = pltpu.get_barrier_semaphore()
    for j, x in plane:
        pl.semaphore_signal(barrier, inc=1, device_id=plane_id(j, x), device_id_type=MESH)
    for k in range(1, nb):
        pl.semaphore_signal(barrier, inc=1, device_id=dict(batch=(z + k) % nb), device_id_type=MESH)
    pl.semaphore_wait(barrier, len(plane) + nb - 1)

    length = r.len[0]
    row_pos = c * half + h * rows + lax.broadcasted_iota(jnp.int32, (rows, 1), 0)
    valid = (row_pos < length).astype(F32)

    zero_w = jnp.zeros((rows, 128), F32)
    r.wide[...] = jnp.zeros(r.wide.shape, F32)
    vlo = r.wide.shape[1] // 2
    r.lse[0] = zero_w
    r.lse[1] = zero_w

    @pl.when(c == 0)
    def _():
        for p in range(2):
            r.kv[p, :, half:, :] = jnp.zeros((KV, half, 128), BF16)

    def fill_mask():
        for blk in range(2 * HEADS):
            own = blk < HEADS
            base = (c if own else 1 - c) * half + peer_of(h, blk % HEADS) * rows
            kp = base + lax.broadcasted_iota(jnp.int32, (rows, rows), 1)
            qp = c * half + h * rows + lax.broadcasted_iota(jnp.int32, (rows, rows), 0)
            ok = (kp <= qp) & (kp < length)
            r.bias[:, blk * rows : (blk + 1) * rows] = jnp.where(ok, 0.0, NEG)

    def fill_cotangent():
        for j in range(HEADS):
            pr = pl.ds(pl.multiple_of(peer_of(h, j) * rows, rows), rows)
            pos = c * half + peer_of(h, j) * rows + lax.broadcasted_iota(jnp.int32, (rows, 1), 0)
            ok = (pos < length).astype(F32)
            for b, lo, w in blocks(d):
                block = r.cot_v[lo : lo + w, pr].astype(F32).T * ok
                r.df[1, j, :, lo : lo + w] = block.astype(BF16)
                if j == 0:
                    r.d_res[:, lo : lo + w] = block

    def clear_sums():
        @pl.loop(0, 12)
        def _(i):
            r.gown[i] = jnp.zeros((cr, ff), F32)
            r.sf[i] = jnp.zeros((cr, ff), BF16)

        r.gain_v[...] = jnp.zeros((2, 1, d), F32)

    def share(k, e, j):
        return remote(r.psend.at[k, j - 1], r.precv.at[k, j - 1], r.p_ss.at[e, j], r.p_rs.at[e, j], j)

    def summed(k, e):
        total = r.part[k].astype(F32)
        for j in (1, 2, 3):
            share(k, e, j).wait_recv()
            total = total + r.precv[k, j - 1].astype(F32)
        return total

    def sent(k, e):
        for j in (1, 2, 3):
            share(k, e, j).wait_send()

    def rms(x, gain):
        inv = lax.rsqrt(jnp.mean(x * x, axis=-1, keepdims=True) + EPS)
        return x * inv * gain

    def turned(x):
        return jnp.where(quarter, -pltpu.roll(x, 128 - HD // 2, 1), pltpu.roll(x, HD // 2, 1))

    def rope(x):
        return x * r.tab_v[:, 0:128] + turned(x) * r.tab_v[:, 128:256]

    def unrope(x):
        return x * r.tab_v[:, 0:128] - turned(x) * r.tab_v[:, 128:256]

    def swap(x):
        return pltpu.roll(x, HD, 1)

    def blocks(width):
        return [(b, b * 128, min(128, width - b * 128)) for b in range(-(-width // 128))]

    def head_row(i):
        return i // GQ, (i % GQ) * rows

    def store_t(dst, src):
        for b, lo, w in blocks(d):
            dst[lo : lo + w, :] = src[:, lo : lo + w].T

    gain_a = lambda: r.gains_v[0]
    gain_f = lambda: r.gains_v[1]

    loads.tab.wait()
    both = r.tab_v[:, 0:128]
    r.tab_v[:, 128:256] = jnp.where(quarter, pltpu.roll(both, 128 - HD // 2, 1), both)
    r.tab_v[:, 0:128] = jnp.where(quarter, both, pltpu.roll(both, HD // 2, 1))
    loads.ga.wait()
    loads.gf.wait()
    loads.hid.wait()
    for b, lo, w in blocks(d):
        r.res[0, :, lo : lo + w] = hid_v[lo : lo + w, :].astype(F32).T

    def gather(e, src, dst, by_owner=False):
        def hop(k, ref, to, j):
            return remote(ref, to, r.ag_ss.at[e, k], r.ag_rs.at[e, k], j)

        at = (lambda j, near, x: dst(near, x)) if by_owner else (lambda j, near, x: dst(j, x))
        first = [hop(0, src(0), at(1, 0, 0), 1), hop(3, src(1), at(2, 0, 1), 2), hop(1, src(1), at(1, 0, 1), 1),
                 hop(2, src(0), at(2, 0, 0), 2)]
        relay = [hop(4, dst(1, 0), at(3, 1, 0), 2), hop(5, dst(2, 1), at(3, 2, 1), 1)]
        def start():
            for cp in first:
                cp.start()

        def hand_on():
            first[0].wait_recv()
            relay[0].start()
            first[1].wait_recv()
            relay[1].start()

        def wait(j):
            for cp in ((first[2],), (first[3],), relay)[j - 1]:
                cp.wait_recv()

        def drain():
            for cp in first + relay:
                cp.wait_send()

        return SimpleNamespace(start=start, hand_on=hand_on, wait=wait, drain=drain)

    def halves(ref):
        n = ref.shape[0] // 2
        return lambda x: ref.at[pl.ds(x * n, n)]

    @pl.loop(0, 2)
    def _(p):
        x = r.res[p]
        na = rms(x, gain_a()).astype(BF16)
        store_t(r.nat.at[p], na)

        @pl.when(p == 0)
        def _():
            loads.wk.wait()
            loads.wv.wait()

        r.wide[:, : KV * HD] = nt(na, r.wk_v[...])
        r.wide[:, vlo : vlo + KV * HD] = nt(na, r.wv_v[...])
        for b in range(-(-KV // 2)):
            kb = rope(r.wide[:, b * 128 : (b + 1) * 128])
            vb = r.wide[:, vlo + b * 128 : vlo + (b + 1) * 128]
            r.kv[p, 2 * b, 0:rows, :] = jnp.where(low, kb, swap(vb)).astype(BF16)
            if 2 * b + 1 < KV:
                r.kv[p, 2 * b + 1, 0:rows, :] = jnp.where(low, swap(kb), vb).astype(BF16)

        def to_peer(j, g):
            return remote(
                r.kv.at[p, g, pl.ds(0, rows)], r.kv.at[p, g, pl.ds(j * rows, rows)],
                r.kv_ss.at[p, g], r.kv_rs.at[p, g], j,
            )

        def to_partner(j, g):
            return across(
                r.kv.at[p, g, pl.ds(j * rows, rows)], r.kv.at[p, g, pl.ds(half + j * rows, rows)],
                r.kvc_ss.at[p, g], r.kvc_rs.at[p, g],
            )

        def all_peers(g):
            span = r.kv.at[p, g, pl.ds(rows, 3 * rows)]
            return remote(span, span, r.kv_ss.at[p, g], r.kv_rs.at[p, g], 1)

        def all_partner(g):
            span = r.kv.at[p, g, pl.ds(half, half)]
            return across(span, span, r.kvc_ss.at[p, g], r.kvc_rs.at[p, g])

        for g in range(KV):
            for j in (1, 2, 3):
                to_peer(j, g).start()

            @pl.when(c == 0)
            def _():
                to_partner(0, g).start()

        def arrive(g):
            all_peers(g).wait_recv()

            @pl.when(c == 0)
            def _():
                for j in (1, 2, 3):
                    to_partner(j, g).start()

        @pl.when(p == 0)
        def _():
            fill_mask()
            loads.wq.wait()

        r.wide[:, :d] = nn(na, r.wq_v[...])
        for b, lo, w in blocks(d):
            y = rope(r.wide[:, lo : lo + 128]).astype(BF16).astype(F32) * HD ** (-0.5)
            g, o = head_row(2 * b)
            r.ql[p, g, o : o + rows, :] = jnp.where(low, y, 0.0).astype(BF16)
            if 2 * b + 1 < QH:
                g, o = head_row(2 * b + 1)
                r.ql[p, g, o : o + rows, :] = jnp.where(low, swap(y), 0.0).astype(BF16)

        arrive(0)

        @pl.loop(0, KV)
        def _(g):
            @pl.when(g < KV - 1)
            def _():
                arrive(g + 1)

            @pl.when(c == 1)
            def _():
                all_partner(g).wait_recv()

            kv = r.kv[p, g]
            for k in range(GQ):
                s = nt(r.ql[p, g, k * rows : (k + 1) * rows, :], kv)
                s = s + r.bias[...]
                m = jnp.max(s, axis=-1, keepdims=True)
                e = jnp.exp(s - m)
                t = jnp.sum(e, axis=-1, keepdims=True)
                r.lse[p] += jnp.where(lane == g * GQ + k, m + jnp.log(t), 0.0)
                r.heads[g * GQ + k] = nn((e * (1.0 / t)).astype(BF16), kv)

        mine = pl.ds(pl.multiple_of(p * rows, rows), rows)
        for g in range(KV):
            o0, o1, o2 = (r.heads[g * GQ + k] for k in range(GQ))
            r.aog[g, mine, 0:128] = jnp.where(low, 0.0, o0).astype(BF16)
            r.aog[g, mine, 128:256] = jnp.where(low, swap(o1), o2).astype(BF16)
        for b, lo, w in blocks(d):
            first = swap(r.heads[2 * b])
            both = jnp.where(low, first, r.heads[2 * b + 1]) if 2 * b + 1 < QH else first
            r.at[:, lo : lo + w] = both[:, :w].astype(BF16)

        @pl.when(p == 0)
        def _():
            loads.wo.wait()

        mid = r.res[p] + nn(r.at[...], r.wo_v[...])
        r.mid[p] = mid
        r.nf[p, 0] = rms(mid, gain_f()).astype(BF16)
        ag = gather(p, halves(r.nf.at[p, 0]), lambda j, x: halves(r.nf.at[p, j])(x))
        ag.start()

        @pl.when(p == 0)
        def _():
            loads.wg.wait()
            loads.wu.wait()
            loads.wd.wait()

        for j in range(HEADS):
            if j == 1:
                ag.hand_on()
            if j:
                ag.wait(j)
            nf = r.nf[p, j]
            gate = nn(nf, wg_v[...])
            up = nn(nf, wu_v[...])
            r.gate[p, j] = gate
            r.up[p, j] = up
            act = (gate / (1.0 + jnp.exp(-gate)) * up).astype(BF16)
            part = nt(act, wd_v[...])
            if j == 0:
                r.part[p] = part.astype(BF16)
            else:
                r.psend[p, j - 1] = part.astype(BF16)
                share(p, p, j).start()
        ag.drain()

        @pl.when(p == 0)
        def _():
            loads.cot.wait()
            fill_cotangent()
            clear_sums()
            r.res[1] = valid * (r.mid[0] + summed(0, 0))
            sent(0, 0)

        @pl.loop(0, KV)
        def _(g):
            all_peers(g).wait_send()

            @pl.when(c == 0)
            def _():
                all_partner(g).wait_send()

    def final(k, out):
        def there(j, x):
            at = pl.ds(pl.multiple_of(peer_of(h, j) * rows, rows), rows)
            return out.at[pl.ds(x * hd2, hd2), at]

        own = pltpu.make_async_copy(r.fin.at[k], out.at[:, my_rows], r.loc_sem.at[k])
        ag = gather(3 + k, halves(r.fin.at[k]), there, True)

        def put(value):
            store_t(r.fin.at[k], value.astype(BF16))
            own.start()

        return SimpleNamespace(put=put, own=own, send=ag.start, hand_on=ag.hand_on, wait=ag.wait, drain=ag.drain)

    low_side = z < nb // 2
    middle = (z == nb // 2 - 1) | (z == nb // 2)
    handed = (z > 0) & (z < nb - 1)
    inwards = jnp.where(low_side, 1, -1)

    def zcopy(src, dst, ss, rs, dz):
        return copy_to(src, dst, ss, rs, dict(batch=z + dz))

    def columns(i):
        return {15: (384, ff - 384), 16: (0, 384)}.get(i, (0, ff)) if isinstance(i, int) else (0, ff)

    def place(i):
        return min(i, 15) if isinstance(i, int) else i

    def view(ref, i):
        lo, n = columns(i)
        return ref.at[i] if n == ff else ref.at[place(i), :, pl.ds(lo, n)]

    def to_next(i):
        return zcopy(view(r.zs, i), view(r.zu, i), r.z_s0.at[i], r.z_ur.at[i], inwards)

    def to_middle(i):
        return zcopy(view(r.zs, i), view(r.zb, i), r.z_s0.at[i], r.z_br.at[i], inwards)

    def to_outer(i, src):
        return zcopy(view(src, i), view(r.zb, i), r.z_s1.at[i], r.z_br.at[i], -inwards)

    def inward(i, own):
        @pl.when(handed)
        def _():
            to_next(i).wait_recv()
            view(r.zs, i)[...] = (own() + view(r.zu, i)[...].astype(F32)).astype(BF16)

        @pl.when(jnp.logical_not(handed))
        def _():
            view(r.zs, i)[...] = own().astype(BF16)

        @pl.when(middle)
        def _():
            to_middle(i).start()

        @pl.when(jnp.logical_not(middle))
        def _():
            to_next(i).start()

    def og_view(i):
        lo, n = columns(i)
        k = place(i)
        at = r.og.at[k // 4, c, k % 4]
        return at if n == ff else at.at[:, pl.ds(lo, n)]

    def og_local(i, src):
        return pltpu.make_async_copy(view(src, i), og_view(i), r.og_loc.at[i])

    def og_across(i, src):
        return across(view(src, i), og_view(i), r.og_ss.at[i], r.og_rs.at[i])

    def ex_local(q, src):
        return pltpu.make_async_copy(src.at[12 + q, :, pl.ds(512, 128)], r.ex.at[h, c, q], r.ex_loc.at[q])

    def ex_plane(q, src, j, x):
        return copy_to(
            src.at[12 + q, :, pl.ds(512, 128)], r.ex.at[h, c, q],
            r.ex_ss.at[q, 2 * j + x], r.ex_rs.at[q, 2 * j + x], plane_id(j, x),
        )

    def ex_hand_on(q, j):
        at = r.ex.at[peer_of(h, j), c, q]
        return across(at, at, r.ex_ss.at[q, 2 * j + 1], r.ex_rs.at[q, 2 * j + 1])

    def ex_arrive(q):
        for j in (1, 2, 3):
            ex_plane(q, r.zs, j, 0).wait_send()
            ex_plane(q, r.zs, j, 0).wait_recv()
            ex_hand_on(q, j).start()

    def outward(i):
        def put(src):
            @pl.when(handed)
            def _():
                to_outer(i, src).start()

            og_local(i, src).start()
            og_across(i, src).start()
            if isinstance(i, int) and 12 <= i < 16:
                ex_local(i - 12, src).start()
                for j, x in ((3, 0), (1, 0), (2, 0), (0, 1)):
                    ex_plane(i - 12, src, j, x).start()

        to_middle(i).wait_recv()

        @pl.when(middle)
        def _():
            to_middle(i).wait_send()
            at = view(r.zs, i)
            at[...] = (at[...].astype(F32) + view(r.zb, i)[...].astype(F32)).astype(BF16)
            put(r.zs)

        @pl.when(jnp.logical_not(middle))
        def _():
            put(r.zb)

    def ffn_half(t):
        sl = pl.ds(4 * t, 4)
        return across(r.sf.at[sl], r.rf.at[sl], r.f_ss.at[t], r.f_rs.at[t])

    def ffn_piece(i):
        @pl.when(i % 4 == 0)
        def _():
            ffn_half(i // 4).wait_recv()

        inward(i, lambda: r.gown[i] + r.rf[i].astype(F32))

    def within(i, cond, do):
        if isinstance(i, int) and not 0 <= i < 17:
            return

        @pl.when((i >= 0) & (i < 17) & cond)
        def _():
            do(i)

    outer = jnp.logical_not(handed)

    def outer_pieces(lo, hi):
        @pl.when(outer)
        def _():
            pl.loop(lo, hi)(ffn_piece)

    def turn(m):
        piece = lambda i: (attention_piece if isinstance(i, int) and i >= 12 else ffn_piece)(i)
        within(m, handed, piece)
        if isinstance(m, int) and m in (9, 11, 13, 15, 16):
            within(12 + (m - 8) // 2, outer, piece)
        if not isinstance(m, int) or m <= 13:
            within(m - 2, middle, outward)
        if isinstance(m, int) and m >= 13:
            within(m - 1, middle, outward)
        within(m - 5, jnp.logical_not(middle), outward)

    def norm_bwd(x, gain, dn):
        inv = lax.rsqrt(jnp.mean(x * x, axis=-1, keepdims=True) + EPS)
        u = gain * dn
        dx = inv * u - x * (inv * inv * inv) * jnp.mean(x * u, axis=-1, keepdims=True)
        return dx, jnp.sum(dn * x * inv, axis=0, keepdims=True)

    mine_half = pl.ds(pl.multiple_of(c * hd2, hd2), hd2)
    other_half = pl.ds(pl.multiple_of((1 - c) * hd2, hd2), hd2)

    def a_half(g):
        src = r.wf.at[pl.ds(pl.multiple_of(g * hd2, hd2), hd2), pl.ds(0, 512)]
        return across(src, r.ra.at[g], r.a_ss.at[g], r.a_rs.at[g])

    def first_group(to):
        g = jnp.int32(KV - 1)
        for k in reversed(range(KV - 1)):
            g = jnp.where(r.own[k] == to, k, g)
        return g

    g1 = jnp.int32(0)
    for k in range(1, KV):
        for i in range(k):
            g1 = jnp.where(r.own[k] == r.own[i], k, g1)

    def own_share(to, i):
        lo, n = columns(i)
        q = place(i) - 12
        at = pl.ds(q * cr, cr)
        g0 = first_group(to)
        span = pl.ds(lo, min(n, 512 - lo))
        first = r.ha[g0, at, span].astype(F32) + r.ra[g0, at, span].astype(F32)
        if lo + n <= 512:
            return first
        cols = pl.ds(pl.multiple_of(to * 128, 128), 128)
        second = r.ha[g1, at, cols].astype(F32) + r.ra[g1, at, cols].astype(F32)
        return jnp.concatenate([first, second], axis=1)

    def share_slot(ref, j, i):
        lo, n = columns(i)
        return ref.at[4 * (j - 1) + place(i) - 12, :, pl.ds(lo, n)]

    def head_share(j, i):
        return remote(share_slot(r.sf, j, i), share_slot(r.rf2, j, i), r.h_ss.at[j, i - 12], r.h_rs.at[j, i - 12], j)

    def attention_sums():
        @pl.loop(0, KV)
        def _(g):
            def product(rows_of):
                first = nn(jnp.concatenate([r.nat[0, rows_of, :], r.nat[1, rows_of, :]], axis=1), r.dpg[g])
                second = nn(jnp.concatenate([r.dat[0, rows_of, :], r.dat[1, rows_of, :]], axis=1), r.aog[g])
                return first[:, :256], first[:, 256:] + second[:, :128], second[:, 128:]

            def put(dst, parts):
                dst[:, 0:256] = parts[0].astype(BF16)
                dst[:, 256:384] = parts[1].astype(BF16)
                dst[:, 384:512] = parts[2].astype(BF16)

            put(r.wf.at[pl.ds(pl.multiple_of(g * hd2, hd2), hd2)], product(other_half))
            a_half(g).start()
            put(r.ha.at[g], product(mine_half))

            @pl.when(g % 3 == 1)
            def _():
                turn(KV + g // 3)

        @pl.loop(0, KV)
        def _(g):
            a_half(g).wait_recv()

        for t in range(3):
            ffn_half(t).wait_send()
        for i in range(12, 17):
            for j in (3, 1, 2):
                share_slot(r.sf, j, i)[...] = own_share(peer_of(h, j), i).astype(BF16)
                head_share(j, i).start()
        turn(KV + 2)

    def attention_piece(i):
        def own():
            v = own_share(h, i)
            for j in (1, 2, 3):
                head_share(j, i).wait_recv()
                v = v + share_slot(r.rf2, j, i)[...].astype(F32)
            return v

        inward(i, own)

    @pl.loop(0, 2)
    def _(back):
        p = 1 - back
        ag = gather(2, halves(r.df.at[0, 0]), lambda j, x: halves(r.df.at[0, j])(x))

        @pl.when(p == 0)
        def _():
            block = r.d_res[...] * valid
            r.d_res[...] = block
            r.df[0, 0] = block.astype(BF16)
            ag.start()

        for j in range(HEADS):
            if j:
                @pl.when(p == 0)
                def _():
                    if j == 1:
                        ag.hand_on()
                    ag.wait(j)

            d_act = nn(r.df[p, j], wd_v[...])
            gate, up = r.gate[p, j], r.up[p, j]
            s = 1.0 / (1.0 + jnp.exp(-gate))
            dg = (d_act * up * s * (1.0 + gate * (1.0 - s))).astype(BF16)
            du = (d_act * (gate * s)).astype(BF16)
            r.act[j] = (gate * s * up).astype(BF16)
            r.dg[j] = dg
            r.du[j] = du
            part = nt(dg, wg_v[...]) + nt(du, wu_v[...])
            if j == 0:
                r.part[1 - p] = part.astype(BF16)
            else:
                r.psend[1 - p, j - 1] = part.astype(BF16)
                share(1 - p, 3 - p, j).start()
        for t, rhs in ((0, r.dg), (1, r.du), (2, r.act)):
            if t != 1:
                src = r.nf if t == 0 else r.df
                for j in range(HEADS):
                    store_t(lhs.at[:, j * rows : (j + 1) * rows], src[p, j])
            right = rhs[...].reshape(half, ff)
            theirs = nn(lhs[other_half, :], right)
            for q in range(4):
                v = theirs[q * cr : (q + 1) * cr] + r.sf[4 * t + q].astype(F32)
                r.sf[4 * t + q] = v.astype(BF16)

            @pl.when(p == 0)
            def _():
                ffn_half(t).start()
                if t:
                    outer_pieces(4 * (t - 1), 4 * t)

            ours = nn(lhs[mine_half, :], right)
            for q in range(4):
                r.gown[4 * t + q] += ours[q * cr : (q + 1) * cr]

        @pl.when(p == 1)
        def _():
            final(0, r.out).put(valid * (r.mid[1] + summed(1, 1)))
            final(0, r.out).send()
            sent(1, 1)

        dn = summed(1 - p, 3 - p)
        dx, dgain = norm_bwd(r.mid[p], gain_f(), dn)
        d_mid = r.d_res[...] + dx
        r.d_mid[...] = d_mid
        r.gain_v[1] += dgain
        da = d_mid.astype(BF16)
        store_t(r.dat.at[p], da)
        r.wide[:, :d] = nt(da, r.wo_v[...])
        for b, lo, w in blocks(d):
            y = r.wide[:, lo : lo + 128]
            g, o = head_row(2 * b)
            r.ou[g, o : o + rows, :] = jnp.where(low, 0.0, swap(y)).astype(BF16)
            if 2 * b + 1 < QH:
                g, o = head_row(2 * b + 1)
                r.ou[g, o : o + rows, :] = jnp.where(low, 0.0, y).astype(BF16)

        def hop(g):
            return across(r.dkv_ctx.at[g], r.dkv_ctx_r.at[p, g], r.dc_ss.at[p, g], r.dc_rs.at[p, g])

        def to_owner(j, g):
            return remote(
                r.dkv_s.at[g, j - 1], r.dkv_r.at[g, j - 1], r.dkv_ss.at[p, g], r.dkv_rs.at[p, g], j
            )

        def all_owners(g):
            return remote(r.dkv_s.at[g], r.dkv_r.at[g], r.dkv_ss.at[p, g], r.dkv_rs.at[p, g], 1)

        def pass_on(g):
            @pl.when(c == 0)
            def _():
                hop(g).wait_recv()
                r.dkv[g] += r.dkv_ctx_r[p, g].astype(F32)

            for j in (1, 2, 3):
                r.dkv_s[g, j - 1] = r.dkv[g, :, j * rows : (j + 1) * rows].astype(BF16)
                to_owner(j, g).start()

        @pl.loop(0, KV)
        def _(g):
            kv = r.kv[p, g]
            acc = None
            for k in range(GQ):
                q = r.ql[p, g, k * rows : (k + 1) * rows, :]
                o = r.ou[g, k * rows : (k + 1) * rows, :]
                s = nt(q, kv)
                s = s + r.bias[...]
                lse = jnp.sum(jnp.where(lane == g * GQ + k, r.lse[p], 0.0), axis=-1, keepdims=True)
                pr = jnp.exp(s - lse)
                dpr = nt(o, kv)
                delta = jnp.sum(pr * dpr, axis=-1, keepdims=True)
                ds = (pr * (dpr - delta)).astype(BF16)
                r.heads[g * GQ + k] = unrope(nn(ds, kv) * HD ** (-0.5))
                t = nn(o.T, pr.astype(BF16)) + nn(q.T, ds)
                acc = t if acc is None else acc + t
            r.dkv[g] = acc[:, :half]
            r.dkv_ctx[g] = acc[:, half:].astype(BF16)

            @pl.when(c == 1)
            def _():
                hop(g).start()

            @pl.when(g > 0)
            def _():
                pass_on(g - 1)

            @pl.when((p == 0) & (g == 0))
            def _():
                outer_pieces(8, 12)

            @pl.when((p == 0) & (g > 0))
            def _():
                turn(g - 1)

        pass_on(KV - 1)
        mine = pl.ds(pl.multiple_of(p * rows, rows), rows)
        for b, lo, w in blocks(d):
            y = r.heads[2 * b]
            if 2 * b + 1 < QH:
                y = jnp.where(low, y, swap(r.heads[2 * b + 1]))
            r.at[:, lo : lo + w] = y[:, :w].astype(BF16)
        for g in range(KV):
            both = jnp.where(low, r.heads[g * GQ], swap(r.heads[g * GQ + 1]))
            r.dpg[g, mine, 0:128] = both.astype(BF16)

        r.wide[:, :d] = nt(r.at[...], r.wq_v[...])

        @pl.when(p == 0)
        def _():
            turn(KV - 1)

        keys, vals = [], []
        for g in range(KV):
            t = r.dkv[g, :, 0:rows]
            all_owners(g).wait_recv()
            for j in range(3):
                t = t + r.dkv_r[g, j].astype(F32)
            t = t.T
            kt, vt = unrope(t), swap(t)
            keys.append(kt)
            vals.append(t)
            r.dpg[g, mine, 128:256] = jnp.where(low, r.heads[g * GQ + 2], swap(kt)).astype(BF16)
            r.dpg[g, mine, 256:384] = jnp.where(low, vt, 0.0).astype(BF16)
        for b, lo, w in blocks(KV * HD):
            kb, vb = keys[2 * b], swap(vals[2 * b])
            if 2 * b + 1 < KV:
                kb = jnp.where(low, kb, swap(keys[2 * b + 1]))
                vb = jnp.where(low, vb, vals[2 * b + 1])
            r.dk[:, lo : lo + w] = kb[:, :w].astype(BF16)
            r.dv[:, lo : lo + w] = vb[:, :w].astype(BF16)
        @pl.when(p == 0)
        def _():
            attention_sums()

        dna = r.wide[:, :d] + nn(r.dk[...], r.wk_v[...]) + nn(r.dv[...], r.wv_v[...])
        dx, dgain = norm_bwd(r.res[p], gain_a(), dna)
        r.d_res[...] = r.d_mid[...] + dx
        r.gain_v[0] += dgain
        sent(1 - p, 3 - p)

        @pl.when(p == 0)
        def _():
            ag.drain()

        @pl.when(p == 1)
        def _():
            final(0, r.out).hand_on()


        @pl.loop(0, KV)
        def _(g):
            all_owners(g).wait_send()

            @pl.when(c == 1)
            def _():
                hop(g).wait_send()

    final(1, r.gin).put(r.d_res[...])

    me = 2 * h + c
    r.gain_p[me] = r.gain_v[...]
    gp = [copy_to(r.gain_p.at[me], r.gain_p.at[me], r.gp_ss.at[2 * j + x], r.gp_rs.at[2 * j + x], plane_id(j, x))
          for j, x in plane]
    for cp in gp:
        cp.start()

    for cp in gp:
        cp.wait_recv()
    total = r.gain_p[0]
    for k in range(1, 2 * HEADS):
        total = total + r.gain_p[k]
    r.gain_z[z] = total
    gz = [copy_to(r.gain_z.at[z], r.gain_z.at[z], r.gz_ss.at[k], r.gz_rs.at[k], dict(batch=(z + k) % nb))
          for k in range(1, nb)]
    for cp in gz:
        cp.start()

    for m in range(KV + 3, 22):
        turn(m)
        if m == 13:
            final(1, r.gin).send()
        if m == 16:
            final(1, r.gin).hand_on()

    for cp in gz:
        cp.wait_recv()
    total = r.gain_z[0]
    for k in range(1, nb):
        total = total + r.gain_z[k]
    r.gain_v[...] = total
    gains_out = pltpu.make_async_copy(r.gain_v, r.gains_out, r.loc_sem.at[2])
    gains_out.start()

    for q in range(4):
        ex_arrive(q)

    gains_out.wait()
    for cp in gp + gz:
        cp.wait_send()
    for j in (1, 2, 3):
        for i in range(12, 17):
            head_share(j, i).wait_send()

    @pl.loop(0, KV)
    def _(g):
        a_half(g).wait_send()

    def settle(i):
        og_local(i, r.zs).wait()
        og_across(i, r.zs).wait_send()
        og_across(i, r.zs).wait_recv()

        @pl.when(jnp.logical_not(middle))
        def _():
            to_next(i).wait_send()

        @pl.when(handed)
        def _():
            to_outer(i, r.zs).wait_send()

    pl.loop(0, 12)(settle)
    for i in range(12, 17):
        settle(i)

    for q in range(4):
        ex_local(q, r.zs).wait()
        ex_plane(q, r.zs, 0, 1).wait()
        for j in (1, 2, 3):
            ex_hand_on(q, j).wait()
    for k, out in ((0, r.out), (1, r.gin)):
        end = final(k, out)
        end.own.wait()
        for j in (1, 2, 3):
            end.wait(j)
        end.drain()


def put_kernel(own, o, gin, og, ex, ga, gf, o_out, gin_out, gq, gk, gv, go, gg, gu, gd, ga_out, gf_out):
    h = lax.axis_index("head")
    held = jnp.int32(0)
    for k in range(KV):
        held = held + jnp.where(own[k] == h, 1, 0)
    gw = GQ * HD
    o_out[...] = o[...]
    gin_out[...] = gin[...].astype(F32)
    wide = lambda x: x.astype(F32).reshape(-1, x.shape[-1])
    gg[...] = wide(og[0])
    gu[...] = wide(og[1])
    gd[...] = wide(og[2])
    ga_out[...] = ga[...]
    gf_out[...] = gf[...]
    first = wide(og[3])[:, 0:512]
    second = jnp.concatenate([wide(ex[k]) for k in range(HEADS)], axis=1)
    second = jnp.where(held > 1, second, 0.0)
    for out, lo, width in ((gq, 0, gw), (gk, gw, HD), (gv, gw + HD, HD), (go, gw + 2 * HD, gw)):
        out[...] = jnp.concatenate([first[:, lo : lo + width], second[:, lo : lo + width]], axis=1)


def body(nb, hidden_in, cotangent, lengths, owners, w_query, w_key, w_value, w_output, gate_weight, up_weight, down_weight,
         gain_attn, gain_ffn):
    half, d = hidden_in.shape[1:]
    ff = gate_weight.shape[1]
    rows = half // HEADS
    cr = d // 8
    scratch = scratch_of(rows, d, ff, nb)
    anyspec = pl.BlockSpec(memory_space=pl.ANY)
    smem = pl.BlockSpec(memory_space=pltpu.SMEM)
    sd = jax.ShapeDtypeStruct
    ins = dict(
        hid=anyspec, cot=anyspec, len=smem, own=smem, ga=anyspec, gf=anyspec, tab=anyspec,
        wq=anyspec, wk=anyspec, wv=anyspec, wo=anyspec, wg=anyspec, wu=anyspec, wd=anyspec,
    )
    outs = dict(
        out=sd((d, half), BF16), gin=sd((d, half), BF16),
        og=sd((4, 2, 4, cr, ff), BF16), ex=sd((HEADS, 2, 4, cr, 128), BF16), gains_out=sd((2, 1, d), F32),
    )
    names = tuple(ins) + tuple(outs) + tuple(scratch)
    o, gin, og, ex, gains = pl.pallas_call(
        functools.partial(step_kernel, names, rows, d, ff, nb),
        out_shape=tuple(outs.values()),
        in_specs=list(ins.values()),
        out_specs=(anyspec,) * len(outs),
        scratch_shapes=list(scratch.values()),
        compiler_params=pltpu.CompilerParams(
            collective_id=0, has_side_effects=True, vmem_limit_bytes=67043328
        ),
    )(
        hidden_in[0].T, cotangent[0].T, lengths, owners, gain_attn[None], gain_ffn[None],
        jnp.asarray(rope_table(2 * half)), w_query, w_key.T, w_value.T, w_output, gate_weight, up_weight, down_weight.T,
    )
    gw, block = GQ * HD, lambda *shape: (lambda index: pl.BlockSpec(shape, index))
    rowwise = lambda width: block(2 * cr, width)(lambda i: (i, 0))
    gains_spec = lambda k: block(None, 1, d)(lambda i: (k, 0, 0))
    gain_out = block(1, d)(lambda i: (0, 0))
    o, gin, gq, gk, gv, go, gg, gu, gd, ga, gf = pl.pallas_call(
        put_kernel,
        grid=(4,),
        out_shape=(
            sd((d, half), BF16), sd((d, half), F32), sd((d, 2 * gw), F32), sd((d, 2 * HD), F32), sd((d, 2 * HD), F32),
            sd((d, 2 * gw), F32), sd((d, ff), F32), sd((d, ff), F32), sd((d, ff), F32), sd((1, d), F32), sd((1, d), F32),
        ),
        in_specs=[
            smem, rowwise(half), rowwise(half), block(4, None, 2, cr, ff)(lambda i: (0, i // 2, i % 2, 0, 0)),
            block(HEADS, None, 2, cr, 128)(lambda i: (0, i // 2, i % 2, 0, 0)), gains_spec(0), gains_spec(1),
        ],
        out_specs=(
            rowwise(half), rowwise(half), rowwise(2 * gw), rowwise(2 * HD), rowwise(2 * HD), rowwise(2 * gw),
            rowwise(ff), rowwise(ff), rowwise(ff), gain_out, gain_out,
        ),
    )(owners, o, gin, og, ex, gains, gains)
    return o.T[None], gin.T[None], gq, gk, gv, go.T, gg, gu, gd.T, ga[0], gf[0]


def solution(mesh):
    rep = P()
    io = P("batch", "ctx", None)
    in_specs = (io, io, P("batch"), rep, rep, rep, rep, rep, P(None, "head"), P(None, "head"), P("head", None), rep, rep)
    out_specs = (io, io, P(None, "head"), P(None, "head"), P(None, "head"), P("head", None), P(None, "head"),
                 P(None, "head"), P("head", None), rep, rep)
    return jax.shard_map(
        functools.partial(body, mesh.shape["batch"]), mesh=mesh, in_specs=in_specs, out_specs=out_specs, check_vma=False
    )
```
